32 devices in a mesh: grp: 2 (over x), row: 8 (over z, y), col: 2 (over core).
Axes of the slice: x: 2, y: 2, z: 4, core: 2. Of those that a mesh axis runs over, the one named last changes fastest.
Arguments:
- pair_act: bfloat16 [64, 32, 128], P(('grp', 'row'), 'col'), parts along dimension 0, may hold values from -200 to 200
- cotangent: bfloat16 [64, 32, 128], P(('grp', 'row'), 'col'), parts along dimension 0, may hold values from -6 to 6
- residue_mask: int32 [64], P('grp'), parts along dimension 0, may hold values from 0 to 1, as said below
- front_weight: bfloat16 [2, 128, 640], replicated, may hold values from -0.5 to 0.5
- out_weight: bfloat16 [2, 128, 128], replicated, may hold values from -0.5 to 0.5
Outputs:
- pair_grad: bfloat16 [64, 32, 128], P(('grp', 'row'), 'col'), parts along dimension 0
The draws below stay inside these ranges and needn't reach their ends.
There are 2 independent parts, one for each index of `grp`. The reference program is written for one: setup_inputs(seed, part) draws one part's arguments, and reference() takes and returns one part's arrays. A program takes and returns all parts, laid end to end along the dimension named above; an argument that names none is the same for every part. Nothing has to cross between parts.
Inputs may be any that keep to these rules, and one draw needn't show every extreme that they name: residue_mask is 1 on residues 0 to L - 1 and 0 from L on, for a chain length L of at least 24.
All inputs are finite; a program needn't handle non-finite values.
Results may differ from the reference program's by a relative error of at most 0.01.
Values may be sent and summed in bfloat16 or wider, within the bound.
A program may use at most 64 MiB of HBM per device.

```python
import math
import jax
import jax.numpy as jnp
from jax import lax

C = 128
H = 128
N = 32


def draw_pair_act(key, part):
    keys = jax.random.split(jax.random.fold_in(key, 11), 3)
    base = jax.random.normal(keys[0], (N, N, C), jnp.float32)
    cell_scale = jnp.exp(jax.random.uniform(keys[1], (N, N, 1), jnp.float32, 0.0, math.log(10.0)))
    channel_scale = jnp.exp(jax.random.uniform(keys[2], (1, 1, C), jnp.float32, 0.0, math.log(10.0)))
    values = base * channel_scale * cell_scale
    return jnp.clip(values / 3.0, -200.0, 200.0).astype(jnp.bfloat16)


def draw_residue_mask(key, part):
    lowest = (3 * N + 3) // 4
    span_len = N - lowest + 1
    offset = jax.random.randint(jax.random.fold_in(key, 23), (), 0, span_len)
    length = lowest + (offset + jnp.asarray(part, jnp.int32)) % span_len
    return (jnp.arange(N, dtype=jnp.int32) < length).astype(jnp.int32)


def block_levels(key, dims, shards, least, high):
    factor_of, own = 1.0, jax.random.fold_in(key, 6)
    for position, parts in shards:
        heights = jnp.exp(jax.random.uniform(jax.random.fold_in(own, position), (parts,), jnp.float32, least / len(shards), high / len(shards)))
        factor_of = factor_of * jnp.repeat(heights, dims[position] // parts).reshape([-1 if axis == position else 1 for axis in range(len(dims))])
    return factor_of


def bell_draw(own_key, extent, scale, limit, pieces=(), kind=jnp.bfloat16):
    factor_of = block_levels(own_key, extent, pieces, -0.22, 0.18) if pieces else 1.0
    array = jax.random.normal(own_key, extent, jnp.float32) * scale * factor_of
    return jnp.minimum(jnp.maximum(array, -limit), limit).astype(kind)


def setup_inputs(seed: int = 0, part: int = 0) -> dict:
    seeds = jax.random.split(jax.random.key(seed), 6)
    own_keys = jax.random.split(jax.random.fold_in(seeds[5], part), 6)
    pair_act = draw_pair_act(jax.random.fold_in(jax.random.fold_in(seeds[5], part), 71), part)
    cotangent = bell_draw(own_keys[1], (N, N, C), 1.0, 6.0, ((0, 8), (1, 2)))
    residue_mask = draw_residue_mask(jax.random.fold_in(jax.random.fold_in(seeds[5], part), 71), part)
    front_weight = bell_draw(seeds[3], (2, C, 4 * H + C), C ** -0.5, 0.5)
    out_weight = bell_draw(seeds[4], (2, H, C), H ** -0.5, 0.5)
    return dict(pair_act=pair_act, cotangent=cotangent, residue_mask=residue_mask, front_weight=front_weight, out_weight=out_weight)


def layer_norm(values):
    centred = values - lax.optimization_barrier(jnp.mean(values, axis=-1, keepdims=True))
    spread = lax.optimization_barrier(jnp.mean(centred * centred, axis=-1, keepdims=True))
    return centred * lax.rsqrt(spread + 1e-05)

def project_pair(inner_pair, mask_pair, weight):
    normed = layer_norm(inner_pair.astype(jnp.float32)).astype(jnp.bfloat16)
    linear = jnp.dot(normed, weight, preferred_element_type=jnp.float32)
    left_side = jax.nn.sigmoid(linear[..., :H]) * linear[..., H:2 * H]
    right_side = jax.nn.sigmoid(linear[..., 2 * H:3 * H]) * linear[..., 3 * H:4 * H]
    operands = (jnp.stack((left_side, right_side)) * mask_pair[None, :, :, None]).astype(jnp.bfloat16)
    return (operands, jax.nn.sigmoid(linear[..., 4 * H:]))

def finish(mixed_part, gate_value, inner_pair, weight):
    normed = layer_norm(mixed_part).astype(jnp.bfloat16)
    update = jnp.dot(normed, weight, preferred_element_type=jnp.float32)
    return (inner_pair.astype(jnp.float32) + gate_value * update).astype(jnp.bfloat16)

def rounded(values):
    return lax.optimization_barrier(values.astype(jnp.bfloat16)).astype(jnp.float32)

def reference(pair_act, cotangent, residue_mask, front_weight, out_weight):
    chain_mask = residue_mask.astype(jnp.float32)
    mask_pair = chain_mask[:, None] * chain_mask[None, :]
    (out_ops, out_gate), out_front_back = jax.vjp(lambda inner_pair: project_pair(inner_pair, mask_pair, front_weight[0]), pair_act)
    out_left = out_ops[0].astype(jnp.float32)
    out_right = out_ops[1].astype(jnp.float32)
    out_mixed = jnp.einsum('ikc,jkc->ijc', out_left, out_right)
    pair_mid, out_finish_back = jax.vjp(lambda mixed_part, gate_value, inner_pair: finish(mixed_part, gate_value, inner_pair, out_weight[0]), out_mixed, out_gate, pair_act)
    (in_ops, in_gate), in_front_back = jax.vjp(lambda inner_pair: project_pair(inner_pair, mask_pair, front_weight[1]), pair_mid)
    in_left = in_ops[0].astype(jnp.float32)
    in_right = in_ops[1].astype(jnp.float32)
    in_mixed = jnp.einsum('kic,kjc->ijc', in_left, in_right)
    unused_pair, in_finish_back = jax.vjp(lambda mixed_part, gate_value, inner_pair: finish(mixed_part, gate_value, inner_pair, out_weight[1]), in_mixed, in_gate, pair_mid)
    grad_mixed, grad_gate, grad_inner = in_finish_back(cotangent)
    signal = rounded(grad_mixed)
    grad_left = jnp.einsum('ijc,kjc->kic', signal, in_right)
    grad_right = jnp.einsum('ijc,kic->kjc', signal, in_left)
    grad_front, = in_front_back((jnp.stack((grad_left, grad_right)).astype(jnp.bfloat16), grad_gate))
    grad_mid = (grad_inner.astype(jnp.float32) + grad_front.astype(jnp.float32)).astype(jnp.bfloat16)
    grad_mixed, grad_gate, grad_inner = out_finish_back(grad_mid)
    signal = rounded(grad_mixed)
    grad_left = jnp.einsum('ijc,jkc->ikc', signal, out_right)
    grad_right = jnp.einsum('ijc,ikc->jkc', signal, out_left)
    grad_front, = out_front_back((jnp.stack((grad_left, grad_right)).astype(jnp.bfloat16), grad_gate))
    return (grad_inner.astype(jnp.float32) + grad_front.astype(jnp.float32)).astype(jnp.bfloat16)
```

```python
import functools

import jax
import jax.numpy as jnp
from jax import lax
from jax.experimental import pallas as pl
from jax.experimental.pallas import tpu as pltpu
from jax.sharding import PartitionSpec as P

H = 128
TILE = 8
F32 = jnp.float32
BF16 = jnp.bfloat16
MESH = pl.DeviceIdType.MESH
VMEM_BUDGET = 24 << 20
FULL_ARRAYS = 16


def sigmoid(x):
    return 0.5 * jnp.tanh(0.5 * x) + 0.5


def norm(v):
    centred = v - jnp.mean(v, axis=-1, keepdims=True)
    r = lax.rsqrt(jnp.mean(centred * centred, axis=-1, keepdims=True) + 1e-05)
    return centred * r, r


def norm_back(y, r, d):
    return r * (d - jnp.mean(d, axis=-1, keepdims=True) - y * jnp.mean(d * y, axis=-1, keepdims=True))


def rounded(v):
    return v.astype(BF16).astype(F32)


def dot(a, b):
    return jnp.dot(a.astype(BF16), b, preferred_element_type=F32)


def dot_t(a, b):
    return lax.dot_general(
        a.astype(BF16), b, (((1,), (1,)), ((), ())), preferred_element_type=F32
    )


def part(p, n):
    return p[:, n * H : (n + 1) * H]


def flip(value, other, bits):
    total = 0
    for b in range(bits):
        w = 1 << b
        total = total + (value // w + other // w) % 2 * w
    return total


def front_back(x, mask, weight, d_a, d_b, d_gate):
    y, r = norm(x)
    p = dot(y, weight)
    s0, s2, s4 = sigmoid(part(p, 0)), sigmoid(part(p, 2)), sigmoid(part(p, 4))
    ma, mb = d_a * mask * s0, d_b * mask * s2
    d = jnp.concatenate(
        [
            (v.astype(BF16))
            for v in (
                ma * part(p, 1) * (1.0 - s0),
                ma,
                mb * part(p, 3) * (1.0 - s2),
                mb,
                d_gate * s4 * (1.0 - s4),
            )
        ],
        axis=1,
    )
    return rounded(norm_back(y, r, rounded(dot_t(d, weight))))


def crop_kernel(
    rows, pair, cot, mask_in, wf_in, wo_in, out,
    x_all, ct_all, wf, wo, chain, mask, left, right, flipped, mixed, gate, mid,
    in_left, in_right, in_mixed, in_gate, sig, d_left, d_right, ct32, out_sig, grad,
    local_sem, send_sem, recv_sem, fsend_sem, frecv_sem,
):
    n, c = left.shape[0], left.shape[2]
    lr, lc = out.shape[0], out.shape[1]
    bits = rows.bit_length() - 1
    me, my_col = lax.axis_index("row"), lax.axis_index("col")
    other = 1 - my_col
    r0 = pl.multiple_of(me * lr, lr)
    c0 = pl.multiple_of(my_col * lc, lc)

    weights = [
        pltpu.make_async_copy(wf_in, wf, local_sem.at[2]),
        pltpu.make_async_copy(wo_in, wo, local_sem.at[3]),
    ]
    own = []
    for t, (src, dst) in enumerate(((pair, x_all), (cot, ct_all))):
        own.append(
            pltpu.make_async_copy(src, dst.at[pl.ds(r0, lr), pl.ds(c0, lc)], local_sem.at[t])
        )
    chain_copy = pltpu.make_async_copy(mask_in, chain, local_sem.at[4])
    for copy in [chain_copy] + own + weights:
        copy.start()

    barrier = pltpu.get_barrier_semaphore()
    for d in range(1, rows):
        pl.semaphore_signal(
            barrier, inc=1, device_id={"row": flip(me, d, bits)}, device_id_type=MESH
        )
    pl.semaphore_signal(barrier, inc=1, device_id={"col": other}, device_id_type=MESH)

    chain_copy.wait()
    span = jnp.broadcast_to(chain[...].astype(F32), (n, n))
    here = lax.broadcasted_iota(jnp.int32, (n, n), 0) == lax.broadcasted_iota(jnp.int32, (n, n), 1)
    along = jnp.broadcast_to(
        jnp.sum(jnp.where(here, span, 0.0), axis=1, keepdims=True), (n, c)
    )
    flipped[0] = along

    def fill_mask(i, carry):
        mask[i] = along * flipped[0, pl.ds(i, 1), :]
        return carry

    lax.fori_loop(0, n, fill_mask, 0)
    pl.semaphore_wait(barrier, rows)

    def block(ref, row, col):
        return ref.at[
            pl.ds(pl.multiple_of(row * lr, lr), lr), pl.ds(pl.multiple_of(col * lc, lc), lc)
        ]

    def direct(t, d):
        src, dst = ((pair, x_all), (cot, ct_all))[t]
        return pltpu.make_async_remote_copy(
            src_ref=src,
            dst_ref=block(dst, me, my_col),
            send_sem=send_sem.at[t, d],
            recv_sem=recv_sem.at[t, d],
            device_id={"row": flip(me, d, bits)},
            device_id_type=MESH,
        )

    def first(t):
        src, dst = ((pair, x_all), (cot, ct_all))[t]
        return pltpu.make_async_remote_copy(
            src_ref=src,
            dst_ref=block(dst, me, my_col),
            send_sem=fsend_sem.at[t, 0],
            recv_sem=frecv_sem.at[t, 0],
            device_id={"col": other},
            device_id_type=MESH,
        )

    def forward(t, d):
        ref = (x_all, ct_all)[t]
        held = block(ref, flip(me, d, bits), my_col)
        return pltpu.make_async_remote_copy(
            src_ref=held,
            dst_ref=held,
            send_sem=fsend_sem.at[t, d],
            recv_sem=frecv_sem.at[t, d],
            device_id={"col": other},
            device_id_type=MESH,
        )

    def loop(count, step, start=0):
        def body(k, carry):
            step(k)
            return carry

        lax.fori_loop(start, count, body, 0)

    for t in range(2):
        first(t).start()
        loop(rows, lambda d: direct(t, d).start(), 1)

    for copy in weights:
        copy.wait()
    own[0].wait()

    def rows_of(ref, k0, nk):
        return ref[pl.ds(k0, nk)].reshape(nk * n, c)

    def put(ref, k0, nk, v):
        ref[pl.ds(k0, nk)] = v.reshape(nk, n, c)

    def projected(x, k0, nk, weight, a_ref, b_ref, g_ref):
        y, _ = norm(x)
        p = dot(y, weight)
        m = rows_of(mask, k0, nk)
        put(a_ref, k0, nk, rounded(sigmoid(part(p, 0)) * part(p, 1) * m))
        put(b_ref, k0, nk, rounded(sigmoid(part(p, 2)) * part(p, 3) * m))
        put(g_ref, k0, nk, sigmoid(part(p, 4)))

    def arrived(d):
        direct(0, d).wait_recv()
        forward(0, d).start()

    def front_step(g):
        d = 2 * g

        @pl.when(d + 2 < rows)
        def _():
            arrived(d + 2)
            arrived(d + 3)

        forward(0, d).wait_recv()
        forward(0, d + 1).wait_recv()
        k0 = pl.multiple_of(flip(me, d, bits) // 2 * 2 * lr, 2 * lr)
        projected(rows_of(x_all, k0, 2 * lr).astype(F32), k0, 2 * lr, wf[0], left, right, gate)

    arrived(1)
    loop(rows // 2, front_step)

    def transpose(src):
        def step(b):
            i = pl.multiple_of(b * TILE, TILE)
            flipped[:, pl.ds(i, TILE), :] = jnp.swapaxes(src[pl.ds(i, TILE)], 0, 1)

        loop(n // TILE, step)

    def triangle(count, width, row_at, tile_at, store, group):
        def step(b):
            def term(q, acc):
                t = tile_at(q)
                return tuple(v + row_at(b * group + a, q) * t for a, v in enumerate(acc))

            zero = jnp.zeros((width, c), F32)
            acc = lax.fori_loop(0, n, term, (zero,) * group, unroll=True)
            for a in range(group):
                store(b * group + a, acc[a])

        loop(count // group, step)

    transpose(right)

    def put_row(ref):
        def store(a, v):
            ref[a] = v

        return store

    triangle(
        n, n,
        lambda i, k: left[i, pl.ds(k, 1), :],
        lambda k: flipped[k],
        put_row(mixed), 4,
    )

    own[1].wait()

    def pass_on(d):
        direct(1, d).wait_recv()
        forward(1, d).start()

    loop(rows, pass_on, 1)

    some = min(n, 4 * lr)

    def middle_step(b):
        k0 = b * some
        z, _ = norm(rows_of(mixed, k0, some))
        x = rows_of(x_all, k0, some).astype(F32)
        x = rounded(x + rows_of(gate, k0, some) * dot(z, wo[0]))
        put(mid, k0, some, x)
        projected(x, k0, some, wf[1], in_left, in_right, in_gate)

    loop(n // some, middle_step)

    triangle(
        n, n,
        lambda i, k: in_left[k, pl.ds(i, 1), :],
        lambda k: in_right[k],
        put_row(in_mixed), 4,
    )

    loop(rows, lambda d: forward(1, d).wait_recv())

    def signal_step(b):
        k0 = b * some
        z, r = norm(rows_of(in_mixed, k0, some))
        ct = rows_of(ct_all, k0, some).astype(F32)
        put(ct32, k0, some, ct)
        dz = rounded(dot_t(ct * rows_of(in_gate, k0, some), wo[1]))
        put(sig, k0, some, rounded(norm_back(z, r, dz)))

    loop(n // some, signal_step)
    transpose(sig)

    def strip(k0, nk, j0, width, group, chunk):
        def take(ref, k, m):
            return ref[pl.ds(k, m), pl.ds(j0, width), :].reshape(m * width, c)

        def give(ref, k, m, v):
            ref[pl.ds(k, m), pl.ds(j0, width), :] = v.reshape(m, width, c)

        def into(ref):
            def store(a, v):
                ref[k0 + a, pl.ds(j0, width), :] = rounded(v)

            return store

        triangle(
            nk, width,
            lambda a, j: in_right[k0 + a, pl.ds(j, 1), :],
            lambda j: flipped[j, pl.ds(j0, width), :],
            into(d_left), group,
        )
        triangle(
            nk, width,
            lambda a, i: in_left[k0 + a, pl.ds(i, 1), :],
            lambda i: sig[i, pl.ds(j0, width), :],
            into(d_right), group,
        )

        def back(b):
            k = k0 + b * chunk
            ct = take(ct32, k, chunk)
            z1, _ = norm(take(in_mixed, k, chunk))
            d_in = front_back(
                take(mid, k, chunk), take(mask, k, chunk), wf[1],
                take(d_left, k, chunk), take(d_right, k, chunk),
                ct * dot(z1, wo[1]),
            )
            g = rounded(ct + d_in)
            z0, r = norm(take(mixed, k, chunk))
            dz = rounded(dot_t(g * take(gate, k, chunk), wo[0]))
            give(grad, k, chunk, g)
            give(out_sig, k, chunk, rounded(norm_back(z0, r, dz)))

        loop(nk // chunk, back)

    t0 = pl.multiple_of(me * lr // TILE * TILE, TILE)
    strip(r0, lr, 0, n, lr, lr)
    strip(0, n, t0, max(TILE, lr), TILE, 4 * TILE if n % (4 * TILE) == 0 else TILE)

    def own_of(ref):
        def store(a, v):
            ref[r0 + a, pl.ds(c0, lc), :] = rounded(v)

        return store

    triangle(
        lr, lc,
        lambda a, j: out_sig[r0 + a, pl.ds(j, 1), :],
        lambda j: right[j, pl.ds(c0, lc), :],
        own_of(d_left), lr,
    )
    triangle(
        lr, lc,
        lambda a, i: out_sig[i, pl.ds(r0 + a, 1), :],
        lambda i: left[i, pl.ds(c0, lc), :],
        own_of(d_right), lr,
    )

    def mine(ref):
        return ref[pl.ds(r0, lr), pl.ds(c0, lc), :].reshape(lr * lc, c)

    z0, _ = norm(mine(mixed))
    g = mine(grad)
    d_front = front_back(
        mine(x_all).astype(F32), mine(mask), wf[0], mine(d_left), mine(d_right),
        g * dot(z0, wo[0]),
    )
    out[...] = (g + d_front).astype(BF16).reshape(lr, lc, c)

    for t in range(2):
        first(t).wait_send()

        def sent(d):
            direct(t, d).wait_send()
            forward(t, d).wait_send()

        loop(rows, sent, 1)


def from_root(array, axis, root):
    mine = lax.axis_index(axis) == root
    return lax.psum(jnp.where(mine, array, jnp.zeros_like(array)), axis)


def layer_norm(values):
    centred = values - jnp.mean(values, axis=-1, keepdims=True)
    spread = jnp.mean(centred * centred, axis=-1, keepdims=True)
    return centred * lax.rsqrt(spread + 1e-05)


def project_pair(inner_pair, mask_pair, weight):
    normed = layer_norm(inner_pair.astype(jnp.float32)).astype(jnp.bfloat16)
    linear = jnp.dot(normed, weight, preferred_element_type=jnp.float32)
    left_side = jax.nn.sigmoid(linear[..., :H]) * linear[..., H : 2 * H]
    right_side = jax.nn.sigmoid(linear[..., 2 * H : 3 * H]) * linear[..., 3 * H : 4 * H]
    operands = (jnp.stack((left_side, right_side)) * mask_pair[None, :, :, None]).astype(
        jnp.bfloat16
    )
    return (operands, jax.nn.sigmoid(linear[..., 4 * H :]))


def finish(mixed_part, gate_value, inner_pair, weight):
    normed = layer_norm(mixed_part).astype(jnp.bfloat16)
    update = jnp.dot(normed, weight, preferred_element_type=jnp.float32)
    return (inner_pair.astype(jnp.float32) + gate_value * update).astype(jnp.bfloat16)


def body(pair_act, cotangent, residue_mask, front_weight, out_weight):
    local_rows = pair_act.shape[0]
    local_cols = pair_act.shape[1]
    row_index = lax.axis_index("row")
    col_index = lax.axis_index("col")
    block_rows = lax.axis_size("row") // lax.axis_size("col")
    owner_col = row_index // block_rows
    offset = row_index % block_rows * local_rows
    chain_mask = residue_mask.astype(jnp.float32)
    mask_rows = lax.dynamic_slice_in_dim(chain_mask, row_index * local_rows, local_rows)
    mask_cols = lax.dynamic_slice_in_dim(chain_mask, col_index * local_cols, local_cols)
    mask_pair = mask_rows[:, None] * mask_cols[None, :]

    def gather_rows(stacked):
        return lax.all_gather(stacked, "row", axis=1, tiled=True)

    def column_block(gathered):
        slab = lax.dynamic_slice_in_dim(gathered, offset, local_rows, 1)
        return from_root(slab, "col", owner_col)

    def gather_cols(values):
        return lax.all_gather(values, "col", axis=1, tiled=True)

    def sum_cols(partial_term):
        return lax.psum_scatter(
            partial_term.astype(jnp.bfloat16), "col", scatter_dimension=1, tiled=True
        ).astype(jnp.float32)

    (out_ops, out_gate), out_front_back = jax.vjp(
        lambda inner_pair: project_pair(inner_pair, mask_pair, front_weight[0]), pair_act
    )
    fetched = gather_rows(out_ops)
    out_mixed = sum_cols(
        jnp.einsum("ikc,jkc->ijc", out_ops[0], fetched[-1], preferred_element_type=jnp.float32)
    )
    pair_mid, out_finish_back = jax.vjp(
        lambda mixed_part, gate_value, inner_pair: finish(
            mixed_part, gate_value, inner_pair, out_weight[0]
        ),
        out_mixed,
        out_gate,
        pair_act,
    )
    (in_ops, in_gate), in_front_back = jax.vjp(
        lambda inner_pair: project_pair(inner_pair, mask_pair, front_weight[1]), pair_mid
    )
    in_fetched = gather_rows(in_ops)
    left_block = column_block(in_fetched[0])
    in_mixed = jnp.einsum(
        "kic,kjc->ijc", left_block, in_fetched[1], preferred_element_type=jnp.float32
    )
    unused_pair, in_finish_back = jax.vjp(
        lambda mixed_part, gate_value, inner_pair: finish(
            mixed_part, gate_value, inner_pair, out_weight[1]
        ),
        in_mixed,
        in_gate,
        pair_mid,
    )
    grad_mixed, grad_gate, grad_inner = in_finish_back(cotangent)
    signal = grad_mixed.astype(jnp.bfloat16)
    signal_rows = gather_rows(signal[None])[0]
    left_rows = gather_cols(in_ops[0])
    grad_right = jnp.einsum(
        "kic,ijc->kjc", left_rows, signal_rows, preferred_element_type=jnp.float32
    )
    grad_left = sum_cols(
        jnp.einsum("kjc,ijc->kic", in_ops[1], signal_rows, preferred_element_type=jnp.float32)
    )
    (grad_front,) = in_front_back(
        (jnp.stack((grad_left, grad_right)).astype(jnp.bfloat16), grad_gate)
    )
    grad_mid = (grad_inner.astype(jnp.float32) + grad_front.astype(jnp.float32)).astype(
        jnp.bfloat16
    )
    grad_mixed, grad_gate, grad_inner = out_finish_back(grad_mid)
    signal = grad_mixed.astype(jnp.bfloat16)
    signal_cols = gather_cols(signal)
    grad_left = jnp.einsum(
        "ijc,jkc->ikc", signal_cols, fetched[-1], preferred_element_type=jnp.float32
    )
    signal_block = column_block(gather_rows(signal[None])[0])
    grad_right = jnp.einsum(
        "ijc,ikc->jkc", signal_block, fetched[0], preferred_element_type=jnp.float32
    )
    (grad_front,) = out_front_back(
        (jnp.stack((grad_left, grad_right)).astype(jnp.bfloat16), grad_gate)
    )
    return (grad_inner.astype(jnp.float32) + grad_front.astype(jnp.float32)).astype(jnp.bfloat16)


def crop_body(rows, pair_act, cotangent, residue_mask, front_weight, out_weight):
    lr, lc, c = pair_act.shape
    n = residue_mask.shape[0]
    full = pltpu.VMEM((n, n, c), F32)
    dma = pltpu.SemaphoreType.DMA
    hbm = pl.BlockSpec(memory_space=pl.ANY)
    return pl.pallas_call(
        functools.partial(crop_kernel, rows),
        out_shape=jax.ShapeDtypeStruct((lr, lc, c), BF16),
        in_specs=[hbm] * 5,
        out_specs=pl.BlockSpec(memory_space=pltpu.VMEM),
        scratch_shapes=[
            pltpu.VMEM((n, n, c), BF16),
            pltpu.VMEM((n, n, c), BF16),
            pltpu.VMEM(front_weight.shape, BF16),
            pltpu.VMEM(out_weight.shape, BF16),
            pltpu.VMEM((1, n), jnp.int32),
        ]
        + [full] * 17
        + [dma((5,)), dma((2, rows)), dma((2, rows)), dma((2, rows)), dma((2, rows))],
        compiler_params=pltpu.CompilerParams(
            collective_id=0, has_side_effects=True, vmem_limit_bytes=24 << 20
        ),
    )(*[pltpu.with_memory_space_constraint(v, pltpu.HBM) for v in (pair_act, cotangent, residue_mask.reshape(1, n), front_weight, out_weight)])


def fits(mesh, n, lr, lc, c):
    rows, cols = mesh.shape["row"], mesh.shape["col"]
    return (
        cols == 2
        and rows >= 2
        and rows & (rows - 1) == 0
        and n % TILE == 0
        and (lr % TILE == 0 or TILE % lr == 0)
        and lc % (2 * TILE) == 0
        and FULL_ARRAYS * 4 * n * n * c <= VMEM_BUDGET
    )


def solution(mesh):
    def dispatch(pair_act, cotangent, residue_mask, front_weight, out_weight):
        n = residue_mask.shape[0]
        if fits(mesh, n, *pair_act.shape):
            return crop_body(
                mesh.shape["row"], pair_act, cotangent, residue_mask, front_weight, out_weight
            )
        return body(pair_act, cotangent, residue_mask, front_weight, out_weight)

    placed = (P(("grp", "row"), "col", None), P(("grp", "row"), "col", None), P("grp"), P(), P())
    return jax.shard_map(
        dispatch,
        mesh=mesh,
        in_specs=placed,
        out_specs=P(("grp", "row"), "col", None),
        check_vma=False,
    )
```

```python
import functools

import jax
import jax.numpy as jnp
from jax import lax
from jax.experimental import pallas as pl
from jax.experimental.pallas import tpu as pltpu
from jax.sharding import PartitionSpec as P

H = 128
TILE = 8
F32 = jnp.float32
BF16 = jnp.bfloat16
MESH = pl.DeviceIdType.MESH
VMEM_BUDGET = 24 << 20
FULL_ARRAYS = 16


def sigmoid(x):
    return 0.5 * jnp.tanh(0.5 * x) + 0.5


def norm(v):
    centred = v - jnp.mean(v, axis=-1, keepdims=True)
    r = lax.rsqrt(jnp.mean(centred * centred, axis=-1, keepdims=True) + 1e-05)
    return centred * r, r


def norm_back(y, r, d):
    return r * (d - jnp.mean(d, axis=-1, keepdims=True) - y * jnp.mean(d * y, axis=-1, keepdims=True))


def rounded(v):
    return v.astype(BF16).astype(F32)


def dot(a, b):
    return jnp.dot(a.astype(BF16), b, preferred_element_type=F32)


def dot_t(a, b):
    return lax.dot_general(
        a.astype(BF16), b, (((1,), (1,)), ((), ())), preferred_element_type=F32
    )


def part(p, n):
    return p[:, n * H : (n + 1) * H]


def factors(x, mask, weight):
    y, r = norm(x)
    p = dot(y, weight)
    s0, s2, s4 = sigmoid(part(p, 0)), sigmoid(part(p, 2)), sigmoid(part(p, 4))
    fa, fb = mask * s0, mask * s2
    return y, r, fa * part(p, 1) * (1.0 - s0), fa, fb * part(p, 3) * (1.0 - s2), fb, s4 * (1.0 - s4)


def front_back(f, weight, d_a, d_b, d_gate):
    y, r, f0, f1, f2, f3, f4 = f
    d = jnp.concatenate(
        [(v.astype(BF16)) for v in (d_a * f0, d_a * f1, d_b * f2, d_b * f3, d_gate * f4)], axis=1
    )
    return rounded(norm_back(y, r, rounded(dot_t(d, weight))))


def crop_kernel(
    rows, pair, cot, mask_in, wf_in, wo_in, out,
    x_h, ct_h, wf, wo, chain,
    left, right, in_left, in_right, sig, left_t, right_t, flip_r, flip_s,
    mask, mixed, gate, mid, in_mixed, in_gate, ct32, along,
    saved, d_left, d_right, sig_row, sig_col,
    local_sem, send_sem, recv_sem, psend, precv,
):
    n, c = left.shape[0], left.shape[2]
    lr, lc = out.shape[0], out.shape[1]
    bits = rows.bit_length() - 1
    me, my_col = lax.axis_index("row"), lax.axis_index("col")
    other = 1 - my_col
    me_bits = [lax.rem(lax.div(me, 1 << b), 2) for b in range(bits)]

    def flip(d, low=0):
        total = 0
        for b in range(low, bits):
            bit = me_bits[b]
            total = total + (1 - bit if d >> b & 1 else bit) * (1 << b)
        return total

    barrier = pltpu.get_barrier_semaphore()
    for d in range(1, rows):
        pl.semaphore_signal(barrier, inc=1, device_id={"row": flip(d)}, device_id_type=MESH)
    pl.semaphore_signal(barrier, inc=1, device_id={"col": other}, device_id_type=MESH)

    r0 = pl.multiple_of(me * lr, lr)
    c0 = pl.multiple_of(my_col * lc, lc)
    o0 = pl.multiple_of(other * lc, lc)
    jl = lax.rem(me * lr, lc)
    owner = lax.div(me * lr, lc) == my_col

    own = [
        pltpu.make_async_copy(src, dst.at[pl.ds(r0, lr)], local_sem.at[t])
        for t, (src, dst) in enumerate(((pair, x_h), (cot, ct_h)))
    ]
    weights = [
        pltpu.make_async_copy(wf_in, wf, local_sem.at[2]),
        pltpu.make_async_copy(wo_in, wo, local_sem.at[3]),
    ]
    chain_copy = pltpu.make_async_copy(mask_in, chain, local_sem.at[4])
    for copy in [chain_copy, own[0]] + weights + [own[1]]:
        copy.start()

    def direct(t, d):
        src, dst = ((pair, x_h), (cot, ct_h))[t]
        return pltpu.make_async_remote_copy(
            src_ref=src,
            dst_ref=dst.at[pl.ds(r0, lr)],
            send_sem=send_sem.at[t, d],
            recv_sem=recv_sem.at[t, d],
            device_id={"row": flip(d)},
            device_id_type=MESH,
        )

    used = []

    def partner(src, dst=None):
        q = len(used)
        copy = pltpu.make_async_remote_copy(
            src_ref=src,
            dst_ref=src if dst is None else dst,
            send_sem=psend.at[q],
            recv_sem=precv.at[q],
            device_id={"col": other},
            device_id_type=MESH,
        )
        used.append(copy)
        return copy

    pl.semaphore_wait(barrier, rows)
    for t in range(2):
        for d in range(1, rows):
            direct(t, d).start()

    chain_copy.wait()
    span = jnp.broadcast_to(chain[...].astype(F32), (n, n))
    here = lax.broadcasted_iota(jnp.int32, (n, n), 0) == lax.broadcasted_iota(jnp.int32, (n, n), 1)
    along[...] = jnp.broadcast_to(
        jnp.sum(jnp.where(here, span, 0.0), axis=1, keepdims=True), (n, c)
    )
    across = along[pl.ds(c0, lc), :]
    for i in range(n):
        mask[i * lc : (i + 1) * lc] = across * along[i : i + 1]

    def block(ref, k0, nk):
        return ref[pl.ds(pl.multiple_of(k0 * lc, lc), nk * lc), :]

    def put(ref, k0, nk, v):
        ref[pl.ds(pl.multiple_of(k0 * lc, lc), nk * lc), :] = v

    def put_half(ref, k0, nk, v):
        ref[pl.ds(k0, nk), pl.ds(c0, lc), :] = v.reshape(nk, lc, c)

    def half(ref, k0, nk):
        return ref.at[pl.ds(k0, nk), pl.ds(c0, lc)]

    def projected(x, k0, nk, weight, a_ref, b_ref, g_ref):
        y, _ = norm(x)
        p = dot(y, weight)
        m = block(mask, k0, nk)
        put_half(a_ref, k0, nk, rounded(sigmoid(part(p, 0)) * part(p, 1) * m))
        put_half(b_ref, k0, nk, rounded(sigmoid(part(p, 2)) * part(p, 3) * m))
        put(g_ref, k0, nk, sigmoid(part(p, 4)))

    def triangle(count, width, first, depth, row_at, tile_at, acc=None):
        def term(q, acc):
            t = tile_at(first + q)
            return tuple(v + row_at(a, first + q) * t for a, v in enumerate(acc))

        if acc is None:
            acc = (jnp.zeros((width, c), F32),) * count
        return lax.fori_loop(0, depth, term, tuple(acc), unroll=True)

    def loop(count, step):
        def body(k, carry):
            step(k)
            return carry

        lax.fori_loop(0, count, body, 0)

    for copy in weights:
        copy.wait()
    two = 2 * lr
    e_left, e_right = [], []
    for g in range(rows // 2):
        k0 = pl.multiple_of(flip(2 * g, 1) * lr, two)
        if g == 0:
            own[0].wait()
            direct(0, 1).wait_recv()
        else:
            direct(0, 2 * g).wait_recv()
            direct(0, 2 * g + 1).wait_recv()
        x = x_h[pl.ds(k0, two)].reshape(two * lc, c).astype(F32)
        projected(x, k0, two, wf[0], left, right, gate)
        e_left.append(partner(half(left, k0, two)))
        e_right.append(partner(half(right, k0, two)))
        e_left[-1].start()
        e_right[-1].start()

    group = TILE

    def outgoing(k0, fresh):
        for b in range(lc // TILE):
            t = jnp.swapaxes(right[pl.ds(c0 + b * TILE, TILE), pl.ds(k0, lc), :], 0, 1)
            flip_r[:, b * TILE : (b + 1) * TILE, :] = t

        def step(b):
            i0 = b * group
            base = pl.multiple_of(i0 * lc, lc * group)
            acc = None
            if not fresh:
                acc = [mixed[pl.ds(base + a * lc, lc), :] for a in range(group)]
            acc = triangle(
                group, lc, 0, lc,
                lambda a, q: left[i0 + a, pl.ds(k0 + q, 1), :],
                lambda q: flip_r[q],
                acc,
            )
            for a in range(group):
                mixed[pl.ds(base + a * lc, lc), :] = acc[a]

        loop(n // group, step)

    outgoing(c0, True)
    for copy in e_left + e_right:
        copy.wait_recv()
    outgoing(o0, False)

    some = n // 2
    e_in = []
    for b in range(2):
        k0 = b * some
        z, _ = norm(block(mixed, k0, some))
        x = x_h[pl.ds(k0, some)].reshape(some * lc, c).astype(F32)
        x = rounded(x + block(gate, k0, some) * dot(z, wo[0]))
        put(mid, k0, some, x)
        projected(x, k0, some, wf[1], in_left, in_right, in_gate)
        e_in.append(partner(half(in_left, k0, some)))
        e_in[-1].start()
    e_right = [partner(half(in_right, 0, n))]
    e_right[0].start()

    def incoming(i0):
        def step(b):
            i1 = pl.multiple_of(i0 + b * group, group)
            acc = triangle(
                group, lc, 0, n,
                lambda a, q: in_left[q, pl.ds(i1 + a, 1), :],
                lambda q: in_right[q, pl.ds(c0, lc), :],
            )
            for a in range(group):
                in_mixed[pl.ds(pl.multiple_of((i1 + a) * lc, lc), lc), :] = acc[a]

        loop(lc // group, step)

    nr, nc = lr * lc, lr * n

    def row_of(ref):
        return ref[pl.ds(pl.multiple_of(r0 * lc, lc), nr), :]

    def col_of(ref):
        return jnp.concatenate([ref[pl.ds(jl + a, n, stride=lc), :] for a in range(lr)], axis=0)

    def strips(ref, wide):
        return jnp.concatenate([row_of(ref), col_of(ref)], axis=0) if wide else row_of(ref)

    def each(step):
        @pl.when(owner)
        def _():
            step(True, nr + nc)

        @pl.when(jnp.logical_not(owner))
        def _():
            step(False, nr)

    def transposed(src, dst, j0):
        for b in range(n // TILE):
            t = jnp.swapaxes(src[b * TILE : (b + 1) * TILE, pl.ds(j0, lc), :], 0, 1)
            dst[pl.ds(j0, lc), b * TILE : (b + 1) * TILE, :] = t

    incoming(c0)

    def prepare(wide, m):
        f = factors(strips(mid, wide), strips(mask, wide), wf[1])
        for q, v in enumerate(f):
            saved[q, :m] = jnp.broadcast_to(v, (m, c))
        if wide:
            transposed(in_left, left_t, c0)
            transposed(in_right, right_t, c0)

    each(prepare)
    for copy in e_in:
        copy.wait_recv()
    incoming(o0)

    for d in range(1, rows):
        direct(1, d).wait_recv()
    own[1].wait()

    def signal(i0):
        z, r = norm(block(in_mixed, i0, lc))
        ct = ct_h[pl.ds(i0, lc)].reshape(lc * lc, c).astype(F32)
        put(ct32, i0, lc, ct)
        dz = rounded(dot_t(ct * block(in_gate, i0, lc), wo[1]))
        put_half(sig, i0, lc, rounded(norm_back(z, r, dz)))

    signal(o0)
    e_sig = partner(half(sig, o0, lc))
    e_sig.start()
    signal(c0)
    e_right[0].wait_recv()

    def turn_signal(j0):
        for b in range(lc // TILE):
            t = jnp.swapaxes(sig[pl.ds(c0 + b * TILE, TILE), pl.ds(j0, lc), :], 0, 1)
            flip_s[:, b * TILE : (b + 1) * TILE, :] = t

    def left_row(j0, acc):
        return triangle(
            lr, lc, 0, lc,
            lambda a, q: in_right[r0 + a, pl.ds(j0 + q, 1), :],
            lambda q: flip_s[q],
            acc,
        )

    def left_col(j0, acc):
        return triangle(
            lr, n, 0, lc,
            lambda a, q: sig[r0 + a, pl.ds(j0 + q, 1), :],
            lambda q: right_t[j0 + q],
            acc,
        )

    def keep(ref, start, width, acc, fix=lambda v: v):
        for a in range(lr):
            ref[start + a * width : start + (a + 1) * width] = fix(acc[a])

    def kept(ref, start, width):
        return [ref[start + a * width : start + (a + 1) * width] for a in range(lr)]

    turn_signal(c0)
    keep(d_right, 0, lc, triangle(
        lr, lc, 0, n,
        lambda a, q: in_left[r0 + a, pl.ds(q, 1), :],
        lambda q: sig[q, pl.ds(c0, lc), :],
    ), rounded)
    keep(d_left, 0, lc, left_row(c0, None))

    @pl.when(owner)
    def _():
        transposed(in_left, left_t, o0)
        transposed(in_right, right_t, o0)
        keep(d_right, nr, n, triangle(
            lr, n, 0, n,
            lambda a, q: sig[q, pl.ds(r0 + a, 1), :],
            lambda q: left_t[q],
        ), rounded)
        keep(d_left, nr, n, left_col(c0, None))

    def prepare_more(wide, m):
        z1, _ = norm(strips(in_mixed, wide))
        saved[7, :m] = strips(ct32, wide) * dot(z1, wo[1])

    each(prepare_more)
    e_sig.wait_recv()
    turn_signal(o0)
    keep(d_left, 0, lc, left_row(o0, kept(d_left, 0, lc)), rounded)

    @pl.when(owner)
    def _():
        keep(d_left, nr, n, left_col(o0, kept(d_left, nr, n)), rounded)

    def back(wide, m):
        f = tuple(saved[q, :m] for q in range(7))
        g = rounded(strips(ct32, wide) + front_back(f, wf[1], d_left[:m], d_right[:m], saved[7, :m]))
        z0, r = norm(strips(mixed, wide))
        dz = rounded(dot_t(g * strips(gate, wide), wo[0]))
        s = rounded(norm_back(z0, r, dz))
        along_row = s[:nr].reshape(lr, lc, c)
        sig_row[:, pl.ds(c0, lc), :] = along_row
        saved[8, :nr] = g[:nr]
        if wide:
            sig_col[...] = s[nr:].reshape(lr, n, c)

    each(back)
    e_row = partner(sig_row.at[:, pl.ds(c0, lc)])
    e_row.start()
    e_col = partner(sig_col)

    @pl.when(owner)
    def _():
        e_col.start()

    x = x_h[pl.ds(r0, lr)].reshape(nr, c).astype(F32)
    f = factors(x, row_of(mask), wf[0])
    z0, _ = norm(row_of(mixed))
    g = saved[8, :nr]
    d_gate = g * dot(z0, wo[0])

    def out_left(j0, acc):
        return triangle(
            lr, lc, 0, lc,
            lambda a, q: sig_row[a, pl.ds(j0 + q, 1), :],
            lambda q: right[j0 + q, pl.ds(c0, lc), :],
            acc,
        )

    acc = out_left(c0, None)
    e_row.wait_recv()
    d_a = jnp.concatenate([rounded(v) for v in out_left(o0, acc)], axis=0)

    @pl.when(jnp.logical_not(owner))
    def _():
        e_col.wait_recv()

    d_b = jnp.concatenate([rounded(v) for v in triangle(
        lr, lc, 0, n,
        lambda a, q: sig_col[a, pl.ds(q, 1), :],
        lambda q: left[q, pl.ds(c0, lc), :],
    )], axis=0)
    out[...] = (g + front_back(f, wf[0], d_a, d_b, d_gate)).astype(BF16).reshape(lr, lc, c)

    for t in range(2):
        for d in range(1, rows):
            direct(t, d).wait_send()
    for copy in used:
        if copy is not e_col:
            copy.wait_send()

    @pl.when(owner)
    def _():
        e_col.wait_send()


def from_root(array, axis, root):
    mine = lax.axis_index(axis) == root
    return lax.psum(jnp.where(mine, array, jnp.zeros_like(array)), axis)


def layer_norm(values):
    centred = values - jnp.mean(values, axis=-1, keepdims=True)
    spread = jnp.mean(centred * centred, axis=-1, keepdims=True)
    return centred * lax.rsqrt(spread + 1e-05)


def project_pair(inner_pair, mask_pair, weight):
    normed = layer_norm(inner_pair.astype(jnp.float32)).astype(jnp.bfloat16)
    linear = jnp.dot(normed, weight, preferred_element_type=jnp.float32)
    left_side = jax.nn.sigmoid(linear[..., :H]) * linear[..., H : 2 * H]
    right_side = jax.nn.sigmoid(linear[..., 2 * H : 3 * H]) * linear[..., 3 * H : 4 * H]
    operands = (jnp.stack((left_side, right_side)) * mask_pair[None, :, :, None]).astype(
        jnp.bfloat16
    )
    return (operands, jax.nn.sigmoid(linear[..., 4 * H :]))


def finish(mixed_part, gate_value, inner_pair, weight):
    normed = layer_norm(mixed_part).astype(jnp.bfloat16)
    update = jnp.dot(normed, weight, preferred_element_type=jnp.float32)
    return (inner_pair.astype(jnp.float32) + gate_value * update).astype(jnp.bfloat16)


def body(pair_act, cotangent, residue_mask, front_weight, out_weight):
    local_rows = pair_act.shape[0]
    local_cols = pair_act.shape[1]
    row_index = lax.axis_index("row")
    col_index = lax.axis_index("col")
    block_rows = lax.axis_size("row") // lax.axis_size("col")
    owner_col = row_index // block_rows
    offset = row_index % block_rows * local_rows
    chain_mask = residue_mask.astype(jnp.float32)
    mask_rows = lax.dynamic_slice_in_dim(chain_mask, row_index * local_rows, local_rows)
    mask_cols = lax.dynamic_slice_in_dim(chain_mask, col_index * local_cols, local_cols)
    mask_pair = mask_rows[:, None] * mask_cols[None, :]

    def gather_rows(stacked):
        return lax.all_gather(stacked, "row", axis=1, tiled=True)

    def column_block(gathered):
        slab = lax.dynamic_slice_in_dim(gathered, offset, local_rows, 1)
        return from_root(slab, "col", owner_col)

    def gather_cols(values):
        return lax.all_gather(values, "col", axis=1, tiled=True)

    def sum_cols(partial_term):
        return lax.psum_scatter(
            partial_term.astype(jnp.bfloat16), "col", scatter_dimension=1, tiled=True
        ).astype(jnp.float32)

    (out_ops, out_gate), out_front_back = jax.vjp(
        lambda inner_pair: project_pair(inner_pair, mask_pair, front_weight[0]), pair_act
    )
    fetched = gather_rows(out_ops)
    out_mixed = sum_cols(
        jnp.einsum("ikc,jkc->ijc", out_ops[0], fetched[-1], preferred_element_type=jnp.float32)
    )
    pair_mid, out_finish_back = jax.vjp(
        lambda mixed_part, gate_value, inner_pair: finish(
            mixed_part, gate_value, inner_pair, out_weight[0]
        ),
        out_mixed,
        out_gate,
        pair_act,
    )
    (in_ops, in_gate), in_front_back = jax.vjp(
        lambda inner_pair: project_pair(inner_pair, mask_pair, front_weight[1]), pair_mid
    )
    in_fetched = gather_rows(in_ops)
    left_block = column_block(in_fetched[0])
    in_mixed = jnp.einsum(
        "kic,kjc->ijc", left_block, in_fetched[1], preferred_element_type=jnp.float32
    )
    unused_pair, in_finish_back = jax.vjp(
        lambda mixed_part, gate_value, inner_pair: finish(
            mixed_part, gate_value, inner_pair, out_weight[1]
        ),
        in_mixed,
        in_gate,
        pair_mid,
    )
    grad_mixed, grad_gate, grad_inner = in_finish_back(cotangent)
    signal = grad_mixed.astype(jnp.bfloat16)
    signal_rows = gather_rows(signal[None])[0]
    left_rows = gather_cols(in_ops[0])
    grad_right = jnp.einsum(
        "kic,ijc->kjc", left_rows, signal_rows, preferred_element_type=jnp.float32
    )
    grad_left = sum_cols(
        jnp.einsum("kjc,ijc->kic", in_ops[1], signal_rows, preferred_element_type=jnp.float32)
    )
    (grad_front,) = in_front_back(
        (jnp.stack((grad_left, grad_right)).astype(jnp.bfloat16), grad_gate)
    )
    grad_mid = (grad_inner.astype(jnp.float32) + grad_front.astype(jnp.float32)).astype(
        jnp.bfloat16
    )
    grad_mixed, grad_gate, grad_inner = out_finish_back(grad_mid)
    signal = grad_mixed.astype(jnp.bfloat16)
    signal_cols = gather_cols(signal)
    grad_left = jnp.einsum(
        "ijc,jkc->ikc", signal_cols, fetched[-1], preferred_element_type=jnp.float32
    )
    signal_block = column_block(gather_rows(signal[None])[0])
    grad_right = jnp.einsum(
        "ijc,ikc->jkc", signal_block, fetched[0], preferred_element_type=jnp.float32
    )
    (grad_front,) = out_front_back(
        (jnp.stack((grad_left, grad_right)).astype(jnp.bfloat16), grad_gate)
    )
    return (grad_inner.astype(jnp.float32) + grad_front.astype(jnp.float32)).astype(jnp.bfloat16)


def crop_body(rows, pair_act, cotangent, residue_mask, front_weight, out_weight):
    lr, lc, c = pair_act.shape
    n = residue_mask.shape[0]
    strip = lr * lc + lr * n
    dma = pltpu.SemaphoreType.DMA
    copies = rows + 6
    operands = (pair_act, cotangent, residue_mask.reshape(1, n), front_weight, out_weight)
    return pl.pallas_call(
        functools.partial(crop_kernel, rows),
        out_shape=jax.ShapeDtypeStruct((lr, lc, c), BF16),
        in_specs=[pl.BlockSpec(memory_space=pl.ANY)] * 5,
        out_specs=pl.BlockSpec(memory_space=pltpu.VMEM),
        scratch_shapes=[
            pltpu.VMEM((n, lc, c), BF16),
            pltpu.VMEM((n, lc, c), BF16),
            pltpu.VMEM(front_weight.shape, BF16),
            pltpu.VMEM(out_weight.shape, BF16),
            pltpu.VMEM((1, n), jnp.int32),
        ]
        + [pltpu.VMEM((n, n, c), F32)] * 7
        + [pltpu.VMEM((lc, lc, c), F32)] * 2
        + [pltpu.VMEM((n * lc, c), F32)] * 7
        + [
            pltpu.VMEM((n, c), F32),
            pltpu.VMEM((9, strip, c), F32),
            pltpu.VMEM((strip, c), F32),
            pltpu.VMEM((strip, c), F32),
            pltpu.VMEM((lr, n, c), F32),
            pltpu.VMEM((lr, n, c), F32),
        ]
        + [dma((5,)), dma((2, rows)), dma((2, rows)), dma((copies,)), dma((copies,))],
        compiler_params=pltpu.CompilerParams(
            collective_id=0, has_side_effects=True, vmem_limit_bytes=VMEM_BUDGET
        ),
    )(*[pltpu.with_memory_space_constraint(v, pltpu.HBM) for v in operands])


def fits(mesh, n, lr, lc, c):
    rows, cols = mesh.shape["row"], mesh.shape["col"]
    return (
        cols == 2
        and rows >= 2
        and rows & (rows - 1) == 0
        and n == 2 * lc
        and lc % (2 * TILE) == 0
        and lc % (2 * lr) == 0
        and FULL_ARRAYS * 4 * n * n * c <= VMEM_BUDGET
    )


def solution(mesh):
    def dispatch(pair_act, cotangent, residue_mask, front_weight, out_weight):
        n = residue_mask.shape[0]
        if fits(mesh, n, *pair_act.shape):
            return crop_body(
                mesh.shape["row"], pair_act, cotangent, residue_mask, front_weight, out_weight
            )
        return body(pair_act, cotangent, residue_mask, front_weight, out_weight)

    placed = (P(("grp", "row"), "col", None), P(("grp", "row"), "col", None), P("grp"), P(), P())
    return jax.shard_map(
        dispatch,
        mesh=mesh,
        in_specs=placed,
        out_specs=P(("grp", "row"), "col", None),
        check_vma=False,
    )
```

```python
import functools

import jax
import jax.numpy as jnp
from jax import lax
from jax.experimental import pallas as pl
from jax.experimental.pallas import tpu as pltpu
from jax.sharding import PartitionSpec as P

H = 128
TILE = 8
F32 = jnp.float32
BF16 = jnp.bfloat16
MESH = pl.DeviceIdType.MESH
VMEM_BUDGET = 24 << 20
FULL_ARRAYS = 16


def sigmoid(x):
    return 0.5 * jnp.tanh(0.5 * x) + 0.5


def norm(v):
    centred = v - jnp.mean(v, axis=-1, keepdims=True)
    r = lax.rsqrt(jnp.mean(centred * centred, axis=-1, keepdims=True) + 1e-05)
    return centred * r, r


def norm_back(y, r, d):
    return r * (d - jnp.mean(d, axis=-1, keepdims=True) - y * jnp.mean(d * y, axis=-1, keepdims=True))


def rounded(v):
    return v.astype(BF16).astype(F32)


def dot(a, b):
    return jnp.dot(a.astype(BF16), b, preferred_element_type=F32)


def dot_t(a, b):
    return lax.dot_general(
        a.astype(BF16), b, (((1,), (1,)), ((), ())), preferred_element_type=F32
    )


def part(p, n):
    return p[:, n * H : (n + 1) * H]


def factors(x, mask, weight):
    y, r = norm(x)
    p = dot(y, weight)
    s0, s2, s4 = sigmoid(part(p, 0)), sigmoid(part(p, 2)), sigmoid(part(p, 4))
    fa, fb = mask * s0, mask * s2
    return y, r, fa * part(p, 1) * (1.0 - s0), fa, fb * part(p, 3) * (1.0 - s2), fb, s4 * (1.0 - s4)


def front_back(f, weight, d_a, d_b, d_gate):
    y, r, f0, f1, f2, f3, f4 = f
    d = jnp.concatenate(
        [(v.astype(BF16)) for v in (d_a * f0, d_a * f1, d_b * f2, d_b * f3, d_gate * f4)], axis=1
    )
    return rounded(norm_back(y, r, rounded(dot_t(d, weight))))


def crop_kernel(
    rows, pair, cot, mask_in, wf_in, wo_in, out,
    x_h, ct_h, wf, wo, chain,
    left, right, in_left, in_right, sig, left_t, right_t, flip_r, flip_s,
    mask, mixed, gate, mid, in_mixed, in_gate, ct32, along,
    saved, d_left, d_right, sig_row, sig_col,
    local_sem, send_sem, recv_sem, psend, precv, ready,
):
    n, c = left.shape[0], left.shape[2]
    lr, lc = out.shape[0], out.shape[1]
    bits = rows.bit_length() - 1
    me, my_col = lax.axis_index("row"), lax.axis_index("col")
    other = 1 - my_col
    me_bits = [lax.rem(lax.div(me, 1 << b), 2) for b in range(bits)]

    def flip(d, low=0):
        total = 0
        for b in range(low, bits):
            bit = me_bits[b]
            total = total + (1 - bit if d >> b & 1 else bit) * (1 << b)
        return total

    barrier = pltpu.get_barrier_semaphore()
    pl.semaphore_signal(barrier, inc=1, device_id={"col": other}, device_id_type=MESH)
    for row in range(1, rows):
        @pl.when(me < row)
        def _():
            pl.semaphore_signal(barrier, inc=1, device_id={"row": row}, device_id_type=MESH)

    r0 = pl.multiple_of(me * lr, lr)
    c0 = pl.multiple_of(my_col * lc, lc)
    o0 = pl.multiple_of(other * lc, lc)
    jl = lax.rem(me * lr, lc)
    owner = lax.div(me * lr, lc) == my_col

    own = [
        pltpu.make_async_copy(src, dst.at[pl.ds(r0, lr)], local_sem.at[t])
        for t, (src, dst) in enumerate(((pair, x_h), (cot, ct_h)))
    ]
    weights = [
        pltpu.make_async_copy(wf_in, wf, local_sem.at[2]),
        pltpu.make_async_copy(wo_in, wo, local_sem.at[3]),
    ]
    chain_copy = pltpu.make_async_copy(mask_in, chain, local_sem.at[4])
    for copy in [chain_copy, own[0]] + weights + [own[1]]:
        copy.start()

    def direct(t, row, mine=None):
        src, dst = ((pair, x_h), (cot, ct_h))[t]
        source = row if mine is None else mine
        return pltpu.make_async_remote_copy(
            src_ref=src,
            dst_ref=dst.at[pl.ds(pl.multiple_of(source * lr, lr), lr)],
            send_sem=send_sem.at[t, row],
            recv_sem=recv_sem.at[t, source],
            device_id={"row": row},
            device_id_type=MESH,
        )

    def lower(step):
        for row in range(rows - 1):
            @pl.when(row < me)
            def _():
                step(row)

    def higher(step):
        for row in range(1, rows):
            @pl.when(row > me)
            def _():
                step(row)

    def answer(row):
        pl.semaphore_signal(ready.at[me], inc=1, device_id={"row": row}, device_id_type=MESH)
        direct(0, row, me).start()

    def follow(row):
        pl.semaphore_wait(ready.at[row], 1)
        direct(0, row, me).start()

    def drain(row):
        direct(0, row, me).wait_send()

    def second(row):
        direct(1, row, me).start()

    used = []

    def partner(src, dst=None):
        q = len(used)
        copy = pltpu.make_async_remote_copy(
            src_ref=src,
            dst_ref=src if dst is None else dst,
            send_sem=psend.at[q],
            recv_sem=precv.at[q],
            device_id={"col": other},
            device_id_type=MESH,
        )
        used.append(copy)
        return copy

    pl.semaphore_wait(barrier, me + 1)
    lower(answer)

    chain_copy.wait()
    span = jnp.broadcast_to(chain[...].astype(F32), (n, n))
    here = lax.broadcasted_iota(jnp.int32, (n, n), 0) == lax.broadcasted_iota(jnp.int32, (n, n), 1)
    along[...] = jnp.broadcast_to(
        jnp.sum(jnp.where(here, span, 0.0), axis=1, keepdims=True), (n, c)
    )
    across = along[pl.ds(c0, lc), :]
    for i in range(n):
        mask[i * lc : (i + 1) * lc] = across * along[i : i + 1]

    def block(ref, k0, nk):
        return ref[pl.ds(pl.multiple_of(k0 * lc, lc), nk * lc), :]

    def put(ref, k0, nk, v):
        ref[pl.ds(pl.multiple_of(k0 * lc, lc), nk * lc), :] = v

    def put_half(ref, k0, nk, v):
        ref[pl.ds(k0, nk), pl.ds(c0, lc), :] = v.reshape(nk, lc, c)

    def half(ref, k0, nk):
        return ref.at[pl.ds(k0, nk), pl.ds(c0, lc)]

    def projected(x, segments, weight, a_ref, b_ref, g_ref):
        y, _ = norm(x)
        p = dot(y, weight)
        m = jnp.concatenate([block(mask, k0, nk) for k0, nk in segments], axis=0)
        a = rounded(sigmoid(part(p, 0)) * part(p, 1) * m)
        b = rounded(sigmoid(part(p, 2)) * part(p, 3) * m)
        g = sigmoid(part(p, 4))
        at = 0
        for k0, nk in segments:
            span = slice(at * lc, (at + nk) * lc)
            put_half(a_ref, k0, nk, a[span])
            put_half(b_ref, k0, nk, b[span])
            put(g_ref, k0, nk, g[span])
            at += nk

    def triangle(count, width, first, depth, row_at, tile_at, acc=None):
        def term(q, acc):
            t = tile_at(first + q)
            return tuple(v + row_at(a, first + q) * t for a, v in enumerate(acc))

        if acc is None:
            acc = (jnp.zeros((width, c), F32),) * count
        return lax.fori_loop(0, depth, term, tuple(acc), unroll=True)

    def loop(count, step):
        def body(k, carry):
            step(k)
            return carry

        lax.fori_loop(0, count, body, 0)

    for copy in weights:
        copy.wait()
    e_left, e_right = [], []
    groups = [[(0, 1)], [(1, 1), (2, 2)], [(4, 2)], [(6, 2)]]
    for g, group in enumerate(groups):
        for d, count in group:
            for q in range(d, d + count):
                if q == 0:
                    own[0].wait()
                else:
                    direct(0, flip(q)).wait_recv()
        segments = [
            (pl.multiple_of(flip(d, count.bit_length() - 1) * lr, count * lr), count * lr)
            for d, count in group
        ]
        x = jnp.concatenate(
            [x_h[pl.ds(k0, nk)].reshape(nk * lc, c).astype(F32) for k0, nk in segments], axis=0
        )
        projected(x, segments, wf[0], left, right, gate)
        for k0, nk in segments:
            e_left.append(partner(half(left, k0, nk)))
            e_right.append(partner(half(right, k0, nk)))
            e_left[-1].start()
            e_right[-1].start()
        if g == 0:
            higher(follow)
            lower(drain)
            e_left[0].wait_recv()
            lower(second)
        if g == 3:
            higher(second)

    group = TILE

    def outgoing(k0, fresh):
        for b in range(lc // TILE):
            t = jnp.swapaxes(right[pl.ds(c0 + b * TILE, TILE), pl.ds(k0, lc), :], 0, 1)
            flip_r[:, b * TILE : (b + 1) * TILE, :] = t

        def step(b):
            i0 = b * group
            base = pl.multiple_of(i0 * lc, lc * group)
            acc = None
            if not fresh:
                acc = [mixed[pl.ds(base + a * lc, lc), :] for a in range(group)]
            acc = triangle(
                group, lc, 0, lc,
                lambda a, q: left[i0 + a, pl.ds(k0 + q, 1), :],
                lambda q: flip_r[q],
                acc,
            )
            for a in range(group):
                mixed[pl.ds(base + a * lc, lc), :] = acc[a]

        loop(n // group, step)

    outgoing(c0, True)
    for copy in e_left[1:] + e_right:
        copy.wait_recv()
    outgoing(o0, False)

    some = n // 2
    e_in = []
    for b in range(2):
        k0 = b * some
        z, _ = norm(block(mixed, k0, some))
        x = x_h[pl.ds(k0, some)].reshape(some * lc, c).astype(F32)
        x = rounded(x + block(gate, k0, some) * dot(z, wo[0]))
        put(mid, k0, some, x)
        projected(x, [(k0, some)], wf[1], in_left, in_right, in_gate)
        e_in.append(partner(half(in_left, k0, some)))
        e_in[-1].start()
    e_right = [partner(half(in_right, 0, n))]
    e_right[0].start()

    def incoming(i0):
        def step(b):
            i1 = pl.multiple_of(i0 + b * group, group)
            acc = triangle(
                group, lc, 0, n,
                lambda a, q: in_left[q, pl.ds(i1 + a, 1), :],
                lambda q: in_right[q, pl.ds(c0, lc), :],
            )
            for a in range(group):
                in_mixed[pl.ds(pl.multiple_of((i1 + a) * lc, lc), lc), :] = acc[a]

        loop(lc // group, step)

    nr, nc = lr * lc, lr * n

    def row_of(ref):
        return ref[pl.ds(pl.multiple_of(r0 * lc, lc), nr), :]

    def col_of(ref):
        return jnp.concatenate([ref[pl.ds(jl + a, n, stride=lc), :] for a in range(lr)], axis=0)

    def strips(ref, wide):
        return jnp.concatenate([row_of(ref), col_of(ref)], axis=0) if wide else row_of(ref)

    def each(step):
        @pl.when(owner)
        def _():
            step(True, nr + nc)

        @pl.when(jnp.logical_not(owner))
        def _():
            step(False, nr)

    def transposed(src, dst, j0):
        for b in range(n // TILE):
            t = jnp.swapaxes(src[b * TILE : (b + 1) * TILE, pl.ds(j0, lc), :], 0, 1)
            dst[pl.ds(j0, lc), b * TILE : (b + 1) * TILE, :] = t

    incoming(c0)

    def prepare(wide, m):
        f = factors(strips(mid, wide), strips(mask, wide), wf[1])
        for q, v in enumerate(f):
            saved[q, :m] = jnp.broadcast_to(v, (m, c))
        if wide:
            transposed(in_left, left_t, c0)
            transposed(in_right, right_t, c0)

    each(prepare)
    for copy in e_in:
        copy.wait_recv()
    incoming(o0)

    for d in range(1, rows):
        direct(1, flip(d)).wait_recv()
    own[1].wait()

    def signal(i0):
        z, r = norm(block(in_mixed, i0, lc))
        ct = ct_h[pl.ds(i0, lc)].reshape(lc * lc, c).astype(F32)
        put(ct32, i0, lc, ct)
        dz = rounded(dot_t(ct * block(in_gate, i0, lc), wo[1]))
        put_half(sig, i0, lc, rounded(norm_back(z, r, dz)))

    signal(o0)
    e_sig = partner(half(sig, o0, lc))
    e_sig.start()
    signal(c0)
    e_right[0].wait_recv()

    def turn_signal(j0):
        for b in range(lc // TILE):
            t = jnp.swapaxes(sig[pl.ds(c0 + b * TILE, TILE), pl.ds(j0, lc), :], 0, 1)
            flip_s[:, b * TILE : (b + 1) * TILE, :] = t

    def left_row(j0, acc):
        return triangle(
            lr, lc, 0, lc,
            lambda a, q: in_right[r0 + a, pl.ds(j0 + q, 1), :],
            lambda q: flip_s[q],
            acc,
        )

    def left_col(j0, acc):
        return triangle(
            lr, n, 0, lc,
            lambda a, q: sig[r0 + a, pl.ds(j0 + q, 1), :],
            lambda q: right_t[j0 + q],
            acc,
        )

    def keep(ref, start, width, acc, fix=lambda v: v):
        for a in range(lr):
            ref[start + a * width : start + (a + 1) * width] = fix(acc[a])

    def kept(ref, start, width):
        return [ref[start + a * width : start + (a + 1) * width] for a in range(lr)]

    turn_signal(c0)
    keep(d_right, 0, lc, triangle(
        lr, lc, 0, n,
        lambda a, q: in_left[r0 + a, pl.ds(q, 1), :],
        lambda q: sig[q, pl.ds(c0, lc), :],
    ), rounded)
    keep(d_left, 0, lc, left_row(c0, None))

    @pl.when(owner)
    def _():
        transposed(in_left, left_t, o0)
        transposed(in_right, right_t, o0)
        keep(d_right, nr, n, triangle(
            lr, n, 0, n,
            lambda a, q: sig[q, pl.ds(r0 + a, 1), :],
            lambda q: left_t[q],
        ), rounded)
        keep(d_left, nr, n, left_col(c0, None))

    def prepare_more(wide, m):
        z1, _ = norm(strips(in_mixed, wide))
        saved[7, :m] = strips(ct32, wide) * dot(z1, wo[1])

    each(prepare_more)
    e_sig.wait_recv()
    turn_signal(o0)
    keep(d_left, 0, lc, left_row(o0, kept(d_left, 0, lc)), rounded)

    @pl.when(owner)
    def _():
        keep(d_left, nr, n, left_col(o0, kept(d_left, nr, n)), rounded)

    def back(wide, m):
        f = tuple(saved[q, :m] for q in range(7))
        g = rounded(strips(ct32, wide) + front_back(f, wf[1], d_left[:m], d_right[:m], saved[7, :m]))
        z0, r = norm(strips(mixed, wide))
        dz = rounded(dot_t(g * strips(gate, wide), wo[0]))
        s = rounded(norm_back(z0, r, dz))
        along_row = s[:nr].reshape(lr, lc, c)
        sig_row[:, pl.ds(c0, lc), :] = along_row
        saved[8, :nr] = g[:nr]
        if wide:
            sig_col[...] = s[nr:].reshape(lr, n, c)

    each(back)
    e_row = partner(sig_row.at[:, pl.ds(c0, lc)])
    e_row.start()
    e_col = partner(sig_col)

    @pl.when(owner)
    def _():
        e_col.start()

    x = x_h[pl.ds(r0, lr)].reshape(nr, c).astype(F32)
    f = factors(x, row_of(mask), wf[0])
    z0, _ = norm(row_of(mixed))
    g = saved[8, :nr]
    d_gate = g * dot(z0, wo[0])

    def out_left(j0, acc):
        return triangle(
            lr, lc, 0, lc,
            lambda a, q: sig_row[a, pl.ds(j0 + q, 1), :],
            lambda q: right[j0 + q, pl.ds(c0, lc), :],
            acc,
        )

    acc = out_left(c0, None)
    e_row.wait_recv()
    d_a = jnp.concatenate([rounded(v) for v in out_left(o0, acc)], axis=0)

    @pl.when(jnp.logical_not(owner))
    def _():
        e_col.wait_recv()

    d_b = jnp.concatenate([rounded(v) for v in triangle(
        lr, lc, 0, n,
        lambda a, q: sig_col[a, pl.ds(q, 1), :],
        lambda q: left[q, pl.ds(c0, lc), :],
    )], axis=0)
    out[...] = (g + front_back(f, wf[0], d_a, d_b, d_gate)).astype(BF16).reshape(lr, lc, c)

    higher(drain)
    for d in range(1, rows):
        direct(1, flip(d)).wait_send()
    for copy in used:
        if copy is not e_col:
            copy.wait_send()

    @pl.when(owner)
    def _():
        e_col.wait_send()


def from_root(array, axis, root):
    mine = lax.axis_index(axis) == root
    return lax.psum(jnp.where(mine, array, jnp.zeros_like(array)), axis)


def layer_norm(values):
    centred = values - jnp.mean(values, axis=-1, keepdims=True)
    spread = jnp.mean(centred * centred, axis=-1, keepdims=True)
    return centred * lax.rsqrt(spread + 1e-05)


def project_pair(inner_pair, mask_pair, weight):
    normed = layer_norm(inner_pair.astype(jnp.float32)).astype(jnp.bfloat16)
    linear = jnp.dot(normed, weight, preferred_element_type=jnp.float32)
    left_side = jax.nn.sigmoid(linear[..., :H]) * linear[..., H : 2 * H]
    right_side = jax.nn.sigmoid(linear[..., 2 * H : 3 * H]) * linear[..., 3 * H : 4 * H]
    operands = (jnp.stack((left_side, right_side)) * mask_pair[None, :, :, None]).astype(
        jnp.bfloat16
    )
    return (operands, jax.nn.sigmoid(linear[..., 4 * H :]))


def finish(mixed_part, gate_value, inner_pair, weight):
    normed = layer_norm(mixed_part).astype(jnp.bfloat16)
    update = jnp.dot(normed, weight, preferred_element_type=jnp.float32)
    return (inner_pair.astype(jnp.float32) + gate_value * update).astype(jnp.bfloat16)


def body(pair_act, cotangent, residue_mask, front_weight, out_weight):
    local_rows = pair_act.shape[0]
    local_cols = pair_act.shape[1]
    row_index = lax.axis_index("row")
    col_index = lax.axis_index("col")
    block_rows = lax.axis_size("row") // lax.axis_size("col")
    owner_col = row_index // block_rows
    offset = row_index % block_rows * local_rows
    chain_mask = residue_mask.astype(jnp.float32)
    mask_rows = lax.dynamic_slice_in_dim(chain_mask, row_index * local_rows, local_rows)
    mask_cols = lax.dynamic_slice_in_dim(chain_mask, col_index * local_cols, local_cols)
    mask_pair = mask_rows[:, None] * mask_cols[None, :]

    def gather_rows(stacked):
        return lax.all_gather(stacked, "row", axis=1, tiled=True)

    def column_block(gathered):
        slab = lax.dynamic_slice_in_dim(gathered, offset, local_rows, 1)
        return from_root(slab, "col", owner_col)

    def gather_cols(values):
        return lax.all_gather(values, "col", axis=1, tiled=True)

    def sum_cols(partial_term):
        return lax.psum_scatter(
            partial_term.astype(jnp.bfloat16), "col", scatter_dimension=1, tiled=True
        ).astype(jnp.float32)

    (out_ops, out_gate), out_front_back = jax.vjp(
        lambda inner_pair: project_pair(inner_pair, mask_pair, front_weight[0]), pair_act
    )
    fetched = gather_rows(out_ops)
    out_mixed = sum_cols(
        jnp.einsum("ikc,jkc->ijc", out_ops[0], fetched[-1], preferred_element_type=jnp.float32)
    )
    pair_mid, out_finish_back = jax.vjp(
        lambda mixed_part, gate_value, inner_pair: finish(
            mixed_part, gate_value, inner_pair, out_weight[0]
        ),
        out_mixed,
        out_gate,
        pair_act,
    )
    (in_ops, in_gate), in_front_back = jax.vjp(
        lambda inner_pair: project_pair(inner_pair, mask_pair, front_weight[1]), pair_mid
    )
    in_fetched = gather_rows(in_ops)
    left_block = column_block(in_fetched[0])
    in_mixed = jnp.einsum(
        "kic,kjc->ijc", left_block, in_fetched[1], preferred_element_type=jnp.float32
    )
    unused_pair, in_finish_back = jax.vjp(
        lambda mixed_part, gate_value, inner_pair: finish(
            mixed_part, gate_value, inner_pair, out_weight[1]
        ),
        in_mixed,
        in_gate,
        pair_mid,
    )
    grad_mixed, grad_gate, grad_inner = in_finish_back(cotangent)
    signal = grad_mixed.astype(jnp.bfloat16)
    signal_rows = gather_rows(signal[None])[0]
    left_rows = gather_cols(in_ops[0])
    grad_right = jnp.einsum(
        "kic,ijc->kjc", left_rows, signal_rows, preferred_element_type=jnp.float32
    )
    grad_left = sum_cols(
        jnp.einsum("kjc,ijc->kic", in_ops[1], signal_rows, preferred_element_type=jnp.float32)
    )
    (grad_front,) = in_front_back(
        (jnp.stack((grad_left, grad_right)).astype(jnp.bfloat16), grad_gate)
    )
    grad_mid = (grad_inner.astype(jnp.float32) + grad_front.astype(jnp.float32)).astype(
        jnp.bfloat16
    )
    grad_mixed, grad_gate, grad_inner = out_finish_back(grad_mid)
    signal = grad_mixed.astype(jnp.bfloat16)
    signal_cols = gather_cols(signal)
    grad_left = jnp.einsum(
        "ijc,jkc->ikc", signal_cols, fetched[-1], preferred_element_type=jnp.float32
    )
    signal_block = column_block(gather_rows(signal[None])[0])
    grad_right = jnp.einsum(
        "ijc,ikc->jkc", signal_block, fetched[0], preferred_element_type=jnp.float32
    )
    (grad_front,) = out_front_back(
        (jnp.stack((grad_left, grad_right)).astype(jnp.bfloat16), grad_gate)
    )
    return (grad_inner.astype(jnp.float32) + grad_front.astype(jnp.float32)).astype(jnp.bfloat16)


def crop_body(rows, pair_act, cotangent, residue_mask, front_weight, out_weight):
    lr, lc, c = pair_act.shape
    n = residue_mask.shape[0]
    strip = lr * lc + lr * n
    dma = pltpu.SemaphoreType.DMA
    copies = 2 * rows + 6
    operands = (pair_act, cotangent, residue_mask.reshape(1, n), front_weight, out_weight)
    return pl.pallas_call(
        functools.partial(crop_kernel, rows),
        out_shape=jax.ShapeDtypeStruct((lr, lc, c), BF16),
        in_specs=[pl.BlockSpec(memory_space=pl.ANY)] * 5,
        out_specs=pl.BlockSpec(memory_space=pltpu.VMEM),
        scratch_shapes=[
            pltpu.VMEM((n, lc, c), BF16),
            pltpu.VMEM((n, lc, c), BF16),
            pltpu.VMEM(front_weight.shape, BF16),
            pltpu.VMEM(out_weight.shape, BF16),
            pltpu.VMEM((1, n), jnp.int32),
        ]
        + [pltpu.VMEM((n, n, c), F32)] * 7
        + [pltpu.VMEM((lc, lc, c), F32)] * 2
        + [pltpu.VMEM((n * lc, c), F32)] * 7
        + [
            pltpu.VMEM((n, c), F32),
            pltpu.VMEM((9, strip, c), F32),
            pltpu.VMEM((strip, c), F32),
            pltpu.VMEM((strip, c), F32),
            pltpu.VMEM((lr, n, c), F32),
            pltpu.VMEM((lr, n, c), F32),
        ]
        + [dma((5,)), dma((2, rows)), dma((2, rows)), dma((copies,)), dma((copies,))]
        + [pltpu.SemaphoreType.REGULAR((rows,))],
        compiler_params=pltpu.CompilerParams(
            collective_id=0, has_side_effects=True, vmem_limit_bytes=VMEM_BUDGET
        ),
    )(*[pltpu.with_memory_space_constraint(v, pltpu.HBM) for v in operands])


def fits(mesh, n, lr, lc, c):
    rows, cols = mesh.shape["row"], mesh.shape["col"]
    return (
        cols == 2
        and rows >= 2
        and rows & (rows - 1) == 0
        and n == 2 * lc
        and lc % (2 * TILE) == 0
        and lc % (2 * lr) == 0
        and FULL_ARRAYS * 4 * n * n * c <= VMEM_BUDGET
    )


def solution(mesh):
    def dispatch(pair_act, cotangent, residue_mask, front_weight, out_weight):
        n = residue_mask.shape[0]
        if fits(mesh, n, *pair_act.shape):
            return crop_body(
                mesh.shape["row"], pair_act, cotangent, residue_mask, front_weight, out_weight
            )
        return body(pair_act, cotangent, residue_mask, front_weight, out_weight)

    placed = (P(("grp", "row"), "col", None), P(("grp", "row"), "col", None), P("grp"), P(), P())
    return jax.shard_map(
        dispatch,
        mesh=mesh,
        in_specs=placed,
        out_specs=P(("grp", "row"), "col", None),
        check_vma=False,
    )
```

```python
import functools

import jax
import jax.numpy as jnp
from jax import lax
from jax.experimental import pallas as pl
from jax.experimental.pallas import tpu as pltpu
from jax.sharding import PartitionSpec as P

H = 128
TILE = 8
F32 = jnp.float32
BF16 = jnp.bfloat16
MESH = pl.DeviceIdType.MESH
VMEM_BUDGET = 24 << 20
FULL_ARRAYS = 16


def sigmoid(x):
    return 0.5 * jnp.tanh(0.5 * x) + 0.5


def norm(v):
    centred = v - jnp.mean(v, axis=-1, keepdims=True)
    r = lax.rsqrt(jnp.mean(centred * centred, axis=-1, keepdims=True) + 1e-05)
    return centred * r, r


def norm_back(y, r, d):
    return r * (d - jnp.mean(d, axis=-1, keepdims=True) - y * jnp.mean(d * y, axis=-1, keepdims=True))


def rounded(v):
    return v.astype(BF16).astype(F32)


def dot(a, b):
    return jnp.dot(a.astype(BF16), b, preferred_element_type=F32)


def dot_t(a, b):
    return lax.dot_general(
        a.astype(BF16), b, (((1,), (1,)), ((), ())), preferred_element_type=F32
    )


def part(p, n):
    return p[:, n * H : (n + 1) * H]


def factors(x, mask, weight):
    y, r = norm(x)
    p = dot(y, weight)
    s0, s2, s4 = sigmoid(part(p, 0)), sigmoid(part(p, 2)), sigmoid(part(p, 4))
    fa, fb = mask * s0, mask * s2
    return y, r, fa * part(p, 1) * (1.0 - s0), fa, fb * part(p, 3) * (1.0 - s2), fb, s4 * (1.0 - s4)


def front_back(f, weight, d_a, d_b, d_gate):
    y, r, f0, f1, f2, f3, f4 = f
    d = jnp.concatenate(
        [(v.astype(BF16)) for v in (d_a * f0, d_a * f1, d_b * f2, d_b * f3, d_gate * f4)], axis=1
    )
    return rounded(norm_back(y, r, rounded(dot_t(d, weight))))


def crop_kernel(
    rows, pair, cot, mask_in, wf_in, wo_in, out,
    x_h, ct_h, wf, wo, chain,
    left, right, in_left, in_right, sig, left_t, right_t, flip_r, flip_s,
    mask, mixed, gate, mid, in_mixed, in_gate, ct32, normed, along,
    saved, d_left, d_right, sig_row, sig_col,
    local_sem, x_send, x_recv, ct_send, ct_recv, psend, precv, ready,
):
    n, c = left.shape[0], left.shape[2]
    lr, lc = out.shape[0], out.shape[1]
    bits = rows.bit_length() - 1
    me, my_col = lax.axis_index("row"), lax.axis_index("col")
    other = 1 - my_col
    me_bits = [lax.rem(lax.div(me, 1 << b), 2) for b in range(bits)]

    def flip(d, low=0):
        total = 0
        for b in range(low, bits):
            bit = me_bits[b]
            total = total + (1 - bit if d >> b & 1 else bit) * (1 << b)
        return total

    barrier = pltpu.get_barrier_semaphore()
    pl.semaphore_signal(barrier, inc=1, device_id={"col": other}, device_id_type=MESH)
    for row in range(1, rows):
        @pl.when(me < row)
        def _():
            pl.semaphore_signal(barrier, inc=1, device_id={"row": row}, device_id_type=MESH)

    r0 = pl.multiple_of(me * lr, lr)
    c0 = pl.multiple_of(my_col * lc, lc)
    o0 = pl.multiple_of(other * lc, lc)
    jl = lax.rem(me * lr, lc)
    owner = lax.div(me * lr, lc) == my_col

    own = [
        pltpu.make_async_copy(src, dst.at[pl.ds(r0, lr)], local_sem.at[t])
        for t, (src, dst) in enumerate(((pair, x_h), (cot, ct_h)))
    ]
    weights = [
        pltpu.make_async_copy(wf_in, wf, local_sem.at[2]),
        pltpu.make_async_copy(wo_in, wo, local_sem.at[3]),
    ]
    chain_copy = pltpu.make_async_copy(mask_in, chain, local_sem.at[4])
    for copy in [chain_copy, own[0]] + weights + [own[1]]:
        copy.start()

    def direct(t, row, mine=None):
        src, dst = ((pair, x_h), (cot, ct_h))[t]
        source = row if mine is None else mine
        return pltpu.make_async_remote_copy(
            src_ref=src,
            dst_ref=dst.at[pl.ds(pl.multiple_of(source * lr, lr), lr)],
            send_sem=x_send.at[row] if t == 0 else ct_send.at[0],
            recv_sem=x_recv.at[source] if t == 0 else ct_recv.at[0],
            device_id={"row": row},
            device_id_type=MESH,
        )

    def lower(step):
        for row in range(rows - 1):
            @pl.when(row < me)
            def _():
                step(row)

    def higher(step):
        for row in range(1, rows):
            @pl.when(row > me)
            def _():
                step(row)

    def answer(row):
        if row < 2:
            direct(0, row, me).start()
        pl.semaphore_signal(ready.at[me], inc=1, device_id={"row": row}, device_id_type=MESH)

    def send(row):
        if row >= 2:
            direct(0, row, me).start()

    def follow(row):
        pl.semaphore_wait(ready.at[row], 1)
        direct(0, row, me).start()

    def drain(row):
        direct(0, row, me).wait_send()

    def second(row):
        direct(1, row, me).start()

    def partner(q, ref):
        return pltpu.make_async_remote_copy(
            src_ref=ref,
            dst_ref=ref,
            send_sem=psend.at[q],
            recv_sem=precv.at[q],
            device_id={"col": other},
            device_id_type=MESH,
        )

    pl.semaphore_wait(barrier, me + 1)
    lower(answer)

    chain_copy.wait()
    span = jnp.broadcast_to(chain[...].astype(F32), (n, n))
    here = lax.broadcasted_iota(jnp.int32, (n, n), 0) == lax.broadcasted_iota(jnp.int32, (n, n), 1)
    along[...] = jnp.broadcast_to(
        jnp.sum(jnp.where(here, span, 0.0), axis=1, keepdims=True), (n, c)
    )
    across = along[pl.ds(c0, lc), :]
    for i in range(n):
        mask[i * lc : (i + 1) * lc] = across * along[i : i + 1]
    lower(send)

    def block(ref, k0, nk):
        return ref[pl.ds(pl.multiple_of(k0 * lc, lc), nk * lc), :]

    def put(ref, k0, nk, v):
        ref[pl.ds(pl.multiple_of(k0 * lc, lc), nk * lc), :] = v

    def put_half(ref, k0, nk, v):
        ref[pl.ds(k0, nk), pl.ds(c0, lc), :] = v.reshape(nk, lc, c)

    def half(ref, k0, nk):
        return ref.at[pl.ds(k0, nk), pl.ds(c0, lc)]

    def projected(x, segments, weight, a_ref, b_ref, g_ref):
        y, _ = norm(x)
        p = dot(y, weight)
        m = jnp.concatenate([block(mask, k0, nk) for k0, nk in segments], axis=0)
        a = rounded(sigmoid(part(p, 0)) * part(p, 1) * m)
        b = rounded(sigmoid(part(p, 2)) * part(p, 3) * m)
        g = sigmoid(part(p, 4))
        at = 0
        for k0, nk in segments:
            span = slice(at * lc, (at + nk) * lc)
            put_half(a_ref, k0, nk, a[span])
            put_half(b_ref, k0, nk, b[span])
            put(g_ref, k0, nk, g[span])
            at += nk

    def triangle(count, width, first, depth, row_at, tile_at, acc=None):
        def term(q, acc):
            t = tile_at(first + q)
            return tuple(v + row_at(a, first + q) * t for a, v in enumerate(acc))

        if acc is None:
            acc = (jnp.zeros((width, c), F32),) * count
        return lax.fori_loop(0, depth, term, tuple(acc), unroll=True)

    def loop(count, step):
        def body(k, carry):
            step(k)
            return carry

        lax.fori_loop(0, count, body, 0)

    for copy in weights:
        copy.wait()
    groups = [[(0, 1)], [(1, 1), (2, 2)] if rows > 2 else [(1, 1)]]
    groups += [[(d, 2)] for d in range(4, rows, 2)]
    for g, group in enumerate(groups):
        for d, count in group:
            for q in range(d, d + count):
                if q == 0:
                    own[0].wait()
                else:
                    direct(0, flip(q)).wait_recv()
        segments = [
            (pl.multiple_of(flip(d, count.bit_length() - 1) * lr, count * lr), count * lr)
            for d, count in group
        ]
        x = jnp.concatenate(
            [x_h[pl.ds(k0, nk)].reshape(nk * lc, c).astype(F32) for k0, nk in segments], axis=0
        )
        projected(x, segments, wf[0], left, right, gate)
        for k0, nk in segments:
            partner(0 if g == 0 else 1, half(left, k0, nk)).start()
            partner(2, half(right, k0, nk)).start()
        if g == 0:
            higher(follow)
            lower(drain)
            partner(0, half(left, r0, lr)).wait_recv()
            lower(second)
        if g == len(groups) - 1:
            higher(second)

    group = TILE

    def outgoing(k0, fresh):
        for b in range(lc // TILE):
            t = jnp.swapaxes(right[pl.ds(c0 + b * TILE, TILE), pl.ds(k0, lc), :], 0, 1)
            flip_r[:, b * TILE : (b + 1) * TILE, :] = t

        def step(b):
            i0 = b * group
            base = pl.multiple_of(i0 * lc, lc * group)
            acc = None
            if not fresh:
                acc = [mixed[pl.ds(base + a * lc, lc), :] for a in range(group)]
            acc = triangle(
                group, lc, 0, lc,
                lambda a, q: left[i0 + a, pl.ds(k0 + q, 1), :],
                lambda q: flip_r[q],
                acc,
            )
            for a in range(group):
                mixed[pl.ds(base + a * lc, lc), :] = acc[a]

        loop(n // group, step)

    outgoing(c0, True)
    e_left = [partner(0, half(left, r0, lr)), partner(1, half(left, 0, n - lr))]
    e_right = partner(2, half(right, 0, n))
    e_left[1].wait_recv()
    e_right.wait_recv()
    outgoing(o0, False)

    z, _ = norm(mixed[...])
    x = x_h[...].reshape(n * lc, c).astype(F32)
    x = rounded(x + gate[...] * dot(z, wo[0]))
    mid[...] = x
    y = norm(x)[0].astype(BF16)
    normed[...] = y
    p = dot(y, wf[1, :, : 2 * H])
    put_half(in_left, 0, n, rounded(sigmoid(part(p, 0)) * part(p, 1) * mask[...]))
    e_in_left = partner(3, half(in_left, 0, n))
    e_in_left.start()
    p = dot(normed[...], wf[1, :, 2 * H :])
    put_half(in_right, 0, n, rounded(sigmoid(part(p, 0)) * part(p, 1) * mask[...]))
    in_gate[...] = sigmoid(part(p, 2))
    e_in_right = partner(4, half(in_right, 0, n))
    e_in_right.start()

    def incoming(i0):
        def step(b):
            i1 = pl.multiple_of(i0 + b * group, group)
            acc = triangle(
                group, lc, 0, n,
                lambda a, q: in_left[q, pl.ds(i1 + a, 1), :],
                lambda q: in_right[q, pl.ds(c0, lc), :],
            )
            for a in range(group):
                in_mixed[pl.ds(pl.multiple_of((i1 + a) * lc, lc), lc), :] = acc[a]

        loop(lc // group, step)

    nr, nc = lr * lc, lr * n

    def row_of(ref):
        return ref[pl.ds(pl.multiple_of(r0 * lc, lc), nr), :]

    def col_of(ref):
        return jnp.concatenate([ref[pl.ds(jl + a, n, stride=lc), :] for a in range(lr)], axis=0)

    def strips(ref, wide):
        return jnp.concatenate([row_of(ref), col_of(ref)], axis=0) if wide else row_of(ref)

    def each(step, here=True):
        @pl.when(jnp.logical_and(here, owner))
        def _():
            step(True, nr + nc)

        @pl.when(jnp.logical_and(here, jnp.logical_not(owner)))
        def _():
            step(False, nr)

    def transposed(src, dst, j0):
        for b in range(n // TILE):
            t = jnp.swapaxes(src[b * TILE : (b + 1) * TILE, pl.ds(j0, lc), :], 0, 1)
            dst[pl.ds(j0, lc), b * TILE : (b + 1) * TILE, :] = t

    incoming(c0)

    def prepare(wide, m):
        f = factors(strips(mid, wide), strips(mask, wide), wf[1])
        for q, v in enumerate(f):
            saved[q, :m] = jnp.broadcast_to(v, (m, c))

    each(prepare, my_col == 0)

    @pl.when(jnp.logical_and(my_col == 0, owner))
    def _():
        transposed(in_left, left_t, c0)
        transposed(in_right, right_t, c0)

    e_in_left.wait_recv()
    incoming(o0)

    others = pl.ds(0, (rows - 1) * lr)
    e_ct = pltpu.make_async_remote_copy(
        src_ref=ct_h.at[others],
        dst_ref=ct_h.at[others],
        send_sem=ct_send.at[0],
        recv_sem=ct_recv.at[0],
        device_id={"col": other},
        device_id_type=MESH,
    )
    e_ct.wait_recv()
    own[1].wait()

    def signal(i0):
        z, r = norm(block(in_mixed, i0, lc))
        ct = ct_h[pl.ds(i0, lc)].reshape(lc * lc, c).astype(F32)
        put(ct32, i0, lc, ct)
        dz = rounded(dot_t(ct * block(in_gate, i0, lc), wo[1]))
        put_half(sig, i0, lc, rounded(norm_back(z, r, dz)))

    signal(o0)
    e_sig = partner(5, half(sig, o0, lc))
    e_sig.start()
    signal(c0)
    e_in_right.wait_recv()

    def turn_signal(j0):
        for b in range(lc // TILE):
            t = jnp.swapaxes(sig[pl.ds(c0 + b * TILE, TILE), pl.ds(j0, lc), :], 0, 1)
            flip_s[:, b * TILE : (b + 1) * TILE, :] = t

    def left_row(j0, acc):
        return triangle(
            lr, lc, 0, lc,
            lambda a, q: in_right[r0 + a, pl.ds(j0 + q, 1), :],
            lambda q: flip_s[q],
            acc,
        )

    def left_col(j0, acc):
        return triangle(
            lr, n, 0, lc,
            lambda a, q: sig[r0 + a, pl.ds(j0 + q, 1), :],
            lambda q: right_t[j0 + q],
            acc,
        )

    def keep(ref, start, width, acc, fix=lambda v: v):
        for a in range(lr):
            ref[start + a * width : start + (a + 1) * width] = fix(acc[a])

    def kept(ref, start, width):
        return [ref[start + a * width : start + (a + 1) * width] for a in range(lr)]

    turn_signal(c0)
    keep(d_right, 0, lc, triangle(
        lr, lc, 0, n,
        lambda a, q: in_left[r0 + a, pl.ds(q, 1), :],
        lambda q: sig[q, pl.ds(c0, lc), :],
    ), rounded)
    keep(d_left, 0, lc, left_row(c0, None))

    @pl.when(owner)
    def _():
        @pl.when(my_col != 0)
        def _():
            transposed(in_left, left_t, c0)
            transposed(in_right, right_t, c0)

        transposed(in_left, left_t, o0)
        transposed(in_right, right_t, o0)
        keep(d_right, nr, n, triangle(
            lr, n, 0, n,
            lambda a, q: sig[q, pl.ds(r0 + a, 1), :],
            lambda q: left_t[q],
        ), rounded)
        keep(d_left, nr, n, left_col(c0, None))

    def prepare_more(wide, m):
        z1, _ = norm(strips(in_mixed, wide))
        saved[7, :m] = strips(ct32, wide) * dot(z1, wo[1])

    each(prepare, my_col == 1)
    each(prepare_more)
    e_sig.wait_recv()
    turn_signal(o0)
    keep(d_left, 0, lc, left_row(o0, kept(d_left, 0, lc)), rounded)

    @pl.when(owner)
    def _():
        keep(d_left, nr, n, left_col(o0, kept(d_left, nr, n)), rounded)

    def back(wide, m):
        f = tuple(saved[q, :m] for q in range(7))
        g = rounded(strips(ct32, wide) + front_back(f, wf[1], d_left[:m], d_right[:m], saved[7, :m]))
        z0, r = norm(strips(mixed, wide))
        dz = rounded(dot_t(g * strips(gate, wide), wo[0]))
        s = rounded(norm_back(z0, r, dz))
        along_row = s[:nr].reshape(lr, lc, c)
        sig_row[:, pl.ds(c0, lc), :] = along_row
        saved[8, :nr] = g[:nr]
        if wide:
            sig_col[...] = s[nr:].reshape(lr, n, c)

    each(back)
    e_row = partner(6, sig_row.at[:, pl.ds(c0, lc)])
    e_row.start()
    e_col = partner(7, sig_col)

    @pl.when(owner)
    def _():
        e_col.start()

    x = x_h[pl.ds(r0, lr)].reshape(nr, c).astype(F32)
    f = factors(x, row_of(mask), wf[0])
    z0, _ = norm(row_of(mixed))
    g = saved[8, :nr]
    d_gate = g * dot(z0, wo[0])

    def out_left(j0, acc):
        return triangle(
            lr, lc, 0, lc,
            lambda a, q: sig_row[a, pl.ds(j0 + q, 1), :],
            lambda q: right[j0 + q, pl.ds(c0, lc), :],
            acc,
        )

    acc = out_left(c0, None)
    e_row.wait_recv()
    d_a = jnp.concatenate([rounded(v) for v in out_left(o0, acc)], axis=0)

    @pl.when(jnp.logical_not(owner))
    def _():
        e_col.wait_recv()

    d_b = jnp.concatenate([rounded(v) for v in triangle(
        lr, lc, 0, n,
        lambda a, q: sig_col[a, pl.ds(q, 1), :],
        lambda q: left[q, pl.ds(c0, lc), :],
    )], axis=0)
    out[...] = (g + front_back(f, wf[0], d_a, d_b, d_gate)).astype(BF16).reshape(lr, lc, c)

    higher(drain)
    e_ct.wait_send()
    for copy in e_left + [e_right, e_in_left, e_in_right, e_sig, e_row]:
        copy.wait_send()

    @pl.when(owner)
    def _():
        e_col.wait_send()


def from_root(array, axis, root):
    mine = lax.axis_index(axis) == root
    return lax.psum(jnp.where(mine, array, jnp.zeros_like(array)), axis)


def layer_norm(values):
    centred = values - jnp.mean(values, axis=-1, keepdims=True)
    spread = jnp.mean(centred * centred, axis=-1, keepdims=True)
    return centred * lax.rsqrt(spread + 1e-05)


def project_pair(inner_pair, mask_pair, weight):
    normed = layer_norm(inner_pair.astype(jnp.float32)).astype(jnp.bfloat16)
    linear = jnp.dot(normed, weight, preferred_element_type=jnp.float32)
    left_side = jax.nn.sigmoid(linear[..., :H]) * linear[..., H : 2 * H]
    right_side = jax.nn.sigmoid(linear[..., 2 * H : 3 * H]) * linear[..., 3 * H : 4 * H]
    operands = (jnp.stack((left_side, right_side)) * mask_pair[None, :, :, None]).astype(
        jnp.bfloat16
    )
    return (operands, jax.nn.sigmoid(linear[..., 4 * H :]))


def finish(mixed_part, gate_value, inner_pair, weight):
    normed = layer_norm(mixed_part).astype(jnp.bfloat16)
    update = jnp.dot(normed, weight, preferred_element_type=jnp.float32)
    return (inner_pair.astype(jnp.float32) + gate_value * update).astype(jnp.bfloat16)


def body(pair_act, cotangent, residue_mask, front_weight, out_weight):
    local_rows = pair_act.shape[0]
    local_cols = pair_act.shape[1]
    row_index = lax.axis_index("row")
    col_index = lax.axis_index("col")
    block_rows = lax.axis_size("row") // lax.axis_size("col")
    owner_col = row_index // block_rows
    offset = row_index % block_rows * local_rows
    chain_mask = residue_mask.astype(jnp.float32)
    mask_rows = lax.dynamic_slice_in_dim(chain_mask, row_index * local_rows, local_rows)
    mask_cols = lax.dynamic_slice_in_dim(chain_mask, col_index * local_cols, local_cols)
    mask_pair = mask_rows[:, None] * mask_cols[None, :]

    def gather_rows(stacked):
        return lax.all_gather(stacked, "row", axis=1, tiled=True)

    def column_block(gathered):
        slab = lax.dynamic_slice_in_dim(gathered, offset, local_rows, 1)
        return from_root(slab, "col", owner_col)

    def gather_cols(values):
        return lax.all_gather(values, "col", axis=1, tiled=True)

    def sum_cols(partial_term):
        return lax.psum_scatter(
            partial_term.astype(jnp.bfloat16), "col", scatter_dimension=1, tiled=True
        ).astype(jnp.float32)

    (out_ops, out_gate), out_front_back = jax.vjp(
        lambda inner_pair: project_pair(inner_pair, mask_pair, front_weight[0]), pair_act
    )
    fetched = gather_rows(out_ops)
    out_mixed = sum_cols(
        jnp.einsum("ikc,jkc->ijc", out_ops[0], fetched[-1], preferred_element_type=jnp.float32)
    )
    pair_mid, out_finish_back = jax.vjp(
        lambda mixed_part, gate_value, inner_pair: finish(
            mixed_part, gate_value, inner_pair, out_weight[0]
        ),
        out_mixed,
        out_gate,
        pair_act,
    )
    (in_ops, in_gate), in_front_back = jax.vjp(
        lambda inner_pair: project_pair(inner_pair, mask_pair, front_weight[1]), pair_mid
    )
    in_fetched = gather_rows(in_ops)
    left_block = column_block(in_fetched[0])
    in_mixed = jnp.einsum(
        "kic,kjc->ijc", left_block, in_fetched[1], preferred_element_type=jnp.float32
    )
    unused_pair, in_finish_back = jax.vjp(
        lambda mixed_part, gate_value, inner_pair: finish(
            mixed_part, gate_value, inner_pair, out_weight[1]
        ),
        in_mixed,
        in_gate,
        pair_mid,
    )
    grad_mixed, grad_gate, grad_inner = in_finish_back(cotangent)
    signal = grad_mixed.astype(jnp.bfloat16)
    signal_rows = gather_rows(signal[None])[0]
    left_rows = gather_cols(in_ops[0])
    grad_right = jnp.einsum(
        "kic,ijc->kjc", left_rows, signal_rows, preferred_element_type=jnp.float32
    )
    grad_left = sum_cols(
        jnp.einsum("kjc,ijc->kic", in_ops[1], signal_rows, preferred_element_type=jnp.float32)
    )
    (grad_front,) = in_front_back(
        (jnp.stack((grad_left, grad_right)).astype(jnp.bfloat16), grad_gate)
    )
    grad_mid = (grad_inner.astype(jnp.float32) + grad_front.astype(jnp.float32)).astype(
        jnp.bfloat16
    )
    grad_mixed, grad_gate, grad_inner = out_finish_back(grad_mid)
    signal = grad_mixed.astype(jnp.bfloat16)
    signal_cols = gather_cols(signal)
    grad_left = jnp.einsum(
        "ijc,jkc->ikc", signal_cols, fetched[-1], preferred_element_type=jnp.float32
    )
    signal_block = column_block(gather_rows(signal[None])[0])
    grad_right = jnp.einsum(
        "ijc,ikc->jkc", signal_block, fetched[0], preferred_element_type=jnp.float32
    )
    (grad_front,) = out_front_back(
        (jnp.stack((grad_left, grad_right)).astype(jnp.bfloat16), grad_gate)
    )
    return (grad_inner.astype(jnp.float32) + grad_front.astype(jnp.float32)).astype(jnp.bfloat16)


def crop_body(rows, pair_act, cotangent, residue_mask, front_weight, out_weight):
    lr, lc, c = pair_act.shape
    n = residue_mask.shape[0]
    strip = lr * lc + lr * n
    dma = pltpu.SemaphoreType.DMA
    operands = (pair_act, cotangent, residue_mask.reshape(1, n), front_weight, out_weight)
    return pl.pallas_call(
        functools.partial(crop_kernel, rows),
        out_shape=jax.ShapeDtypeStruct((lr, lc, c), BF16),
        in_specs=[pl.BlockSpec(memory_space=pl.ANY)] * 5,
        out_specs=pl.BlockSpec(memory_space=pltpu.VMEM),
        scratch_shapes=[
            pltpu.VMEM((n, lc, c), BF16),
            pltpu.VMEM((n, lc, c), BF16),
            pltpu.VMEM(front_weight.shape, BF16),
            pltpu.VMEM(out_weight.shape, BF16),
            pltpu.VMEM((1, n), jnp.int32),
        ]
        + [pltpu.VMEM((n, n, c), F32)] * 7
        + [pltpu.VMEM((lc, lc, c), F32)] * 2
        + [pltpu.VMEM((n * lc, c), F32)] * 7
        + [
            pltpu.VMEM((n * lc, c), BF16),
            pltpu.VMEM((n, c), F32),
            pltpu.VMEM((9, strip, c), F32),
            pltpu.VMEM((strip, c), F32),
            pltpu.VMEM((strip, c), F32),
            pltpu.VMEM((lr, n, c), F32),
            pltpu.VMEM((lr, n, c), F32),
        ]
        + [dma((5,)), dma((rows,)), dma((rows,)), dma((1,)), dma((1,)), dma((8,)), dma((8,))]
        + [pltpu.SemaphoreType.REGULAR((rows,))],
        compiler_params=pltpu.CompilerParams(
            collective_id=0, has_side_effects=True, vmem_limit_bytes=VMEM_BUDGET
        ),
    )(*[pltpu.with_memory_space_constraint(v, pltpu.HBM) for v in operands])


def fits(mesh, n, lr, lc, c):
    rows, cols = mesh.shape["row"], mesh.shape["col"]
    return (
        cols == 2
        and rows >= 2
        and rows & (rows - 1) == 0
        and n == 2 * lc
        and lc % (2 * TILE) == 0
        and lc % (2 * lr) == 0
        and FULL_ARRAYS * 4 * n * n * c <= VMEM_BUDGET
    )


def solution(mesh):
    def dispatch(pair_act, cotangent, residue_mask, front_weight, out_weight):
        n = residue_mask.shape[0]
        if fits(mesh, n, *pair_act.shape):
            return crop_body(
                mesh.shape["row"], pair_act, cotangent, residue_mask, front_weight, out_weight
            )
        return body(pair_act, cotangent, residue_mask, front_weight, out_weight)

    placed = (P(("grp", "row"), "col", None), P(("grp", "row"), "col", None), P("grp"), P(), P())
    return jax.shard_map(
        dispatch,
        mesh=mesh,
        in_specs=placed,
        out_specs=P(("grp", "row"), "col", None),
        check_vma=False,
    )
```

```python
import functools

import jax
import jax.numpy as jnp
from jax import lax
from jax.experimental import pallas as pl
from jax.experimental.pallas import tpu as pltpu
from jax.sharding import PartitionSpec as P

H = 128
TILE = 8
F32 = jnp.float32
BF16 = jnp.bfloat16
MESH = pl.DeviceIdType.MESH
VMEM_BUDGET = 24 << 20
FULL_ARRAYS = 16


def sigmoid(x):
    return 0.5 * jnp.tanh(0.5 * x) + 0.5


def norm(v):
    centred = v - jnp.mean(v, axis=-1, keepdims=True)
    r = lax.rsqrt(jnp.mean(centred * centred, axis=-1, keepdims=True) + 1e-05)
    return centred * r, r


def norm_back(y, r, d):
    return r * (d - jnp.mean(d, axis=-1, keepdims=True) - y * jnp.mean(d * y, axis=-1, keepdims=True))


def rounded(v):
    return v.astype(BF16).astype(F32)


def dot(a, b):
    return jnp.dot(a.astype(BF16), b, preferred_element_type=F32)


def dot_t(a, b):
    return lax.dot_general(
        a.astype(BF16), b, (((1,), (1,)), ((), ())), preferred_element_type=F32
    )


def part(p, n):
    return p[:, n * H : (n + 1) * H]


def factors(x, mask, weight):
    y, r = norm(x)
    p = dot(y, weight)
    s0, s2, s4 = sigmoid(part(p, 0)), sigmoid(part(p, 2)), sigmoid(part(p, 4))
    fa, fb = mask * s0, mask * s2
    return y, r, fa * part(p, 1) * (1.0 - s0), fa, fb * part(p, 3) * (1.0 - s2), fb, s4 * (1.0 - s4)


def front_back(f, weight, d_a, d_b, d_gate):
    y, r, f0, f1, f2, f3, f4 = f
    d = jnp.concatenate(
        [(v.astype(BF16)) for v in (d_a * f0, d_a * f1, d_b * f2, d_b * f3, d_gate * f4)], axis=1
    )
    return rounded(norm_back(y, r, rounded(dot_t(d, weight))))


def crop_kernel(
    rows, pair, cot, mask_in, wf_in, wo_in, out,
    x_h, ct_h, wf, wo, chain,
    left, right, in_left, in_right, sig, left_t, right_t, flip_r, flip_s,
    mask, mixed, gate, mid, in_mixed, in_gate, ct32, normed, along,
    saved, d_left, d_right, sig_row, sig_col,
    local_sem, x_send, x_recv, ct_send, ct_recv, psend, precv, ready,
):
    n, c = left.shape[0], left.shape[2]
    lr, lc = out.shape[0], out.shape[1]
    bits = rows.bit_length() - 1
    me, my_col = lax.axis_index("row"), lax.axis_index("col")
    other = 1 - my_col
    me_bits = [lax.rem(lax.div(me, 1 << b), 2) for b in range(bits)]

    def flip(d, low=0):
        total = 0
        for b in range(low, bits):
            bit = me_bits[b]
            total = total + (1 - bit if d >> b & 1 else bit) * (1 << b)
        return total

    barrier = pltpu.get_barrier_semaphore()
    pl.semaphore_signal(barrier, inc=1, device_id={"col": other}, device_id_type=MESH)
    for row in range(1, rows):
        @pl.when(me < row)
        def _():
            pl.semaphore_signal(barrier, inc=1, device_id={"row": row}, device_id_type=MESH)

    r0 = pl.multiple_of(me * lr, lr)
    c0 = pl.multiple_of(my_col * lc, lc)
    o0 = pl.multiple_of(other * lc, lc)
    jl = lax.rem(me * lr, lc)
    owner = lax.div(me * lr, lc) == my_col

    own = [
        pltpu.make_async_copy(src, dst.at[pl.ds(r0, lr)], local_sem.at[t])
        for t, (src, dst) in enumerate(((pair, x_h), (cot, ct_h)))
    ]
    weights = [
        pltpu.make_async_copy(wf_in, wf, local_sem.at[2]),
        pltpu.make_async_copy(wo_in, wo, local_sem.at[3]),
    ]
    chain_copy = pltpu.make_async_copy(mask_in, chain, local_sem.at[4])
    for copy in [chain_copy, own[0]] + weights + [own[1]]:
        copy.start()

    def direct(t, row, mine=None):
        src, dst = ((pair, x_h), (cot, ct_h))[t]
        source = row if mine is None else mine
        return pltpu.make_async_remote_copy(
            src_ref=src,
            dst_ref=dst.at[pl.ds(pl.multiple_of(source * lr, lr), lr)],
            send_sem=x_send.at[row] if t == 0 else ct_send.at[0],
            recv_sem=x_recv.at[source] if t == 0 else ct_recv.at[0],
            device_id={"row": row},
            device_id_type=MESH,
        )

    def lower(step):
        for row in range(rows - 1):
            @pl.when(row < me)
            def _():
                step(row)

    def higher(step):
        for row in range(1, rows):
            @pl.when(row > me)
            def _():
                step(row)

    def answer(row):
        if row < 2:
            direct(0, row, me).start()
        pl.semaphore_signal(ready.at[me], inc=1, device_id={"row": row}, device_id_type=MESH)

    def send(row):
        if row >= 2:
            direct(0, row, me).start()

    def follow(row):
        pl.semaphore_wait(ready.at[row], 1)
        direct(0, row, me).start()

    def drain(row):
        direct(0, row, me).wait_send()

    def second(row):
        direct(1, row, me).start()

    def partner(q, r, ref):
        return pltpu.make_async_remote_copy(
            src_ref=ref,
            dst_ref=ref,
            send_sem=psend.at[q],
            recv_sem=precv.at[r],
            device_id={"col": other},
            device_id_type=MESH,
        )

    pl.semaphore_wait(barrier, me + 1)
    lower(answer)

    chain_copy.wait()
    span = jnp.broadcast_to(chain[...].astype(F32), (n, n))
    here = lax.broadcasted_iota(jnp.int32, (n, n), 0) == lax.broadcasted_iota(jnp.int32, (n, n), 1)
    along[...] = jnp.broadcast_to(
        jnp.sum(jnp.where(here, span, 0.0), axis=1, keepdims=True), (n, c)
    )
    across = along[pl.ds(c0, lc), :]
    for i in range(n):
        mask[i * lc : (i + 1) * lc] = across * along[i : i + 1]
    lower(send)

    def block(ref, k0, nk):
        return ref[pl.ds(pl.multiple_of(k0 * lc, lc), nk * lc), :]

    def put(ref, k0, nk, v):
        ref[pl.ds(pl.multiple_of(k0 * lc, lc), nk * lc), :] = v

    def put_half(ref, k0, nk, v):
        ref[pl.ds(k0, nk), pl.ds(c0, lc), :] = v.reshape(nk, lc, c)

    def half(ref, k0, nk):
        return ref.at[pl.ds(k0, nk), pl.ds(c0, lc)]

    def projected(x, segments, weight, a_ref, b_ref, g_ref):
        y, _ = norm(x)
        p = dot(y, weight)
        m = jnp.concatenate([block(mask, k0, nk) for k0, nk in segments], axis=0)
        a = rounded(sigmoid(part(p, 0)) * part(p, 1) * m)
        b = rounded(sigmoid(part(p, 2)) * part(p, 3) * m)
        g = sigmoid(part(p, 4))
        at = 0
        for k0, nk in segments:
            span = slice(at * lc, (at + nk) * lc)
            put_half(a_ref, k0, nk, a[span])
            put_half(b_ref, k0, nk, b[span])
            put(g_ref, k0, nk, g[span])
            at += nk

    def triangle(count, width, first, depth, row_at, tile_at, acc=None):
        def term(q, acc):
            t = tile_at(first + q)
            return tuple(v + row_at(a, first + q) * t for a, v in enumerate(acc))

        if acc is None:
            acc = (jnp.zeros((width, c), F32),) * count
        return lax.fori_loop(0, depth, term, tuple(acc), unroll=True)

    def loop(count, step):
        def body(k, carry):
            step(k)
            return carry

        lax.fori_loop(0, count, body, 0)

    for copy in weights:
        copy.wait()
    groups = [[(0, 1)], [(1, 1), (2, 2)] if rows > 2 else [(1, 1)]]
    groups += [[(d, 2)] for d in range(4, rows, 2)]
    for g, group in enumerate(groups):
        for d, count in group:
            for q in range(d, d + count):
                if q == 0:
                    own[0].wait()
                else:
                    direct(0, flip(q)).wait_recv()
        segments = [
            (pl.multiple_of(flip(d, count.bit_length() - 1) * lr, count * lr), count * lr)
            for d, count in group
        ]
        x = jnp.concatenate(
            [x_h[pl.ds(k0, nk)].reshape(nk * lc, c).astype(F32) for k0, nk in segments], axis=0
        )
        projected(x, segments, wf[0], left, right, gate)
        for k0, nk in segments:
            partner(0, 0, half(left, k0, nk)).start()
            partner(0, 0, half(right, k0, nk)).start()
        if g == 0:
            higher(follow)
            lower(drain)
            pl.semaphore_signal(
                ready.at[rows], inc=1, device_id={"col": other}, device_id_type=MESH
            )
            pl.semaphore_wait(ready.at[rows], 1)
            lower(second)
        if g == len(groups) - 1:
            higher(second)

    group = TILE

    def outgoing(k0, fresh):
        for b in range(lc // TILE):
            t = jnp.swapaxes(right[pl.ds(c0 + b * TILE, TILE), pl.ds(k0, lc), :], 0, 1)
            flip_r[:, b * TILE : (b + 1) * TILE, :] = t

        def step(b):
            i0 = b * group
            base = pl.multiple_of(i0 * lc, lc * group)
            acc = None
            if not fresh:
                acc = [mixed[pl.ds(base + a * lc, lc), :] for a in range(group)]
            acc = triangle(
                group, lc, 0, lc,
                lambda a, q: left[i0 + a, pl.ds(k0 + q, 1), :],
                lambda q: flip_r[q],
                acc,
            )
            for a in range(group):
                mixed[pl.ds(base + a * lc, lc), :] = acc[a]

        loop(n // group, step)

    outgoing(c0, True)
    e_out = partner(0, 0, left)
    e_out.wait_recv()
    outgoing(o0, False)

    z, _ = norm(mixed[...])
    x = x_h[...].reshape(n * lc, c).astype(F32)
    x = rounded(x + gate[...] * dot(z, wo[0]))
    mid[...] = x
    y = norm(x)[0].astype(BF16)
    normed[...] = y
    p = dot(y, wf[1, :, : 2 * H])
    put_half(in_left, 0, n, rounded(sigmoid(part(p, 0)) * part(p, 1) * mask[...]))
    e_in_left = [
        partner(1, 1 + b, in_left.at[:, pl.ds(c0 + b * TILE, TILE)]) for b in range(lc // TILE)
    ]
    for copy in e_in_left:
        copy.start()
    p = dot(normed[...], wf[1, :, 2 * H :])
    put_half(in_right, 0, n, rounded(sigmoid(part(p, 0)) * part(p, 1) * mask[...]))
    in_gate[...] = sigmoid(part(p, 2))
    e_in_right = partner(1, 3, half(in_right, 0, n))
    e_in_right.start()

    def incoming(i0, copies=()):
        few = 4

        def step(i1):
            acc = triangle(
                few, lc, 0, n,
                lambda a, q: in_left[q, pl.ds(i1 + a, 1), :],
                lambda q: in_right[q, pl.ds(c0, lc), :],
            )
            for a in range(few):
                in_mixed[pl.ds(pl.multiple_of((i1 + a) * lc, lc), lc), :] = acc[a]

        for b in range(lc // TILE):
            if copies:
                copies[b].wait_recv()
            for a in range(0, TILE, few):
                step(pl.multiple_of(i0 + b * TILE, TILE) + a)

    nr, nc = lr * lc, lr * n

    def row_of(ref):
        return ref[pl.ds(pl.multiple_of(r0 * lc, lc), nr), :]

    def col_of(ref):
        return jnp.concatenate([ref[pl.ds(jl + a, n, stride=lc), :] for a in range(lr)], axis=0)

    def strips(ref, wide):
        return jnp.concatenate([row_of(ref), col_of(ref)], axis=0) if wide else row_of(ref)

    def each(step, here=True):
        @pl.when(jnp.logical_and(here, owner))
        def _():
            step(True, nr + nc)

        @pl.when(jnp.logical_and(here, jnp.logical_not(owner)))
        def _():
            step(False, nr)

    def transposed(src, dst, j0):
        for b in range(n // TILE):
            t = jnp.swapaxes(src[b * TILE : (b + 1) * TILE, pl.ds(j0, lc), :], 0, 1)
            dst[pl.ds(j0, lc), b * TILE : (b + 1) * TILE, :] = t

    incoming(c0)

    def prepare(wide, m):
        f = factors(strips(mid, wide), strips(mask, wide), wf[1])
        for q, v in enumerate(f):
            saved[q, :m] = jnp.broadcast_to(v, (m, c))

    each(prepare, my_col == 0)

    @pl.when(jnp.logical_and(my_col == 0, owner))
    def _():
        transposed(in_left, left_t, c0)
        transposed(in_right, right_t, c0)

    incoming(o0, e_in_left)

    others = pl.ds(0, (rows - 1) * lr)
    e_ct = pltpu.make_async_remote_copy(
        src_ref=ct_h.at[others],
        dst_ref=ct_h.at[others],
        send_sem=ct_send.at[0],
        recv_sem=ct_recv.at[0],
        device_id={"col": other},
        device_id_type=MESH,
    )
    e_ct.wait_recv()
    own[1].wait()

    def signal(i0):
        z, r = norm(block(in_mixed, i0, lc))
        ct = ct_h[pl.ds(i0, lc)].reshape(lc * lc, c).astype(F32)
        put(ct32, i0, lc, ct)
        dz = rounded(dot_t(ct * block(in_gate, i0, lc), wo[1]))
        put_half(sig, i0, lc, rounded(norm_back(z, r, dz)))

    signal(o0)
    e_sig = partner(2, 4, half(sig, o0, lc))
    e_sig.start()
    signal(c0)
    e_in_right.wait_recv()

    def turn_signal(j0):
        for b in range(lc // TILE):
            t = jnp.swapaxes(sig[pl.ds(c0 + b * TILE, TILE), pl.ds(j0, lc), :], 0, 1)
            flip_s[:, b * TILE : (b + 1) * TILE, :] = t

    def left_row(j0, acc):
        return triangle(
            lr, lc, 0, lc,
            lambda a, q: in_right[r0 + a, pl.ds(j0 + q, 1), :],
            lambda q: flip_s[q],
            acc,
        )

    def left_col(j0, acc):
        return triangle(
            lr, n, 0, lc,
            lambda a, q: sig[r0 + a, pl.ds(j0 + q, 1), :],
            lambda q: right_t[j0 + q],
            acc,
        )

    def keep(ref, start, width, acc, fix=lambda v: v):
        for a in range(lr):
            ref[start + a * width : start + (a + 1) * width] = fix(acc[a])

    def kept(ref, start, width):
        return [ref[start + a * width : start + (a + 1) * width] for a in range(lr)]

    turn_signal(c0)
    keep(d_right, 0, lc, triangle(
        lr, lc, 0, n,
        lambda a, q: in_left[r0 + a, pl.ds(q, 1), :],
        lambda q: sig[q, pl.ds(c0, lc), :],
    ), rounded)
    keep(d_left, 0, lc, left_row(c0, None))

    @pl.when(owner)
    def _():
        @pl.when(my_col != 0)
        def _():
            transposed(in_left, left_t, c0)
            transposed(in_right, right_t, c0)

        transposed(in_left, left_t, o0)
        transposed(in_right, right_t, o0)
        keep(d_right, nr, n, triangle(
            lr, n, 0, n,
            lambda a, q: sig[q, pl.ds(r0 + a, 1), :],
            lambda q: left_t[q],
        ), rounded)
        keep(d_left, nr, n, left_col(c0, None))

    def prepare_more(wide, m):
        z1, _ = norm(strips(in_mixed, wide))
        saved[7, :m] = strips(ct32, wide) * dot(z1, wo[1])

    each(prepare, my_col == 1)
    each(prepare_more)
    e_sig.wait_recv()
    turn_signal(o0)
    keep(d_left, 0, lc, left_row(o0, kept(d_left, 0, lc)), rounded)

    @pl.when(owner)
    def _():
        keep(d_left, nr, n, left_col(o0, kept(d_left, nr, n)), rounded)

    def back(wide, m):
        f = tuple(saved[q, :m] for q in range(7))
        g = rounded(strips(ct32, wide) + front_back(f, wf[1], d_left[:m], d_right[:m], saved[7, :m]))
        z0, r = norm(strips(mixed, wide))
        dz = rounded(dot_t(g * strips(gate, wide), wo[0]))
        s = rounded(norm_back(z0, r, dz))
        along_row = s[:nr].reshape(lr, lc, c)
        sig_row[:, pl.ds(c0, lc), :] = along_row
        saved[8, :nr] = g[:nr]
        if wide:
            sig_col[...] = s[nr:].reshape(lr, n, c)

    each(back)
    e_row = partner(3, 5, sig_row.at[:, pl.ds(c0, lc)])
    e_row.start()
    e_col = partner(4, 6, sig_col)

    @pl.when(owner)
    def _():
        e_col.start()

    x = x_h[pl.ds(r0, lr)].reshape(nr, c).astype(F32)
    f = factors(x, row_of(mask), wf[0])
    z0, _ = norm(row_of(mixed))
    g = saved[8, :nr]
    d_gate = g * dot(z0, wo[0])

    def out_left(j0, acc):
        return triangle(
            lr, lc, 0, lc,
            lambda a, q: sig_row[a, pl.ds(j0 + q, 1), :],
            lambda q: right[j0 + q, pl.ds(c0, lc), :],
            acc,
        )

    acc = out_left(c0, None)
    e_row.wait_recv()
    d_a = jnp.concatenate([rounded(v) for v in out_left(o0, acc)], axis=0)

    @pl.when(jnp.logical_not(owner))
    def _():
        e_col.wait_recv()

    d_b = jnp.concatenate([rounded(v) for v in triangle(
        lr, lc, 0, n,
        lambda a, q: sig_col[a, pl.ds(q, 1), :],
        lambda q: left[q, pl.ds(c0, lc), :],
    )], axis=0)
    out[...] = (g + front_back(f, wf[0], d_a, d_b, d_gate)).astype(BF16).reshape(lr, lc, c)

    higher(drain)
    e_ct.wait_send()
    for copy in (e_out, partner(1, 3, in_left), e_sig, e_row):
        copy.wait_send()

    @pl.when(owner)
    def _():
        e_col.wait_send()


def from_root(array, axis, root):
    mine = lax.axis_index(axis) == root
    return lax.psum(jnp.where(mine, array, jnp.zeros_like(array)), axis)


def layer_norm(values):
    centred = values - jnp.mean(values, axis=-1, keepdims=True)
    spread = jnp.mean(centred * centred, axis=-1, keepdims=True)
    return centred * lax.rsqrt(spread + 1e-05)


def project_pair(inner_pair, mask_pair, weight):
    normed = layer_norm(inner_pair.astype(jnp.float32)).astype(jnp.bfloat16)
    linear = jnp.dot(normed, weight, preferred_element_type=jnp.float32)
    left_side = jax.nn.sigmoid(linear[..., :H]) * linear[..., H : 2 * H]
    right_side = jax.nn.sigmoid(linear[..., 2 * H : 3 * H]) * linear[..., 3 * H : 4 * H]
    operands = (jnp.stack((left_side, right_side)) * mask_pair[None, :, :, None]).astype(
        jnp.bfloat16
    )
    return (operands, jax.nn.sigmoid(linear[..., 4 * H :]))


def finish(mixed_part, gate_value, inner_pair, weight):
    normed = layer_norm(mixed_part).astype(jnp.bfloat16)
    update = jnp.dot(normed, weight, preferred_element_type=jnp.float32)
    return (inner_pair.astype(jnp.float32) + gate_value * update).astype(jnp.bfloat16)


def body(pair_act, cotangent, residue_mask, front_weight, out_weight):
    local_rows = pair_act.shape[0]
    local_cols = pair_act.shape[1]
    row_index = lax.axis_index("row")
    col_index = lax.axis_index("col")
    block_rows = lax.axis_size("row") // lax.axis_size("col")
    owner_col = row_index // block_rows
    offset = row_index % block_rows * local_rows
    chain_mask = residue_mask.astype(jnp.float32)
    mask_rows = lax.dynamic_slice_in_dim(chain_mask, row_index * local_rows, local_rows)
    mask_cols = lax.dynamic_slice_in_dim(chain_mask, col_index * local_cols, local_cols)
    mask_pair = mask_rows[:, None] * mask_cols[None, :]

    def gather_rows(stacked):
        return lax.all_gather(stacked, "row", axis=1, tiled=True)

    def column_block(gathered):
        slab = lax.dynamic_slice_in_dim(gathered, offset, local_rows, 1)
        return from_root(slab, "col", owner_col)

    def gather_cols(values):
        return lax.all_gather(values, "col", axis=1, tiled=True)

    def sum_cols(partial_term):
        return lax.psum_scatter(
            partial_term.astype(jnp.bfloat16), "col", scatter_dimension=1, tiled=True
        ).astype(jnp.float32)

    (out_ops, out_gate), out_front_back = jax.vjp(
        lambda inner_pair: project_pair(inner_pair, mask_pair, front_weight[0]), pair_act
    )
    fetched = gather_rows(out_ops)
    out_mixed = sum_cols(
        jnp.einsum("ikc,jkc->ijc", out_ops[0], fetched[-1], preferred_element_type=jnp.float32)
    )
    pair_mid, out_finish_back = jax.vjp(
        lambda mixed_part, gate_value, inner_pair: finish(
            mixed_part, gate_value, inner_pair, out_weight[0]
        ),
        out_mixed,
        out_gate,
        pair_act,
    )
    (in_ops, in_gate), in_front_back = jax.vjp(
        lambda inner_pair: project_pair(inner_pair, mask_pair, front_weight[1]), pair_mid
    )
    in_fetched = gather_rows(in_ops)
    left_block = column_block(in_fetched[0])
    in_mixed = jnp.einsum(
        "kic,kjc->ijc", left_block, in_fetched[1], preferred_element_type=jnp.float32
    )
    unused_pair, in_finish_back = jax.vjp(
        lambda mixed_part, gate_value, inner_pair: finish(
            mixed_part, gate_value, inner_pair, out_weight[1]
        ),
        in_mixed,
        in_gate,
        pair_mid,
    )
    grad_mixed, grad_gate, grad_inner = in_finish_back(cotangent)
    signal = grad_mixed.astype(jnp.bfloat16)
    signal_rows = gather_rows(signal[None])[0]
    left_rows = gather_cols(in_ops[0])
    grad_right = jnp.einsum(
        "kic,ijc->kjc", left_rows, signal_rows, preferred_element_type=jnp.float32
    )
    grad_left = sum_cols(
        jnp.einsum("kjc,ijc->kic", in_ops[1], signal_rows, preferred_element_type=jnp.float32)
    )
    (grad_front,) = in_front_back(
        (jnp.stack((grad_left, grad_right)).astype(jnp.bfloat16), grad_gate)
    )
    grad_mid = (grad_inner.astype(jnp.float32) + grad_front.astype(jnp.float32)).astype(
        jnp.bfloat16
    )
    grad_mixed, grad_gate, grad_inner = out_finish_back(grad_mid)
    signal = grad_mixed.astype(jnp.bfloat16)
    signal_cols = gather_cols(signal)
    grad_left = jnp.einsum(
        "ijc,jkc->ikc", signal_cols, fetched[-1], preferred_element_type=jnp.float32
    )
    signal_block = column_block(gather_rows(signal[None])[0])
    grad_right = jnp.einsum(
        "ijc,ikc->jkc", signal_block, fetched[0], preferred_element_type=jnp.float32
    )
    (grad_front,) = out_front_back(
        (jnp.stack((grad_left, grad_right)).astype(jnp.bfloat16), grad_gate)
    )
    return (grad_inner.astype(jnp.float32) + grad_front.astype(jnp.float32)).astype(jnp.bfloat16)


def crop_body(rows, pair_act, cotangent, residue_mask, front_weight, out_weight):
    lr, lc, c = pair_act.shape
    n = residue_mask.shape[0]
    strip = lr * lc + lr * n
    dma = pltpu.SemaphoreType.DMA
    operands = (pair_act, cotangent, residue_mask.reshape(1, n), front_weight, out_weight)
    return pl.pallas_call(
        functools.partial(crop_kernel, rows),
        out_shape=jax.ShapeDtypeStruct((lr, lc, c), BF16),
        in_specs=[pl.BlockSpec(memory_space=pl.ANY)] * 5,
        out_specs=pl.BlockSpec(memory_space=pltpu.VMEM),
        scratch_shapes=[
            pltpu.VMEM((n, lc, c), BF16),
            pltpu.VMEM((n, lc, c), BF16),
            pltpu.VMEM(front_weight.shape, BF16),
            pltpu.VMEM(out_weight.shape, BF16),
            pltpu.VMEM((1, n), jnp.int32),
        ]
        + [pltpu.VMEM((n, n, c), F32)] * 7
        + [pltpu.VMEM((lc, lc, c), F32)] * 2
        + [pltpu.VMEM((n * lc, c), F32)] * 7
        + [
            pltpu.VMEM((n * lc, c), BF16),
            pltpu.VMEM((n, c), F32),
            pltpu.VMEM((9, strip, c), F32),
            pltpu.VMEM((strip, c), F32),
            pltpu.VMEM((strip, c), F32),
            pltpu.VMEM((lr, n, c), F32),
            pltpu.VMEM((lr, n, c), F32),
        ]
        + [dma((5,)), dma((rows,)), dma((rows,)), dma((1,)), dma((1,)), dma((5,)), dma((7,))]
        + [pltpu.SemaphoreType.REGULAR((rows + 1,))],
        compiler_params=pltpu.CompilerParams(
            collective_id=0, has_side_effects=True, vmem_limit_bytes=VMEM_BUDGET
        ),
    )(*[pltpu.with_memory_space_constraint(v, pltpu.HBM) for v in operands])


def fits(mesh, n, lr, lc, c):
    rows, cols = mesh.shape["row"], mesh.shape["col"]
    return (
        cols == 2
        and rows >= 2
        and rows & (rows - 1) == 0
        and n == 2 * lc
        and lc == 2 * TILE
        and lc % (2 * lr) == 0
        and FULL_ARRAYS * 4 * n * n * c <= VMEM_BUDGET
    )


def solution(mesh):
    def dispatch(pair_act, cotangent, residue_mask, front_weight, out_weight):
        n = residue_mask.shape[0]
        if fits(mesh, n, *pair_act.shape):
            return crop_body(
                mesh.shape["row"], pair_act, cotangent, residue_mask, front_weight, out_weight
            )
        return body(pair_act, cotangent, residue_mask, front_weight, out_weight)

    placed = (P(("grp", "row"), "col", None), P(("grp", "row"), "col", None), P("grp"), P(), P())
    return jax.shard_map(
        dispatch,
        mesh=mesh,
        in_specs=placed,
        out_specs=P(("grp", "row"), "col", None),
        check_vma=False,
    )
```

```python
import functools

import jax
import jax.numpy as jnp
from jax import lax
from jax.experimental import pallas as pl
from jax.experimental.pallas import tpu as pltpu
from jax.sharding import PartitionSpec as P

H = 128
TILE = 8
F32 = jnp.float32
BF16 = jnp.bfloat16
MESH = pl.DeviceIdType.MESH
VMEM_BUDGET = 24 << 20
FULL_ARRAYS = 16


def sigmoid(x):
    return 0.5 * jnp.tanh(0.5 * x) + 0.5


def norm(v):
    centred = v - jnp.mean(v, axis=-1, keepdims=True)
    r = lax.rsqrt(jnp.mean(centred * centred, axis=-1, keepdims=True) + 1e-05)
    return centred * r, r


def scales(v):
    mean = jnp.mean(v, axis=-1, keepdims=True)
    centred = v - mean
    r = lax.rsqrt(jnp.mean(centred * centred, axis=-1, keepdims=True) + 1e-05)
    return r, r * mean


def column_sums(w):
    return jnp.sum(w.astype(F32), axis=0, keepdims=True)


def norm_back(y, r, d):
    return r * (d - jnp.mean(d, axis=-1, keepdims=True) - y * jnp.mean(d * y, axis=-1, keepdims=True))


def rounded(v):
    return v.astype(BF16).astype(F32)


def dot(a, b):
    return jnp.dot(a.astype(BF16), b, preferred_element_type=F32)


def dot_t(a, b):
    return lax.dot_general(
        a.astype(BF16), b, (((1,), (1,)), ((), ())), preferred_element_type=F32
    )


def part(p, n):
    return p[:, n * H : (n + 1) * H]


def factors(x, mask, weight):
    y, r = norm(x)
    p = dot(y, weight)
    s0, s2, s4 = sigmoid(part(p, 0)), sigmoid(part(p, 2)), sigmoid(part(p, 4))
    fa, fb = mask * s0, mask * s2
    return y, r, fa * part(p, 1) * (1.0 - s0), fa, fb * part(p, 3) * (1.0 - s2), fb, s4 * (1.0 - s4)


def front_back(f, weight, d_a, d_b, d_gate):
    y, r, f0, f1, f2, f3, f4 = f
    d = jnp.concatenate(
        [(v.astype(BF16)) for v in (d_a * f0, d_a * f1, d_b * f2, d_b * f3, d_gate * f4)], axis=1
    )
    return rounded(norm_back(y, r, rounded(dot_t(d, weight))))


def crop_kernel(
    rows, pair, cot, mask_in, wf_in, wo_in, out,
    x_h, ct_h, wf, wo, chain,
    left, right, in_left, in_right, sig, left_t, right_t, flip_r, flip_s,
    mask, mixed, gate, mid, in_mixed, in_gate, ct32, normed, along,
    saved, d_left, d_right, sig_row, sig_col,
    local_sem, x_send, x_recv, ct_send, ct_recv, psend, precv, ready,
):
    n, c = left.shape[0], left.shape[2]
    lr, lc = out.shape[0], out.shape[1]
    bits = rows.bit_length() - 1
    me, my_col = lax.axis_index("row"), lax.axis_index("col")
    other = 1 - my_col
    me_bits = [lax.rem(lax.div(me, 1 << b), 2) for b in range(bits)]

    def flip(d, low=0):
        total = 0
        for b in range(low, bits):
            bit = me_bits[b]
            total = total + (1 - bit if d >> b & 1 else bit) * (1 << b)
        return total

    barrier = pltpu.get_barrier_semaphore()
    pl.semaphore_signal(barrier, inc=1, device_id={"col": other}, device_id_type=MESH)
    for row in range(1, rows):
        @pl.when(me < row)
        def _():
            pl.semaphore_signal(barrier, inc=1, device_id={"row": row}, device_id_type=MESH)

    r0 = pl.multiple_of(me * lr, lr)
    c0 = pl.multiple_of(my_col * lc, lc)
    o0 = pl.multiple_of(other * lc, lc)
    jl = lax.rem(me * lr, lc)
    owner = lax.div(me * lr, lc) == my_col

    own = [
        pltpu.make_async_copy(src, dst.at[pl.ds(r0, lr)], local_sem.at[t])
        for t, (src, dst) in enumerate(((pair, x_h), (cot, ct_h)))
    ]
    weights = [
        pltpu.make_async_copy(wf_in, wf, local_sem.at[2]),
        pltpu.make_async_copy(wo_in, wo, local_sem.at[3]),
    ]
    chain_copy = pltpu.make_async_copy(mask_in, chain, local_sem.at[4])
    for copy in [chain_copy, own[0]] + weights + [own[1]]:
        copy.start()

    def direct(t, row, mine=None):
        src, dst = ((pair, x_h), (cot, ct_h))[t]
        source = row if mine is None else mine
        return pltpu.make_async_remote_copy(
            src_ref=src,
            dst_ref=dst.at[pl.ds(pl.multiple_of(source * lr, lr), lr)],
            send_sem=x_send.at[row] if t == 0 else ct_send.at[0],
            recv_sem=x_recv.at[source] if t == 0 else ct_recv.at[0],
            device_id={"row": row},
            device_id_type=MESH,
        )

    def lower(step):
        for row in range(rows - 1):
            @pl.when(row < me)
            def _():
                step(row)

    def higher(step):
        for row in range(1, rows):
            @pl.when(row > me)
            def _():
                step(row)

    def answer(row):
        if row < 2:
            direct(0, row, me).start()
        pl.semaphore_signal(ready.at[me], inc=1, device_id={"row": row}, device_id_type=MESH)

    def send(row):
        if row >= 2:
            direct(0, row, me).start()

    def follow(row):
        pl.semaphore_wait(ready.at[row], 1)
        direct(0, row, me).start()

    def drain(row):
        direct(0, row, me).wait_send()

    def second(row):
        direct(1, row, me).start()

    def partner(q, r, ref):
        return pltpu.make_async_remote_copy(
            src_ref=ref,
            dst_ref=ref,
            send_sem=psend.at[q],
            recv_sem=precv.at[r],
            device_id={"col": other},
            device_id_type=MESH,
        )

    pl.semaphore_wait(barrier, me + 1)
    lower(answer)

    chain_copy.wait()
    span = jnp.broadcast_to(chain[...].astype(F32), (n, n))
    here = lax.broadcasted_iota(jnp.int32, (n, n), 0) == lax.broadcasted_iota(jnp.int32, (n, n), 1)
    along[...] = jnp.broadcast_to(
        jnp.sum(jnp.where(here, span, 0.0), axis=1, keepdims=True), (n, c)
    )
    across = along[pl.ds(c0, lc), :]
    for i in range(n):
        mask[i * lc : (i + 1) * lc] = across * along[i : i + 1]
    lower(send)

    def block(ref, k0, nk):
        return ref[pl.ds(pl.multiple_of(k0 * lc, lc), nk * lc), :]

    def put(ref, k0, nk, v):
        ref[pl.ds(pl.multiple_of(k0 * lc, lc), nk * lc), :] = v

    def put_half(ref, k0, nk, v):
        ref[pl.ds(k0, nk), pl.ds(c0, lc), :] = v.reshape(nk, lc, c)

    def half(ref, k0, nk):
        return ref.at[pl.ds(k0, nk), pl.ds(c0, lc)]

    def projected(x, segments, weight, sums, a_ref, b_ref, g_ref):
        r, rm = scales(x.astype(F32))
        p = dot(x, weight)

        def part(p, q):
            return p[:, q * H : (q + 1) * H] * r - rm * sums[:, q * H : (q + 1) * H]

        m = jnp.concatenate([block(mask, k0, nk) for k0, nk in segments], axis=0)
        a = rounded(sigmoid(part(p, 0)) * part(p, 1) * m)
        b = rounded(sigmoid(part(p, 2)) * part(p, 3) * m)
        g = sigmoid(part(p, 4))
        at = 0
        for k0, nk in segments:
            span = slice(at * lc, (at + nk) * lc)
            put_half(a_ref, k0, nk, a[span])
            put_half(b_ref, k0, nk, b[span])
            put(g_ref, k0, nk, g[span])
            at += nk

    def triangle(count, width, first, depth, row_at, tile_at, acc=None):
        def term(q, acc):
            t = tile_at(first + q)
            return tuple(v + row_at(a, first + q) * t for a, v in enumerate(acc))

        if acc is None:
            acc = (jnp.zeros((width, c), F32),) * count
        return lax.fori_loop(0, depth, term, tuple(acc), unroll=True)

    def loop(count, step):
        def body(k, carry):
            step(k)
            return carry

        lax.fori_loop(0, count, body, 0)

    for copy in weights:
        copy.wait()
    sums_out, sums_in, sums_mix = (column_sums(w) for w in (wf[0], wf[1], wo[0]))
    groups = [[(0, 1)], [(1, 1), (2, 2)] if rows > 2 else [(1, 1)]]
    groups += [[(d, 2)] for d in range(4, rows, 2)]
    for g, group in enumerate(groups):
        for d, count in group:
            for q in range(d, d + count):
                if q == 0:
                    own[0].wait()
                else:
                    direct(0, flip(q)).wait_recv()
        segments = [
            (pl.multiple_of(flip(d, count.bit_length() - 1) * lr, count * lr), count * lr)
            for d, count in group
        ]
        x = jnp.concatenate(
            [x_h[pl.ds(k0, nk)].reshape(nk * lc, c) for k0, nk in segments], axis=0
        )
        projected(x, segments, wf[0], sums_out, left, right, gate)
        for k0, nk in segments:
            partner(0, 0, half(left, k0, nk)).start()
            partner(0, 0, half(right, k0, nk)).start()
        if g == 0:
            higher(follow)
            lower(drain)
            pl.semaphore_signal(
                ready.at[rows], inc=1, device_id={"col": other}, device_id_type=MESH
            )
            pl.semaphore_wait(ready.at[rows], 1)
            lower(second)
        if g == len(groups) - 1:
            higher(second)

    group = TILE

    def outgoing(k0, fresh):
        for b in range(lc // TILE):
            t = jnp.swapaxes(right[pl.ds(c0 + b * TILE, TILE), pl.ds(k0, lc), :], 0, 1)
            flip_r[:, b * TILE : (b + 1) * TILE, :] = t

        def step(b):
            i0 = b * group
            base = pl.multiple_of(i0 * lc, lc * group)
            acc = None
            if not fresh:
                acc = [mixed[pl.ds(base + a * lc, lc), :] for a in range(group)]
            acc = triangle(
                group, lc, 0, lc,
                lambda a, q: left[i0 + a, pl.ds(k0 + q, 1), :],
                lambda q: flip_r[q],
                acc,
            )
            for a in range(group):
                mixed[pl.ds(base + a * lc, lc), :] = acc[a]

        loop(n // group, step)

    outgoing(c0, True)
    e_out = partner(0, 0, left)
    e_out.wait_recv()
    outgoing(o0, False)

    v = mixed[...]
    r, rm = scales(v)
    high = v.astype(BF16)
    low = (v - high.astype(F32)).astype(BF16)
    update = dot(
        jnp.concatenate([high, low], axis=1), jnp.concatenate([wo[0], wo[0]], axis=0)
    )
    x = x_h[...].reshape(n * lc, c).astype(F32)
    x = rounded(x + gate[...] * (update * r - rm * sums_mix))
    mid[...] = x
    r, rm = scales(x)

    def scaled(p, q, at):
        return part(p, q) * r - rm * part(sums_in, at + q)

    x = x.astype(BF16)
    normed[...] = x
    p = dot(x, wf[1, :, : 2 * H])
    put_half(in_left, 0, n, rounded(sigmoid(scaled(p, 0, 0)) * scaled(p, 1, 0) * mask[...]))
    e_in_left = [
        partner(1, 1 + b, in_left.at[:, pl.ds(c0 + b * TILE, TILE)]) for b in range(lc // TILE)
    ]
    for copy in e_in_left:
        copy.start()
    p = dot(normed[...], wf[1, :, 2 * H :])
    v = rounded(sigmoid(scaled(p, 0, 2)) * scaled(p, 1, 2) * mask[...])
    put_half(in_right, 0, n, v)
    in_gate[...] = sigmoid(scaled(p, 2, 2))
    e_in_right = partner(1, 3, half(in_right, 0, n))
    e_in_right.start()

    def incoming(i0, copies=()):
        few = 4

        def step(i1):
            acc = triangle(
                few, lc, 0, n,
                lambda a, q: in_left[q, pl.ds(i1 + a, 1), :],
                lambda q: in_right[q, pl.ds(c0, lc), :],
            )
            for a in range(few):
                in_mixed[pl.ds(pl.multiple_of((i1 + a) * lc, lc), lc), :] = acc[a]

        for b in range(lc // TILE):
            if copies:
                copies[b].wait_recv()
            for a in range(0, TILE, few):
                step(pl.multiple_of(i0 + b * TILE, TILE) + a)

    nr, nc = lr * lc, lr * n

    def row_of(ref):
        return ref[pl.ds(pl.multiple_of(r0 * lc, lc), nr), :]

    def col_of(ref):
        return jnp.concatenate([ref[pl.ds(jl + a, n, stride=lc), :] for a in range(lr)], axis=0)

    def strips(ref, wide):
        return jnp.concatenate([row_of(ref), col_of(ref)], axis=0) if wide else row_of(ref)

    def each(step, here=True):
        @pl.when(jnp.logical_and(here, owner))
        def _():
            step(True, nr + nc)

        @pl.when(jnp.logical_and(here, jnp.logical_not(owner)))
        def _():
            step(False, nr)

    def transposed(src, dst, j0):
        for b in range(n // TILE):
            t = jnp.swapaxes(src[b * TILE : (b + 1) * TILE, pl.ds(j0, lc), :], 0, 1)
            dst[pl.ds(j0, lc), b * TILE : (b + 1) * TILE, :] = t

    incoming(c0)

    def prepare(wide, m):
        f = factors(strips(mid, wide), strips(mask, wide), wf[1])
        for q, v in enumerate(f):
            saved[q, :m] = jnp.broadcast_to(v, (m, c))

    each(prepare, my_col == 0)

    @pl.when(jnp.logical_and(my_col == 0, owner))
    def _():
        transposed(in_left, left_t, c0)
        transposed(in_right, right_t, c0)

    incoming(o0, e_in_left)

    others = pl.ds(0, (rows - 1) * lr)
    e_ct = pltpu.make_async_remote_copy(
        src_ref=ct_h.at[others],
        dst_ref=ct_h.at[others],
        send_sem=ct_send.at[0],
        recv_sem=ct_recv.at[0],
        device_id={"col": other},
        device_id_type=MESH,
    )
    e_ct.wait_recv()
    own[1].wait()

    def signal(i0):
        z, r = norm(block(in_mixed, i0, lc))
        ct = ct_h[pl.ds(i0, lc)].reshape(lc * lc, c).astype(F32)
        put(ct32, i0, lc, ct)
        dz = rounded(dot_t(ct * block(in_gate, i0, lc), wo[1]))
        put_half(sig, i0, lc, rounded(norm_back(z, r, dz)))

    signal(o0)
    e_sig = partner(2, 4, half(sig, o0, lc))
    e_sig.start()
    signal(c0)
    e_in_right.wait_recv()

    def turn_signal(j0):
        for b in range(lc // TILE):
            t = jnp.swapaxes(sig[pl.ds(c0 + b * TILE, TILE), pl.ds(j0, lc), :], 0, 1)
            flip_s[:, b * TILE : (b + 1) * TILE, :] = t

    def left_row(j0, acc):
        return triangle(
            lr, lc, 0, lc,
            lambda a, q: in_right[r0 + a, pl.ds(j0 + q, 1), :],
            lambda q: flip_s[q],
            acc,
        )

    def left_col(j0, acc):
        return triangle(
            lr, n, 0, lc,
            lambda a, q: sig[r0 + a, pl.ds(j0 + q, 1), :],
            lambda q: right_t[j0 + q],
            acc,
        )

    def keep(ref, start, width, acc, fix=lambda v: v):
        for a in range(lr):
            ref[start + a * width : start + (a + 1) * width] = fix(acc[a])

    def kept(ref, start, width):
        return [ref[start + a * width : start + (a + 1) * width] for a in range(lr)]

    turn_signal(c0)
    keep(d_right, 0, lc, triangle(
        lr, lc, 0, n,
        lambda a, q: in_left[r0 + a, pl.ds(q, 1), :],
        lambda q: sig[q, pl.ds(c0, lc), :],
    ), rounded)
    keep(d_left, 0, lc, left_row(c0, None))

    @pl.when(owner)
    def _():
        @pl.when(my_col != 0)
        def _():
            transposed(in_left, left_t, c0)
            transposed(in_right, right_t, c0)

        transposed(in_left, left_t, o0)
        transposed(in_right, right_t, o0)
        keep(d_right, nr, n, triangle(
            lr, n, 0, n,
            lambda a, q: sig[q, pl.ds(r0 + a, 1), :],
            lambda q: left_t[q],
        ), rounded)
        keep(d_left, nr, n, left_col(c0, None))

    def prepare_more(wide, m):
        z1, _ = norm(strips(in_mixed, wide))
        saved[7, :m] = strips(ct32, wide) * dot(z1, wo[1])

    each(prepare, my_col == 1)
    each(prepare_more)
    e_sig.wait_recv()
    turn_signal(o0)
    keep(d_left, 0, lc, left_row(o0, kept(d_left, 0, lc)), rounded)

    @pl.when(owner)
    def _():
        keep(d_left, nr, n, left_col(o0, kept(d_left, nr, n)), rounded)

    def back(wide, m):
        f = tuple(saved[q, :m] for q in range(7))
        g = rounded(strips(ct32, wide) + front_back(f, wf[1], d_left[:m], d_right[:m], saved[7, :m]))
        z0, r = norm(strips(mixed, wide))
        dz = rounded(dot_t(g * strips(gate, wide), wo[0]))
        s = rounded(norm_back(z0, r, dz))
        along_row = s[:nr].reshape(lr, lc, c)
        sig_row[:, pl.ds(c0, lc), :] = along_row
        saved[8, :nr] = g[:nr]
        if wide:
            sig_col[...] = s[nr:].reshape(lr, n, c)

    each(back)
    e_row = partner(3, 5, sig_row.at[:, pl.ds(c0, lc)])
    e_row.start()
    e_col = partner(4, 6, sig_col)

    @pl.when(owner)
    def _():
        e_col.start()

    x = x_h[pl.ds(r0, lr)].reshape(nr, c).astype(F32)
    f = factors(x, row_of(mask), wf[0])
    z0, _ = norm(row_of(mixed))
    g = saved[8, :nr]
    d_gate = g * dot(z0, wo[0])

    def out_left(j0, acc):
        return triangle(
            lr, lc, 0, lc,
            lambda a, q: sig_row[a, pl.ds(j0 + q, 1), :],
            lambda q: right[j0 + q, pl.ds(c0, lc), :],
            acc,
        )

    acc = out_left(c0, None)
    e_row.wait_recv()
    d_a = jnp.concatenate([rounded(v) for v in out_left(o0, acc)], axis=0)

    @pl.when(jnp.logical_not(owner))
    def _():
        e_col.wait_recv()

    d_b = jnp.concatenate([rounded(v) for v in triangle(
        lr, lc, 0, n,
        lambda a, q: sig_col[a, pl.ds(q, 1), :],
        lambda q: left[q, pl.ds(c0, lc), :],
    )], axis=0)
    out[...] = (g + front_back(f, wf[0], d_a, d_b, d_gate)).astype(BF16).reshape(lr, lc, c)

    higher(drain)
    e_ct.wait_send()
    for copy in (e_out, partner(1, 3, in_left), e_sig, e_row):
        copy.wait_send()

    @pl.when(owner)
    def _():
        e_col.wait_send()


def from_root(array, axis, root):
    mine = lax.axis_index(axis) == root
    return lax.psum(jnp.where(mine, array, jnp.zeros_like(array)), axis)


def layer_norm(values):
    centred = values - jnp.mean(values, axis=-1, keepdims=True)
    spread = jnp.mean(centred * centred, axis=-1, keepdims=True)
    return centred * lax.rsqrt(spread + 1e-05)


def project_pair(inner_pair, mask_pair, weight):
    normed = layer_norm(inner_pair.astype(jnp.float32)).astype(jnp.bfloat16)
    linear = jnp.dot(normed, weight, preferred_element_type=jnp.float32)
    left_side = jax.nn.sigmoid(linear[..., :H]) * linear[..., H : 2 * H]
    right_side = jax.nn.sigmoid(linear[..., 2 * H : 3 * H]) * linear[..., 3 * H : 4 * H]
    operands = (jnp.stack((left_side, right_side)) * mask_pair[None, :, :, None]).astype(
        jnp.bfloat16
    )
    return (operands, jax.nn.sigmoid(linear[..., 4 * H :]))


def finish(mixed_part, gate_value, inner_pair, weight):
    normed = layer_norm(mixed_part).astype(jnp.bfloat16)
    update = jnp.dot(normed, weight, preferred_element_type=jnp.float32)
    return (inner_pair.astype(jnp.float32) + gate_value * update).astype(jnp.bfloat16)


def body(pair_act, cotangent, residue_mask, front_weight, out_weight):
    local_rows = pair_act.shape[0]
    local_cols = pair_act.shape[1]
    row_index = lax.axis_index("row")
    col_index = lax.axis_index("col")
    block_rows = lax.axis_size("row") // lax.axis_size("col")
    owner_col = row_index // block_rows
    offset = row_index % block_rows * local_rows
    chain_mask = residue_mask.astype(jnp.float32)
    mask_rows = lax.dynamic_slice_in_dim(chain_mask, row_index * local_rows, local_rows)
    mask_cols = lax.dynamic_slice_in_dim(chain_mask, col_index * local_cols, local_cols)
    mask_pair = mask_rows[:, None] * mask_cols[None, :]

    def gather_rows(stacked):
        return lax.all_gather(stacked, "row", axis=1, tiled=True)

    def column_block(gathered):
        slab = lax.dynamic_slice_in_dim(gathered, offset, local_rows, 1)
        return from_root(slab, "col", owner_col)

    def gather_cols(values):
        return lax.all_gather(values, "col", axis=1, tiled=True)

    def sum_cols(partial_term):
        return lax.psum_scatter(
            partial_term.astype(jnp.bfloat16), "col", scatter_dimension=1, tiled=True
        ).astype(jnp.float32)

    (out_ops, out_gate), out_front_back = jax.vjp(
        lambda inner_pair: project_pair(inner_pair, mask_pair, front_weight[0]), pair_act
    )
    fetched = gather_rows(out_ops)
    out_mixed = sum_cols(
        jnp.einsum("ikc,jkc->ijc", out_ops[0], fetched[-1], preferred_element_type=jnp.float32)
    )
    pair_mid, out_finish_back = jax.vjp(
        lambda mixed_part, gate_value, inner_pair: finish(
            mixed_part, gate_value, inner_pair, out_weight[0]
        ),
        out_mixed,
        out_gate,
        pair_act,
    )
    (in_ops, in_gate), in_front_back = jax.vjp(
        lambda inner_pair: project_pair(inner_pair, mask_pair, front_weight[1]), pair_mid
    )
    in_fetched = gather_rows(in_ops)
    left_block = column_block(in_fetched[0])
    in_mixed = jnp.einsum(
        "kic,kjc->ijc", left_block, in_fetched[1], preferred_element_type=jnp.float32
    )
    unused_pair, in_finish_back = jax.vjp(
        lambda mixed_part, gate_value, inner_pair: finish(
            mixed_part, gate_value, inner_pair, out_weight[1]
        ),
        in_mixed,
        in_gate,
        pair_mid,
    )
    grad_mixed, grad_gate, grad_inner = in_finish_back(cotangent)
    signal = grad_mixed.astype(jnp.bfloat16)
    signal_rows = gather_rows(signal[None])[0]
    left_rows = gather_cols(in_ops[0])
    grad_right = jnp.einsum(
        "kic,ijc->kjc", left_rows, signal_rows, preferred_element_type=jnp.float32
    )
    grad_left = sum_cols(
        jnp.einsum("kjc,ijc->kic", in_ops[1], signal_rows, preferred_element_type=jnp.float32)
    )
    (grad_front,) = in_front_back(
        (jnp.stack((grad_left, grad_right)).astype(jnp.bfloat16), grad_gate)
    )
    grad_mid = (grad_inner.astype(jnp.float32) + grad_front.astype(jnp.float32)).astype(
        jnp.bfloat16
    )
    grad_mixed, grad_gate, grad_inner = out_finish_back(grad_mid)
    signal = grad_mixed.astype(jnp.bfloat16)
    signal_cols = gather_cols(signal)
    grad_left = jnp.einsum(
        "ijc,jkc->ikc", signal_cols, fetched[-1], preferred_element_type=jnp.float32
    )
    signal_block = column_block(gather_rows(signal[None])[0])
    grad_right = jnp.einsum(
        "ijc,ikc->jkc", signal_block, fetched[0], preferred_element_type=jnp.float32
    )
    (grad_front,) = out_front_back(
        (jnp.stack((grad_left, grad_right)).astype(jnp.bfloat16), grad_gate)
    )
    return (grad_inner.astype(jnp.float32) + grad_front.astype(jnp.float32)).astype(jnp.bfloat16)


def crop_body(rows, pair_act, cotangent, residue_mask, front_weight, out_weight):
    lr, lc, c = pair_act.shape
    n = residue_mask.shape[0]
    strip = lr * lc + lr * n
    dma = pltpu.SemaphoreType.DMA
    operands = (pair_act, cotangent, residue_mask.reshape(1, n), front_weight, out_weight)
    return pl.pallas_call(
        functools.partial(crop_kernel, rows),
        out_shape=jax.ShapeDtypeStruct((lr, lc, c), BF16),
        in_specs=[pl.BlockSpec(memory_space=pl.ANY)] * 5,
        out_specs=pl.BlockSpec(memory_space=pltpu.VMEM),
        scratch_shapes=[
            pltpu.VMEM((n, lc, c), BF16),
            pltpu.VMEM((n, lc, c), BF16),
            pltpu.VMEM(front_weight.shape, BF16),
            pltpu.VMEM(out_weight.shape, BF16),
            pltpu.VMEM((1, n), jnp.int32),
        ]
        + [pltpu.VMEM((n, n, c), F32)] * 7
        + [pltpu.VMEM((lc, lc, c), F32)] * 2
        + [pltpu.VMEM((n * lc, c), F32)] * 7
        + [
            pltpu.VMEM((n * lc, c), BF16),
            pltpu.VMEM((n, c), F32),
            pltpu.VMEM((9, strip, c), F32),
            pltpu.VMEM((strip, c), F32),
            pltpu.VMEM((strip, c), F32),
            pltpu.VMEM((lr, n, c), F32),
            pltpu.VMEM((lr, n, c), F32),
        ]
        + [dma((5,)), dma((rows,)), dma((rows,)), dma((1,)), dma((1,)), dma((5,)), dma((7,))]
        + [pltpu.SemaphoreType.REGULAR((rows + 1,))],
        compiler_params=pltpu.CompilerParams(
            collective_id=0, has_side_effects=True, vmem_limit_bytes=VMEM_BUDGET
        ),
    )(*[pltpu.with_memory_space_constraint(v, pltpu.HBM) for v in operands])


def fits(mesh, n, lr, lc, c):
    rows, cols = mesh.shape["row"], mesh.shape["col"]
    return (
        cols == 2
        and rows >= 2
        and rows & (rows - 1) == 0
        and n == 2 * lc
        and lc == 2 * TILE
        and lc % (2 * lr) == 0
        and FULL_ARRAYS * 4 * n * n * c <= VMEM_BUDGET
    )


def solution(mesh):
    def dispatch(pair_act, cotangent, residue_mask, front_weight, out_weight):
        n = residue_mask.shape[0]
        if fits(mesh, n, *pair_act.shape):
            return crop_body(
                mesh.shape["row"], pair_act, cotangent, residue_mask, front_weight, out_weight
            )
        return body(pair_act, cotangent, residue_mask, front_weight, out_weight)

    placed = (P(("grp", "row"), "col", None), P(("grp", "row"), "col", None), P("grp"), P(), P())
    return jax.shard_map(
        dispatch,
        mesh=mesh,
        in_specs=placed,
        out_specs=P(("grp", "row"), "col", None),
        check_vma=False,
    )
```

```python
import functools

import jax
import jax.numpy as jnp
from jax import lax
from jax.experimental import pallas as pl
from jax.experimental.pallas import tpu as pltpu
from jax.sharding import PartitionSpec as P

H = 128
TILE = 8
F32 = jnp.float32
BF16 = jnp.bfloat16
MESH = pl.DeviceIdType.MESH
VMEM_BUDGET = 24 << 20
FULL_ARRAYS = 16


def sigmoid(x):
    return 0.5 * jnp.tanh(0.5 * x) + 0.5


def norm(v):
    centred = v - jnp.mean(v, axis=-1, keepdims=True)
    r = lax.rsqrt(jnp.mean(centred * centred, axis=-1, keepdims=True) + 1e-05)
    return centred * r, r


def scales(v):
    mean = jnp.mean(v, axis=-1, keepdims=True)
    centred = v - mean
    r = lax.rsqrt(jnp.mean(centred * centred, axis=-1, keepdims=True) + 1e-05)
    return r, r * mean


def column_sums(w):
    return jnp.sum(w.astype(F32), axis=0, keepdims=True)


def norm_back(y, r, d):
    return r * (d - jnp.mean(d, axis=-1, keepdims=True) - y * jnp.mean(d * y, axis=-1, keepdims=True))


def rounded(v):
    return v.astype(BF16).astype(F32)


def dot(a, b):
    return jnp.dot(a.astype(BF16), b, preferred_element_type=F32)


def dot_t(a, b):
    return lax.dot_general(
        a.astype(BF16), b, (((1,), (1,)), ((), ())), preferred_element_type=F32
    )


def part(p, n):
    return p[:, n * H : (n + 1) * H]


def factors(x, mask, weight):
    y, r = norm(x)
    p = dot(y, weight)
    s0, s2, s4 = sigmoid(part(p, 0)), sigmoid(part(p, 2)), sigmoid(part(p, 4))
    fa, fb = mask * s0, mask * s2
    return y, r, fa * part(p, 1) * (1.0 - s0), fa, fb * part(p, 3) * (1.0 - s2), fb, s4 * (1.0 - s4)


def front_back(f, weight, d_a, d_b, d_gate):
    y, r, f0, f1, f2, f3, f4 = f
    d = jnp.concatenate(
        [(v.astype(BF16)) for v in (d_a * f0, d_a * f1, d_b * f2, d_b * f3, d_gate * f4)], axis=1
    )
    return rounded(norm_back(y, r, rounded(dot_t(d, weight))))


def crop_kernel(
    rows, pair, cot, mask_in, wf_in, wo_in, out,
    x_h, ct_h, x_far, wf, wo, chain,
    left, right, in_left, in_right, sig, left_t, right_t, flip_r, flip_s,
    mask, mixed, gate, mid, in_mixed, in_gate, ct32, normed, along,
    saved, d_left, d_right, sig_row, sig_col,
    local_sem, x_send, x_recv, ct_send, ct_recv, psend, precv, ready, far_send, far_recv,
):
    n, c = left.shape[0], left.shape[2]
    lr, lc = out.shape[0], out.shape[1]
    bits = rows.bit_length() - 1
    me, my_col = lax.axis_index("row"), lax.axis_index("col")
    other = 1 - my_col
    me_bits = [lax.rem(lax.div(me, 1 << b), 2) for b in range(bits)]

    def flip(d, low=0):
        total = 0
        for b in range(low, bits):
            bit = me_bits[b]
            total = total + (1 - bit if d >> b & 1 else bit) * (1 << b)
        return total

    far = rows - 2 if rows > 4 else rows
    wide_row = jnp.logical_and(me >= far, my_col == 0)
    near_row = jnp.logical_and(me == 0, rows > 4)
    barrier = pltpu.get_barrier_semaphore()
    pl.semaphore_signal(barrier, inc=1, device_id={"col": other}, device_id_type=MESH)
    for row in range(1, rows):
        @pl.when(jnp.logical_and(me < row, me != row - 1) if row == far else me < row)
        def _():
            pl.semaphore_signal(barrier, inc=1, device_id={"row": row}, device_id_type=MESH)

    for row in range(far, rows):
        @pl.when(jnp.logical_and(me == 0, my_col == 1))
        def _():
            pl.semaphore_signal(
                barrier, inc=1, device_id={"row": row, "col": 0}, device_id_type=MESH
            )

    r0 = pl.multiple_of(me * lr, lr)
    c0 = pl.multiple_of(my_col * lc, lc)
    o0 = pl.multiple_of(other * lc, lc)
    jl = lax.rem(me * lr, lc)
    owner = lax.div(me * lr, lc) == my_col

    own = [
        pltpu.make_async_copy(src, dst.at[pl.ds(r0, lr)], local_sem.at[t])
        for t, (src, dst) in enumerate(((pair, x_h), (cot, ct_h)))
    ]
    weights = [
        pltpu.make_async_copy(wf_in, wf, local_sem.at[2]),
        pltpu.make_async_copy(wo_in, wo, local_sem.at[3]),
    ]
    chain_copy = pltpu.make_async_copy(mask_in, chain, local_sem.at[4])
    for copy in [chain_copy, own[0]] + weights + [own[1]]:
        copy.start()

    def direct(t, row, mine=None):
        src, dst = ((pair, x_h), (cot, ct_h))[t]
        source = row if mine is None else mine
        return pltpu.make_async_remote_copy(
            src_ref=src,
            dst_ref=dst.at[pl.ds(pl.multiple_of(source * lr, lr), lr)],
            send_sem=x_send.at[row] if t == 0 else ct_send.at[0],
            recv_sem=x_recv.at[source] if t == 0 else ct_recv.at[0],
            device_id={"row": row},
            device_id_type=MESH,
        )

    def lower(step, start=0):
        for row in range(start, rows - 1):
            @pl.when(jnp.logical_and(row < me, me != far) if row == far - 1 else row < me)
            def _():
                step(row)

    def higher(step):
        for row in range(1, rows):
            @pl.when(jnp.logical_or(row > me, me == far) if row == far - 1 else row > me)
            def _():
                step(row)

    def far_copy():
        at = pl.ds(pl.multiple_of((me - far) * lr, lr), lr)
        return pltpu.make_async_remote_copy(
            src_ref=pair,
            dst_ref=x_far.at[at],
            send_sem=far_send.at[0],
            recv_sem=far_recv.at[me - far],
            device_id={"row": 0, "col": 1},
            device_id_type=MESH,
        )

    def answer(row):
        if row == 0:
            @pl.when(jnp.logical_not(wide_row))
            def _():
                direct(0, row, me).start()
        elif row < 2:
            direct(0, row, me).start()
        pl.semaphore_signal(ready.at[me], inc=1, device_id={"row": row}, device_id_type=MESH)

    def send(row):
        if row >= 2:
            direct(0, row, me).start()

    def tell(row, about):
        pl.semaphore_signal(ready.at[about], inc=1, device_id={"row": row}, device_id_type=MESH)

    def follow(row):
        pl.semaphore_wait(ready.at[row], 1)
        direct(0, row, me).start()
        if row == far:
            @pl.when(me == far - 2)
            def _():
                tell(far, far - 1)
                tell(far - 1, far)

    def drain(row):
        direct(0, row, me).wait_send()

    def second(row):
        direct(1, row, me).start()

    def partner(q, r, ref):
        return pltpu.make_async_remote_copy(
            src_ref=ref,
            dst_ref=ref,
            send_sem=psend.at[q],
            recv_sem=precv.at[r],
            device_id={"col": other},
            device_id_type=MESH,
        )

    greeted = me + 1 - jnp.where(me == far, 1, 0)
    pl.semaphore_wait(barrier, greeted + jnp.where(wide_row, 1, 0))

    @pl.when(wide_row)
    def _():
        direct(0, 0, me).start()
        far_copy().start()

    lower(answer)

    chain_copy.wait()
    span = jnp.broadcast_to(chain[...].astype(F32), (n, n))
    here = lax.broadcasted_iota(jnp.int32, (n, n), 0) == lax.broadcasted_iota(jnp.int32, (n, n), 1)
    along[...] = jnp.broadcast_to(
        jnp.sum(jnp.where(here, span, 0.0), axis=1, keepdims=True), (n, c)
    )
    across = along[pl.ds(c0, lc), :]
    for i in range(n):
        mask[i * lc : (i + 1) * lc] = across * along[i : i + 1]
    lower(send)

    def block(ref, k0, nk):
        return ref[pl.ds(pl.multiple_of(k0 * lc, lc), nk * lc), :]

    def put(ref, k0, nk, v):
        ref[pl.ds(pl.multiple_of(k0 * lc, lc), nk * lc), :] = v

    def put_half(ref, k0, nk, v):
        ref[pl.ds(k0, nk), pl.ds(c0, lc), :] = v.reshape(nk, lc, c)

    def half(ref, k0, nk):
        return ref.at[pl.ds(k0, nk), pl.ds(c0, lc)]

    def projected(x, segments, weight, sums, a_ref, b_ref, g_ref):
        r, rm = scales(x.astype(F32))
        p = dot(x, weight)

        def part(p, q):
            return p[:, q * H : (q + 1) * H] * r - rm * sums[:, q * H : (q + 1) * H]

        m = jnp.concatenate([block(mask, k0, nk) for k0, nk in segments], axis=0)
        a = rounded(sigmoid(part(p, 0)) * part(p, 1) * m)
        b = rounded(sigmoid(part(p, 2)) * part(p, 3) * m)
        g = sigmoid(part(p, 4))
        at = 0
        for k0, nk in segments:
            span = slice(at * lc, (at + nk) * lc)
            put_half(a_ref, k0, nk, a[span])
            put_half(b_ref, k0, nk, b[span])
            put(g_ref, k0, nk, g[span])
            at += nk

    def triangle(count, width, first, depth, row_at, tile_at, acc=None):
        def term(q, acc):
            t = tile_at(first + q)
            return tuple(v + row_at(a, first + q) * t for a, v in enumerate(acc))

        if acc is None:
            acc = (jnp.zeros((width, c), F32),) * count
        return lax.fori_loop(0, depth, term, tuple(acc), unroll=True)

    def loop(count, step):
        def body(k, carry):
            step(k)
            return carry

        lax.fori_loop(0, count, body, 0)

    for copy in weights:
        copy.wait()
    sums_out, sums_in, sums_mix = (column_sums(w) for w in (wf[0], wf[1], wo[0]))
    groups = [[(0, 1)], [(1, 1), (2, 2)] if rows > 2 else [(1, 1)]]
    groups += [[(d, 2)] for d in range(4, rows, 2)]
    for g, group in enumerate(groups):
        for d, count in group:
            for q in range(d, d + count):
                if q == 0:
                    own[0].wait()
                else:
                    direct(0, flip(q)).wait_recv()
        segments = [
            (pl.multiple_of(flip(d, count.bit_length() - 1) * lr, count * lr), count * lr)
            for d, count in group
        ]
        x = jnp.concatenate(
            [x_h[pl.ds(k0, nk)].reshape(nk * lc, c) for k0, nk in segments], axis=0
        )
        projected(x, segments, wf[0], sums_out, left, right, gate)
        def exchange():
            for k0, nk in segments:
                partner(0, 0, half(left, k0, nk)).start()
                partner(0, 0, half(right, k0, nk)).start()

        if g == len(groups) - 1 and rows > 4:
            pl.when(jnp.logical_not(jnp.logical_and(near_row, my_col == 0)))(exchange)
        else:
            exchange()
        if g == 0:
            higher(follow)

            @pl.when(me > 0)
            def _():
                second(0)

            lower(drain)
            pl.semaphore_signal(
                ready.at[rows], inc=1, device_id={"col": other}, device_id_type=MESH
            )
            pl.semaphore_wait(ready.at[rows], 1)
            lower(second, 1)
        if g == len(groups) - 1:
            higher(second)

    group = TILE

    def outgoing(k0, fresh):
        for b in range(lc // TILE):
            t = jnp.swapaxes(right[pl.ds(c0 + b * TILE, TILE), pl.ds(k0, lc), :], 0, 1)
            flip_r[:, b * TILE : (b + 1) * TILE, :] = t

        def step(b):
            i0 = b * group
            base = pl.multiple_of(i0 * lc, lc * group)
            acc = None
            if not fresh:
                acc = [mixed[pl.ds(base + a * lc, lc), :] for a in range(group)]
            acc = triangle(
                group, lc, 0, lc,
                lambda a, q: left[i0 + a, pl.ds(k0 + q, 1), :],
                lambda q: flip_r[q],
                acc,
            )
            for a in range(group):
                mixed[pl.ds(base + a * lc, lc), :] = acc[a]

        loop(n // group, step)

    outgoing(c0, True)

    @pl.when(jnp.logical_and(near_row, my_col == 1))
    def _():
        for q in range(2):
            pltpu.make_async_remote_copy(
                src_ref=pair,
                dst_ref=x_far.at[pl.ds(q * lr, lr)],
                send_sem=far_send.at[0],
                recv_sem=far_recv.at[q],
                device_id={"row": 0, "col": 0},
                device_id_type=MESH,
            ).wait_recv()
        x = x_far[...].reshape(2 * lr * lc, c)
        r, rm = scales(x.astype(F32))
        p = dot(x, wf[0, :, : 4 * H])

        def scaled(q):
            return part(p, q) * r - rm * part(sums_out, q)

        k0 = far * lr
        over = along[pl.ds(o0, lc), :]
        m = jnp.concatenate([over * along[k0 + i : k0 + i + 1] for i in range(2 * lr)], axis=0)
        a = rounded(sigmoid(scaled(0)) * scaled(1) * m)
        b = rounded(sigmoid(scaled(2)) * scaled(3) * m)
        left[k0:, pl.ds(o0, lc), :] = a.reshape(2 * lr, lc, c)
        right[k0:, pl.ds(o0, lc), :] = b.reshape(2 * lr, lc, c)

    def pair_bytes(column, step):
        @pl.when(jnp.logical_and(near_row, my_col == column))
        def _():
            step(partner(0, 0, left.at[pl.ds(0, far * lr)]))

        @pl.when(jnp.logical_not(jnp.logical_and(near_row, my_col == column)))
        def _():
            step(partner(0, 0, left))

    pair_bytes(1, lambda copy: copy.wait_recv())
    outgoing(o0, False)

    v = mixed[...]
    r, rm = scales(v)
    high = v.astype(BF16)
    low = (v - high.astype(F32)).astype(BF16)
    update = dot(
        jnp.concatenate([high, low], axis=1), jnp.concatenate([wo[0], wo[0]], axis=0)
    )
    x = x_h[...].reshape(n * lc, c).astype(F32)
    x = rounded(x + gate[...] * (update * r - rm * sums_mix))
    mid[...] = x
    r, rm = scales(x)

    def scaled(p, q, at):
        return part(p, q) * r - rm * part(sums_in, at + q)

    x = x.astype(BF16)
    normed[...] = x
    p = dot(x, wf[1, :, : 2 * H])
    put_half(in_left, 0, n, rounded(sigmoid(scaled(p, 0, 0)) * scaled(p, 1, 0) * mask[...]))
    e_in_left = [
        partner(1, 1 + b, in_left.at[:, pl.ds(c0 + b * TILE, TILE)]) for b in range(lc // TILE)
    ]
    for copy in e_in_left:
        copy.start()
    p = dot(normed[...], wf[1, :, 2 * H :])
    v = rounded(sigmoid(scaled(p, 0, 2)) * scaled(p, 1, 2) * mask[...])
    put_half(in_right, 0, n, v)
    in_gate[...] = sigmoid(scaled(p, 2, 2))
    e_in_right = partner(1, 3, half(in_right, 0, n))
    e_in_right.start()

    def incoming(i0, copies=()):
        few = 4

        def step(i1):
            acc = triangle(
                few, lc, 0, n,
                lambda a, q: in_left[q, pl.ds(i1 + a, 1), :],
                lambda q: in_right[q, pl.ds(c0, lc), :],
            )
            for a in range(few):
                in_mixed[pl.ds(pl.multiple_of((i1 + a) * lc, lc), lc), :] = acc[a]

        for b in range(lc // TILE):
            if copies:
                copies[b].wait_recv()
            for a in range(0, TILE, few):
                step(pl.multiple_of(i0 + b * TILE, TILE) + a)

    nr, nc = lr * lc, lr * n

    def row_of(ref):
        return ref[pl.ds(pl.multiple_of(r0 * lc, lc), nr), :]

    def col_of(ref):
        return jnp.concatenate([ref[pl.ds(jl + a, n, stride=lc), :] for a in range(lr)], axis=0)

    def strips(ref, wide):
        return jnp.concatenate([row_of(ref), col_of(ref)], axis=0) if wide else row_of(ref)

    def each(step, here=True):
        @pl.when(jnp.logical_and(here, owner))
        def _():
            step(True, nr + nc)

        @pl.when(jnp.logical_and(here, jnp.logical_not(owner)))
        def _():
            step(False, nr)

    def transposed(src, dst, j0):
        for b in range(n // TILE):
            t = jnp.swapaxes(src[b * TILE : (b + 1) * TILE, pl.ds(j0, lc), :], 0, 1)
            dst[pl.ds(j0, lc), b * TILE : (b + 1) * TILE, :] = t

    incoming(c0)

    def prepare(wide, m):
        f = factors(strips(mid, wide), strips(mask, wide), wf[1])
        for q, v in enumerate(f):
            saved[q, :m] = jnp.broadcast_to(v, (m, c))

    each(prepare, my_col == 0)

    @pl.when(jnp.logical_and(my_col == 0, owner))
    def _():
        transposed(in_left, left_t, c0)
        transposed(in_right, right_t, c0)

    incoming(o0, e_in_left)

    others = pl.ds(0, (rows - 1) * lr)
    e_ct = pltpu.make_async_remote_copy(
        src_ref=ct_h.at[others],
        dst_ref=ct_h.at[others],
        send_sem=ct_send.at[0],
        recv_sem=ct_recv.at[0],
        device_id={"col": other},
        device_id_type=MESH,
    )
    e_ct.wait_recv()
    own[1].wait()

    def signal(i0):
        z, r = norm(block(in_mixed, i0, lc))
        ct = ct_h[pl.ds(i0, lc)].reshape(lc * lc, c).astype(F32)
        put(ct32, i0, lc, ct)
        dz = rounded(dot_t(ct * block(in_gate, i0, lc), wo[1]))
        put_half(sig, i0, lc, rounded(norm_back(z, r, dz)))

    signal(o0)
    e_sig = partner(2, 4, half(sig, o0, lc))
    e_sig.start()
    signal(c0)
    e_in_right.wait_recv()

    def turn_signal(j0):
        for b in range(lc // TILE):
            t = jnp.swapaxes(sig[pl.ds(c0 + b * TILE, TILE), pl.ds(j0, lc), :], 0, 1)
            flip_s[:, b * TILE : (b + 1) * TILE, :] = t

    def left_row(j0, acc):
        return triangle(
            lr, lc, 0, lc,
            lambda a, q: in_right[r0 + a, pl.ds(j0 + q, 1), :],
            lambda q: flip_s[q],
            acc,
        )

    def left_col(j0, acc):
        return triangle(
            lr, n, 0, lc,
            lambda a, q: sig[r0 + a, pl.ds(j0 + q, 1), :],
            lambda q: right_t[j0 + q],
            acc,
        )

    def keep(ref, start, width, acc, fix=lambda v: v):
        for a in range(lr):
            ref[start + a * width : start + (a + 1) * width] = fix(acc[a])

    def kept(ref, start, width):
        return [ref[start + a * width : start + (a + 1) * width] for a in range(lr)]

    turn_signal(c0)
    keep(d_right, 0, lc, triangle(
        lr, lc, 0, n,
        lambda a, q: in_left[r0 + a, pl.ds(q, 1), :],
        lambda q: sig[q, pl.ds(c0, lc), :],
    ), rounded)
    keep(d_left, 0, lc, left_row(c0, None))

    @pl.when(owner)
    def _():
        @pl.when(my_col != 0)
        def _():
            transposed(in_left, left_t, c0)
            transposed(in_right, right_t, c0)

        transposed(in_left, left_t, o0)
        transposed(in_right, right_t, o0)
        keep(d_right, nr, n, triangle(
            lr, n, 0, n,
            lambda a, q: sig[q, pl.ds(r0 + a, 1), :],
            lambda q: left_t[q],
        ), rounded)
        keep(d_left, nr, n, left_col(c0, None))

    def prepare_more(wide, m):
        z1, _ = norm(strips(in_mixed, wide))
        saved[7, :m] = strips(ct32, wide) * dot(z1, wo[1])

    each(prepare, my_col == 1)
    each(prepare_more)
    e_sig.wait_recv()
    turn_signal(o0)
    keep(d_left, 0, lc, left_row(o0, kept(d_left, 0, lc)), rounded)

    @pl.when(owner)
    def _():
        keep(d_left, nr, n, left_col(o0, kept(d_left, nr, n)), rounded)

    def back(wide, m):
        f = tuple(saved[q, :m] for q in range(7))
        g = rounded(strips(ct32, wide) + front_back(f, wf[1], d_left[:m], d_right[:m], saved[7, :m]))
        z0, r = norm(strips(mixed, wide))
        dz = rounded(dot_t(g * strips(gate, wide), wo[0]))
        s = rounded(norm_back(z0, r, dz))
        along_row = s[:nr].reshape(lr, lc, c)
        sig_row[:, pl.ds(c0, lc), :] = along_row
        saved[8, :nr] = g[:nr]
        if wide:
            sig_col[...] = s[nr:].reshape(lr, n, c)

    each(back)
    e_row = partner(3, 5, sig_row.at[:, pl.ds(c0, lc)])
    e_row.start()
    e_col = partner(4, 6, sig_col)

    @pl.when(owner)
    def _():
        e_col.start()

    x = x_h[pl.ds(r0, lr)].reshape(nr, c).astype(F32)
    f = factors(x, row_of(mask), wf[0])
    z0, _ = norm(row_of(mixed))
    g = saved[8, :nr]
    d_gate = g * dot(z0, wo[0])

    def out_left(j0, acc):
        return triangle(
            lr, lc, 0, lc,
            lambda a, q: sig_row[a, pl.ds(j0 + q, 1), :],
            lambda q: right[j0 + q, pl.ds(c0, lc), :],
            acc,
        )

    acc = out_left(c0, None)
    e_row.wait_recv()
    d_a = jnp.concatenate([rounded(v) for v in out_left(o0, acc)], axis=0)

    @pl.when(jnp.logical_not(owner))
    def _():
        e_col.wait_recv()

    d_b = jnp.concatenate([rounded(v) for v in triangle(
        lr, lc, 0, n,
        lambda a, q: sig_col[a, pl.ds(q, 1), :],
        lambda q: left[q, pl.ds(c0, lc), :],
    )], axis=0)
    out[...] = (g + front_back(f, wf[0], d_a, d_b, d_gate)).astype(BF16).reshape(lr, lc, c)

    higher(drain)
    e_ct.wait_send()
    pair_bytes(0, lambda copy: copy.wait_send())

    @pl.when(wide_row)
    def _():
        far_copy().wait_send()

    for copy in (partner(1, 3, in_left), e_sig, e_row):
        copy.wait_send()

    @pl.when(owner)
    def _():
        e_col.wait_send()


def from_root(array, axis, root):
    mine = lax.axis_index(axis) == root
    return lax.psum(jnp.where(mine, array, jnp.zeros_like(array)), axis)


def layer_norm(values):
    centred = values - jnp.mean(values, axis=-1, keepdims=True)
    spread = jnp.mean(centred * centred, axis=-1, keepdims=True)
    return centred * lax.rsqrt(spread + 1e-05)


def project_pair(inner_pair, mask_pair, weight):
    normed = layer_norm(inner_pair.astype(jnp.float32)).astype(jnp.bfloat16)
    linear = jnp.dot(normed, weight, preferred_element_type=jnp.float32)
    left_side = jax.nn.sigmoid(linear[..., :H]) * linear[..., H : 2 * H]
    right_side = jax.nn.sigmoid(linear[..., 2 * H : 3 * H]) * linear[..., 3 * H : 4 * H]
    operands = (jnp.stack((left_side, right_side)) * mask_pair[None, :, :, None]).astype(
        jnp.bfloat16
    )
    return (operands, jax.nn.sigmoid(linear[..., 4 * H :]))


def finish(mixed_part, gate_value, inner_pair, weight):
    normed = layer_norm(mixed_part).astype(jnp.bfloat16)
    update = jnp.dot(normed, weight, preferred_element_type=jnp.float32)
    return (inner_pair.astype(jnp.float32) + gate_value * update).astype(jnp.bfloat16)


def body(pair_act, cotangent, residue_mask, front_weight, out_weight):
    local_rows = pair_act.shape[0]
    local_cols = pair_act.shape[1]
    row_index = lax.axis_index("row")
    col_index = lax.axis_index("col")
    block_rows = lax.axis_size("row") // lax.axis_size("col")
    owner_col = row_index // block_rows
    offset = row_index % block_rows * local_rows
    chain_mask = residue_mask.astype(jnp.float32)
    mask_rows = lax.dynamic_slice_in_dim(chain_mask, row_index * local_rows, local_rows)
    mask_cols = lax.dynamic_slice_in_dim(chain_mask, col_index * local_cols, local_cols)
    mask_pair = mask_rows[:, None] * mask_cols[None, :]

    def gather_rows(stacked):
        return lax.all_gather(stacked, "row", axis=1, tiled=True)

    def column_block(gathered):
        slab = lax.dynamic_slice_in_dim(gathered, offset, local_rows, 1)
        return from_root(slab, "col", owner_col)

    def gather_cols(values):
        return lax.all_gather(values, "col", axis=1, tiled=True)

    def sum_cols(partial_term):
        return lax.psum_scatter(
            partial_term.astype(jnp.bfloat16), "col", scatter_dimension=1, tiled=True
        ).astype(jnp.float32)

    (out_ops, out_gate), out_front_back = jax.vjp(
        lambda inner_pair: project_pair(inner_pair, mask_pair, front_weight[0]), pair_act
    )
    fetched = gather_rows(out_ops)
    out_mixed = sum_cols(
        jnp.einsum("ikc,jkc->ijc", out_ops[0], fetched[-1], preferred_element_type=jnp.float32)
    )
    pair_mid, out_finish_back = jax.vjp(
        lambda mixed_part, gate_value, inner_pair: finish(
            mixed_part, gate_value, inner_pair, out_weight[0]
        ),
        out_mixed,
        out_gate,
        pair_act,
    )
    (in_ops, in_gate), in_front_back = jax.vjp(
        lambda inner_pair: project_pair(inner_pair, mask_pair, front_weight[1]), pair_mid
    )
    in_fetched = gather_rows(in_ops)
    left_block = column_block(in_fetched[0])
    in_mixed = jnp.einsum(
        "kic,kjc->ijc", left_block, in_fetched[1], preferred_element_type=jnp.float32
    )
    unused_pair, in_finish_back = jax.vjp(
        lambda mixed_part, gate_value, inner_pair: finish(
            mixed_part, gate_value, inner_pair, out_weight[1]
        ),
        in_mixed,
        in_gate,
        pair_mid,
    )
    grad_mixed, grad_gate, grad_inner = in_finish_back(cotangent)
    signal = grad_mixed.astype(jnp.bfloat16)
    signal_rows = gather_rows(signal[None])[0]
    left_rows = gather_cols(in_ops[0])
    grad_right = jnp.einsum(
        "kic,ijc->kjc", left_rows, signal_rows, preferred_element_type=jnp.float32
    )
    grad_left = sum_cols(
        jnp.einsum("kjc,ijc->kic", in_ops[1], signal_rows, preferred_element_type=jnp.float32)
    )
    (grad_front,) = in_front_back(
        (jnp.stack((grad_left, grad_right)).astype(jnp.bfloat16), grad_gate)
    )
    grad_mid = (grad_inner.astype(jnp.float32) + grad_front.astype(jnp.float32)).astype(
        jnp.bfloat16
    )
    grad_mixed, grad_gate, grad_inner = out_finish_back(grad_mid)
    signal = grad_mixed.astype(jnp.bfloat16)
    signal_cols = gather_cols(signal)
    grad_left = jnp.einsum(
        "ijc,jkc->ikc", signal_cols, fetched[-1], preferred_element_type=jnp.float32
    )
    signal_block = column_block(gather_rows(signal[None])[0])
    grad_right = jnp.einsum(
        "ijc,ikc->jkc", signal_block, fetched[0], preferred_element_type=jnp.float32
    )
    (grad_front,) = out_front_back(
        (jnp.stack((grad_left, grad_right)).astype(jnp.bfloat16), grad_gate)
    )
    return (grad_inner.astype(jnp.float32) + grad_front.astype(jnp.float32)).astype(jnp.bfloat16)


def crop_body(rows, pair_act, cotangent, residue_mask, front_weight, out_weight):
    lr, lc, c = pair_act.shape
    n = residue_mask.shape[0]
    strip = lr * lc + lr * n
    dma = pltpu.SemaphoreType.DMA
    operands = (pair_act, cotangent, residue_mask.reshape(1, n), front_weight, out_weight)
    return pl.pallas_call(
        functools.partial(crop_kernel, rows),
        out_shape=jax.ShapeDtypeStruct((lr, lc, c), BF16),
        in_specs=[pl.BlockSpec(memory_space=pl.ANY)] * 5,
        out_specs=pl.BlockSpec(memory_space=pltpu.VMEM),
        scratch_shapes=[
            pltpu.VMEM((n, lc, c), BF16),
            pltpu.VMEM((n, lc, c), BF16),
            pltpu.VMEM((2 * lr, lc, c), BF16),
            pltpu.VMEM(front_weight.shape, BF16),
            pltpu.VMEM(out_weight.shape, BF16),
            pltpu.VMEM((1, n), jnp.int32),
        ]
        + [pltpu.VMEM((n, n, c), F32)] * 7
        + [pltpu.VMEM((lc, lc, c), F32)] * 2
        + [pltpu.VMEM((n * lc, c), F32)] * 7
        + [
            pltpu.VMEM((n * lc, c), BF16),
            pltpu.VMEM((n, c), F32),
            pltpu.VMEM((9, strip, c), F32),
            pltpu.VMEM((strip, c), F32),
            pltpu.VMEM((strip, c), F32),
            pltpu.VMEM((lr, n, c), F32),
            pltpu.VMEM((lr, n, c), F32),
        ]
        + [dma((5,)), dma((rows,)), dma((rows,)), dma((1,)), dma((1,)), dma((5,)), dma((7,))]
        + [pltpu.SemaphoreType.REGULAR((rows + 1,)), dma((1,)), dma((2,))],
        compiler_params=pltpu.CompilerParams(
            collective_id=0, has_side_effects=True, vmem_limit_bytes=VMEM_BUDGET
        ),
    )(*[pltpu.with_memory_space_constraint(v, pltpu.HBM) for v in operands])


def fits(mesh, n, lr, lc, c):
    rows, cols = mesh.shape["row"], mesh.shape["col"]
    return (
        cols == 2
        and rows >= 2
        and rows & (rows - 1) == 0
        and n == 2 * lc
        and lc == 2 * TILE
        and lc % (2 * lr) == 0
        and FULL_ARRAYS * 4 * n * n * c <= VMEM_BUDGET
    )


def solution(mesh):
    def dispatch(pair_act, cotangent, residue_mask, front_weight, out_weight):
        n = residue_mask.shape[0]
        if fits(mesh, n, *pair_act.shape):
            return crop_body(
                mesh.shape["row"], pair_act, cotangent, residue_mask, front_weight, out_weight
            )
        return body(pair_act, cotangent, residue_mask, front_weight, out_weight)

    placed = (P(("grp", "row"), "col", None), P(("grp", "row"), "col", None), P("grp"), P(), P())
    return jax.shard_map(
        dispatch,
        mesh=mesh,
        in_specs=placed,
        out_specs=P(("grp", "row"), "col", None),
        check_vma=False,
    )
```

```python
import functools

import jax
import jax.numpy as jnp
from jax import lax
from jax.experimental import pallas as pl
from jax.experimental.pallas import tpu as pltpu
from jax.sharding import PartitionSpec as P

H = 128
TILE = 8
F32 = jnp.float32
BF16 = jnp.bfloat16
MESH = pl.DeviceIdType.MESH
VMEM_BUDGET = 24 << 20
FULL_ARRAYS = 16


def sigmoid(x):
    return 0.5 * jnp.tanh(0.5 * x) + 0.5


def norm(v):
    centred = v - jnp.mean(v, axis=-1, keepdims=True)
    r = lax.rsqrt(jnp.mean(centred * centred, axis=-1, keepdims=True) + 1e-05)
    return centred * r, r


def scales(v):
    mean = jnp.mean(v, axis=-1, keepdims=True)
    centred = v - mean
    r = lax.rsqrt(jnp.mean(centred * centred, axis=-1, keepdims=True) + 1e-05)
    return r, r * mean


def column_sums(w):
    return jnp.sum(w.astype(F32), axis=0, keepdims=True)


def norm_back(y, r, d):
    return r * (d - jnp.mean(d, axis=-1, keepdims=True) - y * jnp.mean(d * y, axis=-1, keepdims=True))


def rounded(v):
    return v.astype(BF16).astype(F32)


def dot(a, b):
    return jnp.dot(a.astype(BF16), b, preferred_element_type=F32)


def dot_t(a, b):
    return lax.dot_general(
        a.astype(BF16), b, (((1,), (1,)), ((), ())), preferred_element_type=F32
    )


def part(p, n):
    return p[:, n * H : (n + 1) * H]


def factors(x, mask, weight):
    y, r = norm(x)
    p = dot(y, weight)
    s0, s2, s4 = sigmoid(part(p, 0)), sigmoid(part(p, 2)), sigmoid(part(p, 4))
    fa, fb = mask * s0, mask * s2
    return y, r, fa * part(p, 1) * (1.0 - s0), fa, fb * part(p, 3) * (1.0 - s2), fb, s4 * (1.0 - s4)


def front_back(f, weight, d_a, d_b, d_gate):
    y, r, f0, f1, f2, f3, f4 = f
    d = jnp.concatenate(
        [(v.astype(BF16)) for v in (d_a * f0, d_a * f1, d_b * f2, d_b * f3, d_gate * f4)], axis=1
    )
    return rounded(norm_back(y, r, rounded(dot_t(d, weight))))


def crop_kernel(
    rows, pair, cot, mask_in, wf_in, wo_in, out,
    x_h, ct_h, x_far, wf, wo, chain,
    left, right, in_left, in_right, sig, left_t, right_t, flip_r, flip_s,
    mask, mixed, gate, mid, in_mixed, in_gate, ct32, normed, along,
    saved, d_left, d_right, sig_row, sig_col,
    local_sem, x_send, x_recv, ct_send, ct_recv, psend, precv, ready, far_send, far_recv,
):
    n, c = left.shape[0], left.shape[2]
    lr, lc = out.shape[0], out.shape[1]
    bits = rows.bit_length() - 1
    me, my_col = lax.axis_index("row"), lax.axis_index("col")
    other = 1 - my_col
    me_bits = [lax.rem(lax.div(me, 1 << b), 2) for b in range(bits)]

    def flip(d, low=0):
        total = 0
        for b in range(low, bits):
            bit = me_bits[b]
            total = total + (1 - bit if d >> b & 1 else bit) * (1 << b)
        return total

    far = rows - 2 if rows > 4 else rows
    wide_row = jnp.logical_and(me >= far, my_col == 0)
    near_row = jnp.logical_and(me == 0, rows > 4)
    barrier = pltpu.get_barrier_semaphore()
    pl.semaphore_signal(barrier, inc=1, device_id={"col": other}, device_id_type=MESH)
    for row in range(1, rows):
        @pl.when(jnp.logical_and(me < row, me != row - 1) if row == far else me < row)
        def _():
            pl.semaphore_signal(barrier, inc=1, device_id={"row": row}, device_id_type=MESH)

    for row in range(far, rows):
        @pl.when(jnp.logical_and(me == 0, my_col == 1))
        def _():
            pl.semaphore_signal(
                barrier, inc=1, device_id={"row": row, "col": 0}, device_id_type=MESH
            )

    r0 = pl.multiple_of(me * lr, lr)
    c0 = pl.multiple_of(my_col * lc, lc)
    o0 = pl.multiple_of(other * lc, lc)
    jl = lax.rem(me * lr, lc)
    owner = lax.div(me * lr, lc) == my_col

    own = [
        pltpu.make_async_copy(src, dst.at[pl.ds(r0, lr)], local_sem.at[t])
        for t, (src, dst) in enumerate(((pair, x_h), (cot, ct_h)))
    ]
    weights = [
        pltpu.make_async_copy(wf_in, wf, local_sem.at[2]),
        pltpu.make_async_copy(wo_in, wo, local_sem.at[3]),
    ]
    chain_copy = pltpu.make_async_copy(mask_in, chain, local_sem.at[4])
    for copy in [chain_copy, own[0]] + weights + [own[1]]:
        copy.start()

    def direct(t, row, mine=None):
        src, dst = ((pair, x_h), (cot, ct_h))[t]
        source = row if mine is None else mine
        return pltpu.make_async_remote_copy(
            src_ref=src,
            dst_ref=dst.at[pl.ds(pl.multiple_of(source * lr, lr), lr)],
            send_sem=x_send.at[row] if t == 0 else ct_send.at[0],
            recv_sem=x_recv.at[source] if t == 0 else ct_recv.at[0],
            device_id={"row": row},
            device_id_type=MESH,
        )

    def lower(step, start=0):
        for row in range(start, rows - 1):
            @pl.when(jnp.logical_and(row < me, me != far) if row == far - 1 else row < me)
            def _():
                step(row)

    def higher(step):
        for row in range(1, rows):
            @pl.when(jnp.logical_or(row > me, me == far) if row == far - 1 else row > me)
            def _():
                step(row)

    def far_copy():
        at = pl.ds(pl.multiple_of((me - far) * lr, lr), lr)
        return pltpu.make_async_remote_copy(
            src_ref=pair,
            dst_ref=x_far.at[at],
            send_sem=far_send.at[0],
            recv_sem=far_recv.at[me - far],
            device_id={"row": 0, "col": 1},
            device_id_type=MESH,
        )

    def answer(row):
        if row == 0:
            @pl.when(jnp.logical_not(wide_row))
            def _():
                direct(0, row, me).start()
        elif row < 2:
            direct(0, row, me).start()
        pl.semaphore_signal(ready.at[me], inc=1, device_id={"row": row}, device_id_type=MESH)

    def send(row):
        if row >= 2:
            direct(0, row, me).start()

    def tell(row, about):
        pl.semaphore_signal(ready.at[about], inc=1, device_id={"row": row}, device_id_type=MESH)

    def follow(row):
        pl.semaphore_wait(ready.at[row], 1)
        direct(0, row, me).start()
        if row == far:
            @pl.when(me == far - 2)
            def _():
                tell(far, far - 1)
                tell(far - 1, far)

    def drain(row):
        direct(0, row, me).wait_send()

    def second(row):
        direct(1, row, me).start()

    def partner(q, r, ref):
        return pltpu.make_async_remote_copy(
            src_ref=ref,
            dst_ref=ref,
            send_sem=psend.at[q],
            recv_sem=precv.at[r],
            device_id={"col": other},
            device_id_type=MESH,
        )

    greeted = me + 1 - jnp.where(me == far, 1, 0)
    pl.semaphore_wait(barrier, greeted + jnp.where(wide_row, 1, 0))

    @pl.when(wide_row)
    def _():
        direct(0, 0, me).start()
        far_copy().start()

    lower(answer)

    chain_copy.wait()
    span = jnp.broadcast_to(chain[...].astype(F32), (n, n))
    here = lax.broadcasted_iota(jnp.int32, (n, n), 0) == lax.broadcasted_iota(jnp.int32, (n, n), 1)
    along[...] = jnp.broadcast_to(
        jnp.sum(jnp.where(here, span, 0.0), axis=1, keepdims=True), (n, c)
    )
    across = along[pl.ds(c0, lc), :]
    for i in range(n):
        mask[i * lc : (i + 1) * lc] = across * along[i : i + 1]
    lower(send)

    def block(ref, k0, nk):
        return ref[pl.ds(pl.multiple_of(k0 * lc, lc), nk * lc), :]

    def put(ref, k0, nk, v):
        ref[pl.ds(pl.multiple_of(k0 * lc, lc), nk * lc), :] = v

    def put_half(ref, k0, nk, v):
        ref[pl.ds(k0, nk), pl.ds(c0, lc), :] = v.reshape(nk, lc, c)

    def half(ref, k0, nk):
        return ref.at[pl.ds(k0, nk), pl.ds(c0, lc)]

    def projected(x, segments, weight, sums, a_ref, b_ref, g_ref):
        r, rm = scales(x.astype(F32))
        p = dot(x, weight)

        def part(p, q):
            return p[:, q * H : (q + 1) * H] * r - rm * sums[:, q * H : (q + 1) * H]

        m = jnp.concatenate([block(mask, k0, nk) for k0, nk in segments], axis=0)
        a = rounded(sigmoid(part(p, 0)) * part(p, 1) * m)
        b = rounded(sigmoid(part(p, 2)) * part(p, 3) * m)
        g = sigmoid(part(p, 4))
        at = 0
        for k0, nk in segments:
            span = slice(at * lc, (at + nk) * lc)
            put_half(a_ref, k0, nk, a[span])
            put_half(b_ref, k0, nk, b[span])
            put(g_ref, k0, nk, g[span])
            at += nk

    def triangle(count, width, first, depth, row_at, tile_at, acc=None):
        def term(q, acc):
            t = tile_at(first + q)
            return tuple(v + row_at(a, first + q) * t for a, v in enumerate(acc))

        if acc is None:
            acc = (jnp.zeros((width, c), F32),) * count
        return lax.fori_loop(0, depth, term, tuple(acc), unroll=True)

    def loop(count, step):
        def body(k, carry):
            step(k)
            return carry

        lax.fori_loop(0, count, body, 0)

    for copy in weights:
        copy.wait()
    sums_out, sums_in, sums_mix = (column_sums(w) for w in (wf[0], wf[1], wo[0]))
    groups = [[(0, 1)], [(1, 1), (2, 2)] if rows > 2 else [(1, 1)]]
    groups += [[(d, 2)] for d in range(4, rows, 2)]
    for g, group in enumerate(groups):
        for d, count in group:
            for q in range(d, d + count):
                if q == 0:
                    own[0].wait()
                else:
                    direct(0, flip(q)).wait_recv()
        segments = [
            (pl.multiple_of(flip(d, count.bit_length() - 1) * lr, count * lr), count * lr)
            for d, count in group
        ]
        x = jnp.concatenate(
            [x_h[pl.ds(k0, nk)].reshape(nk * lc, c) for k0, nk in segments], axis=0
        )
        projected(x, segments, wf[0], sums_out, left, right, gate)
        def exchange():
            for k0, nk in segments:
                partner(0, 0, half(left, k0, nk)).start()
                partner(0, 0, half(right, k0, nk)).start()

        if g == len(groups) - 1 and rows > 4:
            pl.when(jnp.logical_not(jnp.logical_and(near_row, my_col == 0)))(exchange)
        else:
            exchange()
        if g == 0:
            higher(follow)

            @pl.when(me > 0)
            def _():
                second(0)

            lower(drain)
            pl.semaphore_signal(
                ready.at[rows], inc=1, device_id={"col": other}, device_id_type=MESH
            )
            pl.semaphore_wait(ready.at[rows], 1)
            lower(second, 1)
        if g == len(groups) - 1:
            higher(second)

    group = TILE

    def outgoing(k0, fresh):
        for b in range(lc // TILE):
            t = jnp.swapaxes(right[pl.ds(c0 + b * TILE, TILE), pl.ds(k0, lc), :], 0, 1)
            flip_r[:, b * TILE : (b + 1) * TILE, :] = t

        def step(b):
            i0 = b * group
            base = pl.multiple_of(i0 * lc, lc * group)
            acc = None
            if not fresh:
                acc = [mixed[pl.ds(base + a * lc, lc), :] for a in range(group)]
            acc = triangle(
                group, lc, 0, lc,
                lambda a, q: left[i0 + a, pl.ds(k0 + q, 1), :],
                lambda q: flip_r[q],
                acc,
            )
            for a in range(group):
                mixed[pl.ds(base + a * lc, lc), :] = acc[a]

        loop(n // group, step)

    outgoing(c0, True)

    @pl.when(jnp.logical_and(near_row, my_col == 1))
    def _():
        for q in range(2):
            pltpu.make_async_remote_copy(
                src_ref=pair,
                dst_ref=x_far.at[pl.ds(q * lr, lr)],
                send_sem=far_send.at[0],
                recv_sem=far_recv.at[q],
                device_id={"row": 0, "col": 0},
                device_id_type=MESH,
            ).wait_recv()
        x = x_far[...].reshape(2 * lr * lc, c)
        r, rm = scales(x.astype(F32))
        p = dot(x, wf[0, :, : 4 * H])

        def scaled(q):
            return part(p, q) * r - rm * part(sums_out, q)

        k0 = far * lr
        over = along[pl.ds(o0, lc), :]
        m = jnp.concatenate([over * along[k0 + i : k0 + i + 1] for i in range(2 * lr)], axis=0)
        a = rounded(sigmoid(scaled(0)) * scaled(1) * m)
        b = rounded(sigmoid(scaled(2)) * scaled(3) * m)
        left[k0:, pl.ds(o0, lc), :] = a.reshape(2 * lr, lc, c)
        right[k0:, pl.ds(o0, lc), :] = b.reshape(2 * lr, lc, c)

    def pair_bytes(column, step):
        @pl.when(jnp.logical_and(near_row, my_col == column))
        def _():
            step(partner(0, 0, left.at[pl.ds(0, far * lr)]))

        @pl.when(jnp.logical_not(jnp.logical_and(near_row, my_col == column)))
        def _():
            step(partner(0, 0, left))

    pair_bytes(1, lambda copy: copy.wait_recv())
    outgoing(o0, False)

    v = mixed[...]
    r, rm = scales(v)
    high = v.astype(BF16)
    low = (v - high.astype(F32)).astype(BF16)
    update = dot(
        jnp.concatenate([high, low], axis=1), jnp.concatenate([wo[0], wo[0]], axis=0)
    )
    x = x_h[...].reshape(n * lc, c).astype(F32)
    x = rounded(x + gate[...] * (update * r - rm * sums_mix))
    mid[...] = x
    r, rm = scales(x)

    def scaled(p, q, at):
        return part(p, q) * r - rm * part(sums_in, at + q)

    x = x.astype(BF16)
    normed[...] = x
    p = dot(x, wf[1, :, : 2 * H])
    put_half(in_left, 0, n, rounded(sigmoid(scaled(p, 0, 0)) * scaled(p, 1, 0) * mask[...]))
    e_in_left = [
        partner(1, 1 + b, in_left.at[:, pl.ds(c0 + b * TILE, TILE)]) for b in range(lc // TILE)
    ]
    for copy in e_in_left:
        copy.start()
    p = dot(normed[...], wf[1, :, 2 * H :])
    v = rounded(sigmoid(scaled(p, 0, 2)) * scaled(p, 1, 2) * mask[...])
    put_half(in_right, 0, n, v)
    in_gate[...] = sigmoid(scaled(p, 2, 2))
    e_in_right = partner(1, 3, half(in_right, 0, n))
    e_in_right.start()

    def incoming(i0, copies=()):
        few = 4

        def step(i1):
            acc = triangle(
                few, lc, 0, n,
                lambda a, q: in_left[q, pl.ds(i1 + a, 1), :],
                lambda q: in_right[q, pl.ds(c0, lc), :],
            )
            for a in range(few):
                in_mixed[pl.ds(pl.multiple_of((i1 + a) * lc, lc), lc), :] = acc[a]

        for b in range(lc // TILE):
            if copies:
                copies[b].wait_recv()
            for a in range(0, TILE, few):
                step(pl.multiple_of(i0 + b * TILE, TILE) + a)

    nr, nc = lr * lc, lr * n

    def row_of(ref):
        return ref[pl.ds(pl.multiple_of(r0 * lc, lc), nr), :]

    def col_of(ref):
        return jnp.concatenate([ref[pl.ds(jl + a, n, stride=lc), :] for a in range(lr)], axis=0)

    def strips(ref, wide):
        return jnp.concatenate([row_of(ref), col_of(ref)], axis=0) if wide else row_of(ref)

    def each(step, here=True):
        @pl.when(jnp.logical_and(here, owner))
        def _():
            step(True, nr + nc)

        @pl.when(jnp.logical_and(here, jnp.logical_not(owner)))
        def _():
            step(False, nr)

    def transposed(src, dst, j0):
        for b in range(n // TILE):
            t = jnp.swapaxes(src[b * TILE : (b + 1) * TILE, pl.ds(j0, lc), :], 0, 1)
            dst[pl.ds(j0, lc), b * TILE : (b + 1) * TILE, :] = t

    incoming(c0)

    def prepare(wide, m):
        f = factors(strips(mid, wide), strips(mask, wide), wf[1])
        for q, v in enumerate(f):
            saved[q, :m] = jnp.broadcast_to(v, (m, c))

    def early(wide, m):
        prepare(wide, m)
        if wide:
            transposed(in_left, left_t, c0)
            transposed(in_right, right_t, c0)

    each(early, my_col == 0)

    incoming(o0, e_in_left)

    others = pl.ds(0, (rows - 1) * lr)
    e_ct = pltpu.make_async_remote_copy(
        src_ref=ct_h.at[others],
        dst_ref=ct_h.at[others],
        send_sem=ct_send.at[0],
        recv_sem=ct_recv.at[0],
        device_id={"col": other},
        device_id_type=MESH,
    )
    e_ct.wait_recv()
    own[1].wait()

    def signal(i0):
        z, r = norm(block(in_mixed, i0, lc))
        ct = ct_h[pl.ds(i0, lc)].reshape(lc * lc, c).astype(F32)
        put(ct32, i0, lc, ct)
        dz = rounded(dot_t(ct * block(in_gate, i0, lc), wo[1]))
        put_half(sig, i0, lc, rounded(norm_back(z, r, dz)))

    signal(o0)
    e_sig = partner(2, 4, half(sig, o0, lc))
    e_sig.start()
    e_in_right.wait_recv()

    def turn_signal(j0):
        for b in range(lc // TILE):
            t = jnp.swapaxes(sig[pl.ds(c0 + b * TILE, TILE), pl.ds(j0, lc), :], 0, 1)
            flip_s[:, b * TILE : (b + 1) * TILE, :] = t

    def left_row(j0, acc):
        return triangle(
            lr, lc, 0, lc,
            lambda a, q: in_right[r0 + a, pl.ds(j0 + q, 1), :],
            lambda q: flip_s[q],
            acc,
        )

    def left_col(j0, acc):
        return triangle(
            lr, n, 0, lc,
            lambda a, q: sig[r0 + a, pl.ds(j0 + q, 1), :],
            lambda q: right_t[j0 + q],
            acc,
        )

    def keep(ref, start, width, acc, fix=lambda v: v):
        for a in range(lr):
            ref[start + a * width : start + (a + 1) * width] = fix(acc[a])

    def kept(ref, start, width):
        return [ref[start + a * width : start + (a + 1) * width] for a in range(lr)]

    def window(late):
        def step(wide, m):
            signal(c0)
            z1, _ = norm(strips(in_mixed, wide))
            u1 = dot(z1, wo[1])
            if late:
                prepare(wide, m)
            elif wide:
                transposed(in_left, left_t, o0)
                transposed(in_right, right_t, o0)
            turn_signal(c0)
            keep(d_right, 0, lc, triangle(
                lr, lc, 0, n,
                lambda a, q: in_left[r0 + a, pl.ds(q, 1), :],
                lambda q: sig[q, pl.ds(c0, lc), :],
            ), rounded)
            keep(d_left, 0, lc, left_row(c0, None))
            if wide:
                if late:
                    for j0 in (c0, o0):
                        transposed(in_left, left_t, j0)
                        transposed(in_right, right_t, j0)
                keep(d_right, nr, n, triangle(
                    lr, n, 0, n,
                    lambda a, q: sig[q, pl.ds(r0 + a, 1), :],
                    lambda q: left_t[q],
                ), rounded)
                keep(d_left, nr, n, left_col(c0, None))
            saved[7, :m] = strips(ct32, wide) * u1

        return step

    each(window(False), my_col == 0)
    each(window(True), my_col == 1)
    e_sig.wait_recv()

    def back(wide, m):
        turn_signal(o0)
        keep(d_left, 0, lc, left_row(o0, kept(d_left, 0, lc)), rounded)
        if wide:
            keep(d_left, nr, n, left_col(o0, kept(d_left, nr, n)), rounded)
        f = tuple(saved[q, :m] for q in range(7))
        g = rounded(strips(ct32, wide) + front_back(f, wf[1], d_left[:m], d_right[:m], saved[7, :m]))
        z0, r = norm(strips(mixed, wide))
        dz = rounded(dot_t(g * strips(gate, wide), wo[0]))
        s = rounded(norm_back(z0, r, dz))
        along_row = s[:nr].reshape(lr, lc, c)
        sig_row[:, pl.ds(c0, lc), :] = along_row
        saved[8, :nr] = g[:nr]
        if wide:
            sig_col[...] = s[nr:].reshape(lr, n, c)

    each(back)
    e_row = partner(3, 5, sig_row.at[:, pl.ds(c0, lc)])
    e_row.start()
    e_col = partner(4, 6, sig_col)

    @pl.when(owner)
    def _():
        e_col.start()

    x = x_h[pl.ds(r0, lr)].reshape(nr, c).astype(F32)
    f = factors(x, row_of(mask), wf[0])
    z0, _ = norm(row_of(mixed))
    g = saved[8, :nr]
    d_gate = g * dot(z0, wo[0])

    def out_left(j0, acc):
        return triangle(
            lr, lc, 0, lc,
            lambda a, q: sig_row[a, pl.ds(j0 + q, 1), :],
            lambda q: right[j0 + q, pl.ds(c0, lc), :],
            acc,
        )

    acc = out_left(c0, None)
    e_row.wait_recv()
    d_a = jnp.concatenate([rounded(v) for v in out_left(o0, acc)], axis=0)

    @pl.when(jnp.logical_not(owner))
    def _():
        e_col.wait_recv()

    d_b = jnp.concatenate([rounded(v) for v in triangle(
        lr, lc, 0, n,
        lambda a, q: sig_col[a, pl.ds(q, 1), :],
        lambda q: left[q, pl.ds(c0, lc), :],
    )], axis=0)
    out[...] = (g + front_back(f, wf[0], d_a, d_b, d_gate)).astype(BF16).reshape(lr, lc, c)

    higher(drain)
    e_ct.wait_send()
    pair_bytes(0, lambda copy: copy.wait_send())

    @pl.when(wide_row)
    def _():
        far_copy().wait_send()

    for copy in (partner(1, 3, in_left), e_sig, e_row):
        copy.wait_send()

    @pl.when(owner)
    def _():
        e_col.wait_send()


def from_root(array, axis, root):
    mine = lax.axis_index(axis) == root
    return lax.psum(jnp.where(mine, array, jnp.zeros_like(array)), axis)


def layer_norm(values):
    centred = values - jnp.mean(values, axis=-1, keepdims=True)
    spread = jnp.mean(centred * centred, axis=-1, keepdims=True)
    return centred * lax.rsqrt(spread + 1e-05)


def project_pair(inner_pair, mask_pair, weight):
    normed = layer_norm(inner_pair.astype(jnp.float32)).astype(jnp.bfloat16)
    linear = jnp.dot(normed, weight, preferred_element_type=jnp.float32)
    left_side = jax.nn.sigmoid(linear[..., :H]) * linear[..., H : 2 * H]
    right_side = jax.nn.sigmoid(linear[..., 2 * H : 3 * H]) * linear[..., 3 * H : 4 * H]
    operands = (jnp.stack((left_side, right_side)) * mask_pair[None, :, :, None]).astype(
        jnp.bfloat16
    )
    return (operands, jax.nn.sigmoid(linear[..., 4 * H :]))


def finish(mixed_part, gate_value, inner_pair, weight):
    normed = layer_norm(mixed_part).astype(jnp.bfloat16)
    update = jnp.dot(normed, weight, preferred_element_type=jnp.float32)
    return (inner_pair.astype(jnp.float32) + gate_value * update).astype(jnp.bfloat16)


def body(pair_act, cotangent, residue_mask, front_weight, out_weight):
    local_rows = pair_act.shape[0]
    local_cols = pair_act.shape[1]
    row_index = lax.axis_index("row")
    col_index = lax.axis_index("col")
    block_rows = lax.axis_size("row") // lax.axis_size("col")
    owner_col = row_index // block_rows
    offset = row_index % block_rows * local_rows
    chain_mask = residue_mask.astype(jnp.float32)
    mask_rows = lax.dynamic_slice_in_dim(chain_mask, row_index * local_rows, local_rows)
    mask_cols = lax.dynamic_slice_in_dim(chain_mask, col_index * local_cols, local_cols)
    mask_pair = mask_rows[:, None] * mask_cols[None, :]

    def gather_rows(stacked):
        return lax.all_gather(stacked, "row", axis=1, tiled=True)

    def column_block(gathered):
        slab = lax.dynamic_slice_in_dim(gathered, offset, local_rows, 1)
        return from_root(slab, "col", owner_col)

    def gather_cols(values):
        return lax.all_gather(values, "col", axis=1, tiled=True)

    def sum_cols(partial_term):
        return lax.psum_scatter(
            partial_term.astype(jnp.bfloat16), "col", scatter_dimension=1, tiled=True
        ).astype(jnp.float32)

    (out_ops, out_gate), out_front_back = jax.vjp(
        lambda inner_pair: project_pair(inner_pair, mask_pair, front_weight[0]), pair_act
    )
    fetched = gather_rows(out_ops)
    out_mixed = sum_cols(
        jnp.einsum("ikc,jkc->ijc", out_ops[0], fetched[-1], preferred_element_type=jnp.float32)
    )
    pair_mid, out_finish_back = jax.vjp(
        lambda mixed_part, gate_value, inner_pair: finish(
            mixed_part, gate_value, inner_pair, out_weight[0]
        ),
        out_mixed,
        out_gate,
        pair_act,
    )
    (in_ops, in_gate), in_front_back = jax.vjp(
        lambda inner_pair: project_pair(inner_pair, mask_pair, front_weight[1]), pair_mid
    )
    in_fetched = gather_rows(in_ops)
    left_block = column_block(in_fetched[0])
    in_mixed = jnp.einsum(
        "kic,kjc->ijc", left_block, in_fetched[1], preferred_element_type=jnp.float32
    )
    unused_pair, in_finish_back = jax.vjp(
        lambda mixed_part, gate_value, inner_pair: finish(
            mixed_part, gate_value, inner_pair, out_weight[1]
        ),
        in_mixed,
        in_gate,
        pair_mid,
    )
    grad_mixed, grad_gate, grad_inner = in_finish_back(cotangent)
    signal = grad_mixed.astype(jnp.bfloat16)
    signal_rows = gather_rows(signal[None])[0]
    left_rows = gather_cols(in_ops[0])
    grad_right = jnp.einsum(
        "kic,ijc->kjc", left_rows, signal_rows, preferred_element_type=jnp.float32
    )
    grad_left = sum_cols(
        jnp.einsum("kjc,ijc->kic", in_ops[1], signal_rows, preferred_element_type=jnp.float32)
    )
    (grad_front,) = in_front_back(
        (jnp.stack((grad_left, grad_right)).astype(jnp.bfloat16), grad_gate)
    )
    grad_mid = (grad_inner.astype(jnp.float32) + grad_front.astype(jnp.float32)).astype(
        jnp.bfloat16
    )
    grad_mixed, grad_gate, grad_inner = out_finish_back(grad_mid)
    signal = grad_mixed.astype(jnp.bfloat16)
    signal_cols = gather_cols(signal)
    grad_left = jnp.einsum(
        "ijc,jkc->ikc", signal_cols, fetched[-1], preferred_element_type=jnp.float32
    )
    signal_block = column_block(gather_rows(signal[None])[0])
    grad_right = jnp.einsum(
        "ijc,ikc->jkc", signal_block, fetched[0], preferred_element_type=jnp.float32
    )
    (grad_front,) = out_front_back(
        (jnp.stack((grad_left, grad_right)).astype(jnp.bfloat16), grad_gate)
    )
    return (grad_inner.astype(jnp.float32) + grad_front.astype(jnp.float32)).astype(jnp.bfloat16)


def crop_body(rows, pair_act, cotangent, residue_mask, front_weight, out_weight):
    lr, lc, c = pair_act.shape
    n = residue_mask.shape[0]
    strip = lr * lc + lr * n
    dma = pltpu.SemaphoreType.DMA
    operands = (pair_act, cotangent, residue_mask.reshape(1, n), front_weight, out_weight)
    return pl.pallas_call(
        functools.partial(crop_kernel, rows),
        out_shape=jax.ShapeDtypeStruct((lr, lc, c), BF16),
        in_specs=[pl.BlockSpec(memory_space=pl.ANY)] * 5,
        out_specs=pl.BlockSpec(memory_space=pltpu.VMEM),
        scratch_shapes=[
            pltpu.VMEM((n, lc, c), BF16),
            pltpu.VMEM((n, lc, c), BF16),
            pltpu.VMEM((2 * lr, lc, c), BF16),
            pltpu.VMEM(front_weight.shape, BF16),
            pltpu.VMEM(out_weight.shape, BF16),
            pltpu.VMEM((1, n), jnp.int32),
        ]
        + [pltpu.VMEM((n, n, c), F32)] * 7
        + [pltpu.VMEM((lc, lc, c), F32)] * 2
        + [pltpu.VMEM((n * lc, c), F32)] * 7
        + [
            pltpu.VMEM((n * lc, c), BF16),
            pltpu.VMEM((n, c), F32),
            pltpu.VMEM((9, strip, c), F32),
            pltpu.VMEM((strip, c), F32),
            pltpu.VMEM((strip, c), F32),
            pltpu.VMEM((lr, n, c), F32),
            pltpu.VMEM((lr, n, c), F32),
        ]
        + [dma((5,)), dma((rows,)), dma((rows,)), dma((1,)), dma((1,)), dma((5,)), dma((7,))]
        + [pltpu.SemaphoreType.REGULAR((rows + 1,)), dma((1,)), dma((2,))],
        compiler_params=pltpu.CompilerParams(
            collective_id=0, has_side_effects=True, vmem_limit_bytes=VMEM_BUDGET
        ),
    )(*[pltpu.with_memory_space_constraint(v, pltpu.HBM) for v in operands])


def fits(mesh, n, lr, lc, c):
    rows, cols = mesh.shape["row"], mesh.shape["col"]
    return (
        cols == 2
        and rows >= 2
        and rows & (rows - 1) == 0
        and n == 2 * lc
        and lc == 2 * TILE
        and lc % (2 * lr) == 0
        and FULL_ARRAYS * 4 * n * n * c <= VMEM_BUDGET
    )


def solution(mesh):
    def dispatch(pair_act, cotangent, residue_mask, front_weight, out_weight):
        n = residue_mask.shape[0]
        if fits(mesh, n, *pair_act.shape):
            return crop_body(
                mesh.shape["row"], pair_act, cotangent, residue_mask, front_weight, out_weight
            )
        return body(pair_act, cotangent, residue_mask, front_weight, out_weight)

    placed = (P(("grp", "row"), "col", None), P(("grp", "row"), "col", None), P("grp"), P(), P())
    return jax.shard_map(
        dispatch,
        mesh=mesh,
        in_specs=placed,
        out_specs=P(("grp", "row"), "col", None),
        check_vma=False,
    )
```

```python
import functools

import jax
import jax.numpy as jnp
from jax import lax
from jax.experimental import pallas as pl
from jax.experimental.pallas import tpu as pltpu
from jax.sharding import PartitionSpec as P

H = 128
TILE = 8
F32 = jnp.float32
BF16 = jnp.bfloat16
MESH = pl.DeviceIdType.MESH
VMEM_BUDGET = 24 << 20
FULL_ARRAYS = 16


def sigmoid(x):
    return 0.5 * jnp.tanh(0.5 * x) + 0.5


def norm(v):
    centred = v - jnp.mean(v, axis=-1, keepdims=True)
    r = lax.rsqrt(jnp.mean(centred * centred, axis=-1, keepdims=True) + 1e-05)
    return centred * r, r


def scales(v):
    mean = jnp.mean(v, axis=-1, keepdims=True)
    centred = v - mean
    r = lax.rsqrt(jnp.mean(centred * centred, axis=-1, keepdims=True) + 1e-05)
    return r, r * mean


def column_sums(w):
    return jnp.sum(w.astype(F32), axis=0, keepdims=True)


def norm_back(y, r, d):
    return r * (d - jnp.mean(d, axis=-1, keepdims=True) - y * jnp.mean(d * y, axis=-1, keepdims=True))


def rounded(v):
    return v.astype(BF16).astype(F32)


def dot(a, b):
    return jnp.dot(a.astype(BF16), b, preferred_element_type=F32)


def dot_t(a, b):
    return lax.dot_general(
        a.astype(BF16), b, (((1,), (1,)), ((), ())), preferred_element_type=F32
    )


def part(p, n):
    return p[:, n * H : (n + 1) * H]


def factors(x, mask, weight):
    y, r = norm(x)
    p = dot(y, weight)
    s0, s2, s4 = sigmoid(part(p, 0)), sigmoid(part(p, 2)), sigmoid(part(p, 4))
    fa, fb = mask * s0, mask * s2
    return y, r, fa * part(p, 1) * (1.0 - s0), fa, fb * part(p, 3) * (1.0 - s2), fb, s4 * (1.0 - s4)


def front_back(f, weight, d_a, d_b, d_gate):
    y, r, f0, f1, f2, f3, f4 = f
    d = jnp.concatenate(
        [(v.astype(BF16)) for v in (d_a * f0, d_a * f1, d_b * f2, d_b * f3, d_gate * f4)], axis=1
    )
    return rounded(norm_back(y, r, rounded(dot_t(d, weight))))


def crop_kernel(
    rows, pair, cot, mask_in, wf_in, wo_in, out,
    x_h, ct_h, x_far, wf, wo, chain,
    left, right, in_left, in_right, sig, left_t, right_t, flip_r, flip_s,
    mask, mixed, gate, mid, in_mixed, in_gate, ct32, normed, along,
    saved, d_left, d_right, sig_row, sig_col, sig_out, sig_got,
    local_sem, x_send, x_recv, ct_send, ct_recv, psend, precv, ready, far_send, far_recv,
):
    n, c = left.shape[0], left.shape[2]
    lr, lc = out.shape[0], out.shape[1]
    bits = rows.bit_length() - 1
    me, my_col = lax.axis_index("row"), lax.axis_index("col")
    other = 1 - my_col
    me_bits = [lax.rem(lax.div(me, 1 << b), 2) for b in range(bits)]

    def flip(d, low=0):
        total = 0
        for b in range(low, bits):
            bit = me_bits[b]
            total = total + (1 - bit if d >> b & 1 else bit) * (1 << b)
        return total

    far = rows - 2 if rows > 4 else rows
    wide_row = jnp.logical_and(me >= far, my_col == 0)
    near_row = jnp.logical_and(me == 0, rows > 4)
    barrier = pltpu.get_barrier_semaphore()
    pl.semaphore_signal(barrier, inc=1, device_id={"col": other}, device_id_type=MESH)
    for row in range(1, rows):
        @pl.when(jnp.logical_and(me < row, me != row - 1) if row == far else me < row)
        def _():
            pl.semaphore_signal(barrier, inc=1, device_id={"row": row}, device_id_type=MESH)

    for row in range(far, rows):
        @pl.when(jnp.logical_and(me == 0, my_col == 1))
        def _():
            pl.semaphore_signal(
                barrier, inc=1, device_id={"row": row, "col": 0}, device_id_type=MESH
            )

    r0 = pl.multiple_of(me * lr, lr)
    c0 = pl.multiple_of(my_col * lc, lc)
    o0 = pl.multiple_of(other * lc, lc)
    jl = lax.rem(me * lr, lc)
    owner = lax.div(me * lr, lc) == my_col

    own = [
        pltpu.make_async_copy(src, dst.at[pl.ds(r0, lr)], local_sem.at[t])
        for t, (src, dst) in enumerate(((pair, x_h), (cot, ct_h)))
    ]
    weights = [
        pltpu.make_async_copy(wf_in, wf, local_sem.at[2]),
        pltpu.make_async_copy(wo_in, wo, local_sem.at[3]),
    ]
    chain_copy = pltpu.make_async_copy(mask_in, chain, local_sem.at[4])
    for copy in [chain_copy, own[0]] + weights + [own[1]]:
        copy.start()

    def direct(t, row, mine=None):
        src, dst = ((pair, x_h), (cot, ct_h))[t]
        source = row if mine is None else mine
        return pltpu.make_async_remote_copy(
            src_ref=src,
            dst_ref=dst.at[pl.ds(pl.multiple_of(source * lr, lr), lr)],
            send_sem=x_send.at[row] if t == 0 else ct_send.at[0],
            recv_sem=x_recv.at[source] if t == 0 else ct_recv.at[0],
            device_id={"row": row},
            device_id_type=MESH,
        )

    def lower(step, start=0):
        for row in range(start, rows - 1):
            @pl.when(jnp.logical_and(row < me, me != far) if row == far - 1 else row < me)
            def _():
                step(row)

    def higher(step):
        for row in range(1, rows):
            @pl.when(jnp.logical_or(row > me, me == far) if row == far - 1 else row > me)
            def _():
                step(row)

    def far_copy():
        at = pl.ds(pl.multiple_of((me - far) * lr, lr), lr)
        return pltpu.make_async_remote_copy(
            src_ref=pair,
            dst_ref=x_far.at[at],
            send_sem=far_send.at[0],
            recv_sem=far_recv.at[me - far],
            device_id={"row": 0, "col": 1},
            device_id_type=MESH,
        )

    def answer(row):
        if row == 0:
            @pl.when(jnp.logical_not(wide_row))
            def _():
                direct(0, row, me).start()
        elif row < 2:
            direct(0, row, me).start()
        pl.semaphore_signal(ready.at[me], inc=1, device_id={"row": row}, device_id_type=MESH)

    def send(row):
        if row >= 2:
            direct(0, row, me).start()

    def tell(row, about):
        pl.semaphore_signal(ready.at[about], inc=1, device_id={"row": row}, device_id_type=MESH)

    def follow(row):
        pl.semaphore_wait(ready.at[row], 1)
        direct(0, row, me).start()
        if row == far:
            @pl.when(me == far - 2)
            def _():
                tell(far, far - 1)
                tell(far - 1, far)

    def drain(row):
        direct(0, row, me).wait_send()

    def second(row):
        direct(1, row, me).start()

    def partner(q, r, ref):
        return pltpu.make_async_remote_copy(
            src_ref=ref,
            dst_ref=ref,
            send_sem=psend.at[q],
            recv_sem=precv.at[r],
            device_id={"col": other},
            device_id_type=MESH,
        )

    greeted = me + 1 - jnp.where(me == far, 1, 0)
    pl.semaphore_wait(barrier, greeted + jnp.where(wide_row, 1, 0))

    @pl.when(wide_row)
    def _():
        direct(0, 0, me).start()
        far_copy().start()

    lower(answer)

    chain_copy.wait()
    span = jnp.broadcast_to(chain[...].astype(F32), (n, n))
    here = lax.broadcasted_iota(jnp.int32, (n, n), 0) == lax.broadcasted_iota(jnp.int32, (n, n), 1)
    along[...] = jnp.broadcast_to(
        jnp.sum(jnp.where(here, span, 0.0), axis=1, keepdims=True), (n, c)
    )
    across = along[pl.ds(c0, lc), :]
    for i in range(n):
        mask[i * lc : (i + 1) * lc] = across * along[i : i + 1]
    lower(send)

    def block(ref, k0, nk):
        return ref[pl.ds(pl.multiple_of(k0 * lc, lc), nk * lc), :]

    def put(ref, k0, nk, v):
        ref[pl.ds(pl.multiple_of(k0 * lc, lc), nk * lc), :] = v

    def put_half(ref, k0, nk, v):
        ref[pl.ds(k0, nk), pl.ds(c0, lc), :] = v.reshape(nk, lc, c)

    def half(ref, k0, nk):
        return ref.at[pl.ds(k0, nk), pl.ds(c0, lc)]

    def projected(x, segments, weight, sums, a_ref, b_ref, g_ref):
        r, rm = scales(x.astype(F32))
        p = dot(x, weight)

        def part(p, q):
            return p[:, q * H : (q + 1) * H] * r - rm * sums[:, q * H : (q + 1) * H]

        m = jnp.concatenate([block(mask, k0, nk) for k0, nk in segments], axis=0)
        a = rounded(sigmoid(part(p, 0)) * part(p, 1) * m)
        b = rounded(sigmoid(part(p, 2)) * part(p, 3) * m)
        g = sigmoid(part(p, 4))
        at = 0
        for k0, nk in segments:
            span = slice(at * lc, (at + nk) * lc)
            put_half(a_ref, k0, nk, a[span])
            put_half(b_ref, k0, nk, b[span])
            put(g_ref, k0, nk, g[span])
            at += nk

    def triangle(count, width, first, depth, row_at, tile_at, acc=None):
        def term(q, acc):
            t = tile_at(first + q)
            return tuple(v + row_at(a, first + q) * t for a, v in enumerate(acc))

        if acc is None:
            acc = (jnp.zeros((width, c), F32),) * count
        return lax.fori_loop(0, depth, term, tuple(acc), unroll=True)

    def loop(count, step):
        def body(k, carry):
            step(k)
            return carry

        lax.fori_loop(0, count, body, 0)

    for copy in weights:
        copy.wait()
    sums_out, sums_in, sums_mix = (column_sums(w) for w in (wf[0], wf[1], wo[0]))
    groups = [[(0, 1)], [(1, 1), (2, 2)] if rows > 2 else [(1, 1)]]
    groups += [[(d, 2)] for d in range(4, rows, 2)]
    for g, group in enumerate(groups):
        for d, count in group:
            for q in range(d, d + count):
                if q == 0:
                    own[0].wait()
                else:
                    direct(0, flip(q)).wait_recv()
        segments = [
            (pl.multiple_of(flip(d, count.bit_length() - 1) * lr, count * lr), count * lr)
            for d, count in group
        ]
        x = jnp.concatenate(
            [x_h[pl.ds(k0, nk)].reshape(nk * lc, c) for k0, nk in segments], axis=0
        )
        projected(x, segments, wf[0], sums_out, left, right, gate)
        def exchange():
            for k0, nk in segments:
                partner(0, 0, half(left, k0, nk)).start()
                partner(0, 0, half(right, k0, nk)).start()

        if g == len(groups) - 1 and rows > 4:
            pl.when(jnp.logical_not(jnp.logical_and(near_row, my_col == 0)))(exchange)
        else:
            exchange()
        if g == 0:
            higher(follow)

            @pl.when(me > 0)
            def _():
                second(0)

            lower(drain)
            pl.semaphore_signal(
                ready.at[rows], inc=1, device_id={"col": other}, device_id_type=MESH
            )
            pl.semaphore_wait(ready.at[rows], 1)
            lower(second, 1)
        if g == len(groups) - 1:
            higher(second)

    group = TILE

    def outgoing(k0, fresh):
        for b in range(lc // TILE):
            t = jnp.swapaxes(right[pl.ds(c0 + b * TILE, TILE), pl.ds(k0, lc), :], 0, 1)
            flip_r[:, b * TILE : (b + 1) * TILE, :] = t

        def step(b):
            i0 = b * group
            base = pl.multiple_of(i0 * lc, lc * group)
            acc = None
            if not fresh:
                acc = [mixed[pl.ds(base + a * lc, lc), :] for a in range(group)]
            acc = triangle(
                group, lc, 0, lc,
                lambda a, q: left[i0 + a, pl.ds(k0 + q, 1), :],
                lambda q: flip_r[q],
                acc,
            )
            for a in range(group):
                mixed[pl.ds(base + a * lc, lc), :] = acc[a]

        loop(n // group, step)

    outgoing(c0, True)

    @pl.when(jnp.logical_and(near_row, my_col == 1))
    def _():
        for q in range(2):
            pltpu.make_async_remote_copy(
                src_ref=pair,
                dst_ref=x_far.at[pl.ds(q * lr, lr)],
                send_sem=far_send.at[0],
                recv_sem=far_recv.at[q],
                device_id={"row": 0, "col": 0},
                device_id_type=MESH,
            ).wait_recv()
        x = x_far[...].reshape(2 * lr * lc, c)
        r, rm = scales(x.astype(F32))
        p = dot(x, wf[0, :, : 4 * H])

        def scaled(q):
            return part(p, q) * r - rm * part(sums_out, q)

        k0 = far * lr
        over = along[pl.ds(o0, lc), :]
        m = jnp.concatenate([over * along[k0 + i : k0 + i + 1] for i in range(2 * lr)], axis=0)
        a = rounded(sigmoid(scaled(0)) * scaled(1) * m)
        b = rounded(sigmoid(scaled(2)) * scaled(3) * m)
        left[k0:, pl.ds(o0, lc), :] = a.reshape(2 * lr, lc, c)
        right[k0:, pl.ds(o0, lc), :] = b.reshape(2 * lr, lc, c)

    def pair_bytes(column, step):
        @pl.when(jnp.logical_and(near_row, my_col == column))
        def _():
            step(partner(0, 0, left.at[pl.ds(0, far * lr)]))

        @pl.when(jnp.logical_not(jnp.logical_and(near_row, my_col == column)))
        def _():
            step(partner(0, 0, left))

    pair_bytes(1, lambda copy: copy.wait_recv())
    outgoing(o0, False)

    v = mixed[...]
    r, rm = scales(v)
    high = v.astype(BF16)
    low = (v - high.astype(F32)).astype(BF16)
    update = dot(
        jnp.concatenate([high, low], axis=1), jnp.concatenate([wo[0], wo[0]], axis=0)
    )
    x = x_h[...].reshape(n * lc, c).astype(F32)
    x = rounded(x + gate[...] * (update * r - rm * sums_mix))
    mid[...] = x
    r, rm = scales(x)

    def scaled(p, q, at):
        return part(p, q) * r - rm * part(sums_in, at + q)

    x = x.astype(BF16)
    normed[...] = x
    p = dot(x, wf[1, :, : 2 * H])
    put_half(in_left, 0, n, rounded(sigmoid(scaled(p, 0, 0)) * scaled(p, 1, 0) * mask[...]))
    e_in_left = [
        partner(1, 1 + b, in_left.at[:, pl.ds(c0 + b * TILE, TILE)]) for b in range(lc // TILE)
    ]
    for copy in e_in_left:
        copy.start()
    p = dot(normed[...], wf[1, :, 2 * H :])
    v = rounded(sigmoid(scaled(p, 0, 2)) * scaled(p, 1, 2) * mask[...])
    put_half(in_right, 0, n, v)
    in_gate[...] = sigmoid(scaled(p, 2, 2))
    e_in_right = partner(1, 3, half(in_right, 0, n))
    e_in_right.start()

    def incoming(i0, copies=()):
        few = 4

        def step(i1):
            acc = triangle(
                few, lc, 0, n,
                lambda a, q: in_left[q, pl.ds(i1 + a, 1), :],
                lambda q: in_right[q, pl.ds(c0, lc), :],
            )
            for a in range(few):
                in_mixed[pl.ds(pl.multiple_of((i1 + a) * lc, lc), lc), :] = acc[a]

        for b in range(lc // TILE):
            if copies:
                copies[b].wait_recv()
            for a in range(0, TILE, few):
                step(pl.multiple_of(i0 + b * TILE, TILE) + a)

    nr, nc = lr * lc, lr * n

    def row_of(ref):
        return ref[pl.ds(pl.multiple_of(r0 * lc, lc), nr), :]

    def col_of(ref):
        return jnp.concatenate([ref[pl.ds(jl + a, n, stride=lc), :] for a in range(lr)], axis=0)

    def strips(ref, wide):
        return jnp.concatenate([row_of(ref), col_of(ref)], axis=0) if wide else row_of(ref)

    def each(step, here=True):
        @pl.when(jnp.logical_and(here, owner))
        def _():
            step(True, nr + nc)

        @pl.when(jnp.logical_and(here, jnp.logical_not(owner)))
        def _():
            step(False, nr)

    def transposed(src, dst, j0):
        for b in range(n // TILE):
            t = jnp.swapaxes(src[b * TILE : (b + 1) * TILE, pl.ds(j0, lc), :], 0, 1)
            dst[pl.ds(j0, lc), b * TILE : (b + 1) * TILE, :] = t

    incoming(c0)

    def prepare(wide, m):
        f = factors(strips(mid, wide), strips(mask, wide), wf[1])
        for q, v in enumerate(f):
            saved[q, :m] = jnp.broadcast_to(v, (m, c))

    def early(wide, m):
        prepare(wide, m)
        if wide:
            transposed(in_left, left_t, c0)
            transposed(in_right, right_t, c0)

    each(early, my_col == 0)

    incoming(o0, e_in_left)

    others = pl.ds(0, (rows - 1) * lr)
    e_ct = pltpu.make_async_remote_copy(
        src_ref=ct_h.at[others],
        dst_ref=ct_h.at[others],
        send_sem=ct_send.at[0],
        recv_sem=ct_recv.at[0],
        device_id={"col": other},
        device_id_type=MESH,
    )
    e_ct.wait_recv()
    own[1].wait()

    def signal(i0):
        z, r = norm(block(in_mixed, i0, lc))
        ct = ct_h[pl.ds(i0, lc)].reshape(lc * lc, c).astype(F32)
        put(ct32, i0, lc, ct)
        dz = rounded(dot_t(ct * block(in_gate, i0, lc), wo[1]))
        v = norm_back(z, r, dz).astype(BF16)
        put_half(sig, i0, lc, v.astype(F32))
        return v

    sig_out[...] = signal(o0).reshape(lc, lc, c)
    e_sig = pltpu.make_async_remote_copy(
        src_ref=sig_out,
        dst_ref=sig_got,
        send_sem=psend.at[2],
        recv_sem=precv.at[4],
        device_id={"col": other},
        device_id_type=MESH,
    )
    e_sig.start()
    e_in_right.wait_recv()

    def turn_signal(j0):
        for b in range(lc // TILE):
            t = jnp.swapaxes(sig[pl.ds(c0 + b * TILE, TILE), pl.ds(j0, lc), :], 0, 1)
            flip_s[:, b * TILE : (b + 1) * TILE, :] = t

    def left_row(j0, acc):
        return triangle(
            lr, lc, 0, lc,
            lambda a, q: in_right[r0 + a, pl.ds(j0 + q, 1), :],
            lambda q: flip_s[q],
            acc,
        )

    def left_col(j0, acc):
        return triangle(
            lr, n, 0, lc,
            lambda a, q: sig[r0 + a, pl.ds(j0 + q, 1), :],
            lambda q: right_t[j0 + q],
            acc,
        )

    def keep(ref, start, width, acc, fix=lambda v: v):
        for a in range(lr):
            ref[start + a * width : start + (a + 1) * width] = fix(acc[a])

    def kept(ref, start, width):
        return [ref[start + a * width : start + (a + 1) * width] for a in range(lr)]

    def window(late):
        def step(wide, m):
            signal(c0)
            z1, _ = norm(strips(in_mixed, wide))
            u1 = dot(z1, wo[1])
            if late:
                prepare(wide, m)
            elif wide:
                transposed(in_left, left_t, o0)
                transposed(in_right, right_t, o0)
            turn_signal(c0)
            keep(d_right, 0, lc, triangle(
                lr, lc, 0, n,
                lambda a, q: in_left[r0 + a, pl.ds(q, 1), :],
                lambda q: sig[q, pl.ds(c0, lc), :],
            ), rounded)
            keep(d_left, 0, lc, left_row(c0, None))
            if wide:
                if late:
                    for j0 in (c0, o0):
                        transposed(in_left, left_t, j0)
                        transposed(in_right, right_t, j0)
                keep(d_right, nr, n, triangle(
                    lr, n, 0, n,
                    lambda a, q: sig[q, pl.ds(r0 + a, 1), :],
                    lambda q: left_t[q],
                ), rounded)
                keep(d_left, nr, n, left_col(c0, None))
            saved[7, :m] = strips(ct32, wide) * u1

        return step

    each(window(False), my_col == 0)
    each(window(True), my_col == 1)
    e_sig.wait_recv()

    def back(wide, m):
        for b in range(lc // TILE):
            t = sig_got[b * TILE : (b + 1) * TILE].astype(F32)
            flip_s[:, b * TILE : (b + 1) * TILE, :] = jnp.swapaxes(t, 0, 1)
        keep(d_left, 0, lc, left_row(o0, kept(d_left, 0, lc)), rounded)
        if wide:
            sig[pl.ds(r0, lr), pl.ds(o0, lc), :] = sig_got[pl.ds(jl, lr)].astype(F32)
            keep(d_left, nr, n, left_col(o0, kept(d_left, nr, n)), rounded)
        f = tuple(saved[q, :m] for q in range(7))
        g = rounded(strips(ct32, wide) + front_back(f, wf[1], d_left[:m], d_right[:m], saved[7, :m]))
        z0, r = norm(strips(mixed, wide))
        dz = rounded(dot_t(g * strips(gate, wide), wo[0]))
        s = rounded(norm_back(z0, r, dz))
        along_row = s[:nr].reshape(lr, lc, c)
        sig_row[:, pl.ds(c0, lc), :] = along_row
        saved[8, :nr] = g[:nr]
        if wide:
            sig_col[...] = s[nr:].reshape(lr, n, c)

    each(back)
    e_row = partner(3, 5, sig_row.at[:, pl.ds(c0, lc)])
    e_row.start()
    e_col = partner(4, 6, sig_col)

    @pl.when(owner)
    def _():
        e_col.start()

    x = x_h[pl.ds(r0, lr)].reshape(nr, c).astype(F32)
    f = factors(x, row_of(mask), wf[0])
    z0, _ = norm(row_of(mixed))
    g = saved[8, :nr]
    d_gate = g * dot(z0, wo[0])

    def out_left(j0, acc):
        return triangle(
            lr, lc, 0, lc,
            lambda a, q: sig_row[a, pl.ds(j0 + q, 1), :],
            lambda q: right[j0 + q, pl.ds(c0, lc), :],
            acc,
        )

    acc = out_left(c0, None)
    e_row.wait_recv()
    d_a = jnp.concatenate([rounded(v) for v in out_left(o0, acc)], axis=0)

    @pl.when(jnp.logical_not(owner))
    def _():
        e_col.wait_recv()

    d_b = jnp.concatenate([rounded(v) for v in triangle(
        lr, lc, 0, n,
        lambda a, q: sig_col[a, pl.ds(q, 1), :],
        lambda q: left[q, pl.ds(c0, lc), :],
    )], axis=0)
    out[...] = (g + front_back(f, wf[0], d_a, d_b, d_gate)).astype(BF16).reshape(lr, lc, c)

    higher(drain)
    e_ct.wait_send()
    pair_bytes(0, lambda copy: copy.wait_send())

    @pl.when(wide_row)
    def _():
        far_copy().wait_send()

    for copy in (partner(1, 3, in_left), e_sig, e_row):
        copy.wait_send()

    @pl.when(owner)
    def _():
        e_col.wait_send()


def from_root(array, axis, root):
    mine = lax.axis_index(axis) == root
    return lax.psum(jnp.where(mine, array, jnp.zeros_like(array)), axis)


def layer_norm(values):
    centred = values - jnp.mean(values, axis=-1, keepdims=True)
    spread = jnp.mean(centred * centred, axis=-1, keepdims=True)
    return centred * lax.rsqrt(spread + 1e-05)


def project_pair(inner_pair, mask_pair, weight):
    normed = layer_norm(inner_pair.astype(jnp.float32)).astype(jnp.bfloat16)
    linear = jnp.dot(normed, weight, preferred_element_type=jnp.float32)
    left_side = jax.nn.sigmoid(linear[..., :H]) * linear[..., H : 2 * H]
    right_side = jax.nn.sigmoid(linear[..., 2 * H : 3 * H]) * linear[..., 3 * H : 4 * H]
    operands = (jnp.stack((left_side, right_side)) * mask_pair[None, :, :, None]).astype(
        jnp.bfloat16
    )
    return (operands, jax.nn.sigmoid(linear[..., 4 * H :]))


def finish(mixed_part, gate_value, inner_pair, weight):
    normed = layer_norm(mixed_part).astype(jnp.bfloat16)
    update = jnp.dot(normed, weight, preferred_element_type=jnp.float32)
    return (inner_pair.astype(jnp.float32) + gate_value * update).astype(jnp.bfloat16)


def body(pair_act, cotangent, residue_mask, front_weight, out_weight):
    local_rows = pair_act.shape[0]
    local_cols = pair_act.shape[1]
    row_index = lax.axis_index("row")
    col_index = lax.axis_index("col")
    block_rows = lax.axis_size("row") // lax.axis_size("col")
    owner_col = row_index // block_rows
    offset = row_index % block_rows * local_rows
    chain_mask = residue_mask.astype(jnp.float32)
    mask_rows = lax.dynamic_slice_in_dim(chain_mask, row_index * local_rows, local_rows)
    mask_cols = lax.dynamic_slice_in_dim(chain_mask, col_index * local_cols, local_cols)
    mask_pair = mask_rows[:, None] * mask_cols[None, :]

    def gather_rows(stacked):
        return lax.all_gather(stacked, "row", axis=1, tiled=True)

    def column_block(gathered):
        slab = lax.dynamic_slice_in_dim(gathered, offset, local_rows, 1)
        return from_root(slab, "col", owner_col)

    def gather_cols(values):
        return lax.all_gather(values, "col", axis=1, tiled=True)

    def sum_cols(partial_term):
        return lax.psum_scatter(
            partial_term.astype(jnp.bfloat16), "col", scatter_dimension=1, tiled=True
        ).astype(jnp.float32)

    (out_ops, out_gate), out_front_back = jax.vjp(
        lambda inner_pair: project_pair(inner_pair, mask_pair, front_weight[0]), pair_act
    )
    fetched = gather_rows(out_ops)
    out_mixed = sum_cols(
        jnp.einsum("ikc,jkc->ijc", out_ops[0], fetched[-1], preferred_element_type=jnp.float32)
    )
    pair_mid, out_finish_back = jax.vjp(
        lambda mixed_part, gate_value, inner_pair: finish(
            mixed_part, gate_value, inner_pair, out_weight[0]
        ),
        out_mixed,
        out_gate,
        pair_act,
    )
    (in_ops, in_gate), in_front_back = jax.vjp(
        lambda inner_pair: project_pair(inner_pair, mask_pair, front_weight[1]), pair_mid
    )
    in_fetched = gather_rows(in_ops)
    left_block = column_block(in_fetched[0])
    in_mixed = jnp.einsum(
        "kic,kjc->ijc", left_block, in_fetched[1], preferred_element_type=jnp.float32
    )
    unused_pair, in_finish_back = jax.vjp(
        lambda mixed_part, gate_value, inner_pair: finish(
            mixed_part, gate_value, inner_pair, out_weight[1]
        ),
        in_mixed,
        in_gate,
        pair_mid,
    )
    grad_mixed, grad_gate, grad_inner = in_finish_back(cotangent)
    signal = grad_mixed.astype(jnp.bfloat16)
    signal_rows = gather_rows(signal[None])[0]
    left_rows = gather_cols(in_ops[0])
    grad_right = jnp.einsum(
        "kic,ijc->kjc", left_rows, signal_rows, preferred_element_type=jnp.float32
    )
    grad_left = sum_cols(
        jnp.einsum("kjc,ijc->kic", in_ops[1], signal_rows, preferred_element_type=jnp.float32)
    )
    (grad_front,) = in_front_back(
        (jnp.stack((grad_left, grad_right)).astype(jnp.bfloat16), grad_gate)
    )
    grad_mid = (grad_inner.astype(jnp.float32) + grad_front.astype(jnp.float32)).astype(
        jnp.bfloat16
    )
    grad_mixed, grad_gate, grad_inner = out_finish_back(grad_mid)
    signal = grad_mixed.astype(jnp.bfloat16)
    signal_cols = gather_cols(signal)
    grad_left = jnp.einsum(
        "ijc,jkc->ikc", signal_cols, fetched[-1], preferred_element_type=jnp.float32
    )
    signal_block = column_block(gather_rows(signal[None])[0])
    grad_right = jnp.einsum(
        "ijc,ikc->jkc", signal_block, fetched[0], preferred_element_type=jnp.float32
    )
    (grad_front,) = out_front_back(
        (jnp.stack((grad_left, grad_right)).astype(jnp.bfloat16), grad_gate)
    )
    return (grad_inner.astype(jnp.float32) + grad_front.astype(jnp.float32)).astype(jnp.bfloat16)


def crop_body(rows, pair_act, cotangent, residue_mask, front_weight, out_weight):
    lr, lc, c = pair_act.shape
    n = residue_mask.shape[0]
    strip = lr * lc + lr * n
    dma = pltpu.SemaphoreType.DMA
    operands = (pair_act, cotangent, residue_mask.reshape(1, n), front_weight, out_weight)
    return pl.pallas_call(
        functools.partial(crop_kernel, rows),
        out_shape=jax.ShapeDtypeStruct((lr, lc, c), BF16),
        in_specs=[pl.BlockSpec(memory_space=pl.ANY)] * 5,
        out_specs=pl.BlockSpec(memory_space=pltpu.VMEM),
        scratch_shapes=[
            pltpu.VMEM((n, lc, c), BF16),
            pltpu.VMEM((n, lc, c), BF16),
            pltpu.VMEM((2 * lr, lc, c), BF16),
            pltpu.VMEM(front_weight.shape, BF16),
            pltpu.VMEM(out_weight.shape, BF16),
            pltpu.VMEM((1, n), jnp.int32),
        ]
        + [pltpu.VMEM((n, n, c), F32)] * 7
        + [pltpu.VMEM((lc, lc, c), F32)] * 2
        + [pltpu.VMEM((n * lc, c), F32)] * 7
        + [
            pltpu.VMEM((n * lc, c), BF16),
            pltpu.VMEM((n, c), F32),
            pltpu.VMEM((9, strip, c), F32),
            pltpu.VMEM((strip, c), F32),
            pltpu.VMEM((strip, c), F32),
            pltpu.VMEM((lr, n, c), F32),
            pltpu.VMEM((lr, n, c), F32),
            pltpu.VMEM((lc, lc, c), BF16),
            pltpu.VMEM((lc, lc, c), BF16),
        ]
        + [dma((5,)), dma((rows,)), dma((rows,)), dma((1,)), dma((1,)), dma((5,)), dma((7,))]
        + [pltpu.SemaphoreType.REGULAR((rows + 1,)), dma((1,)), dma((2,))],
        compiler_params=pltpu.CompilerParams(
            collective_id=0, has_side_effects=True, vmem_limit_bytes=VMEM_BUDGET
        ),
    )(*[pltpu.with_memory_space_constraint(v, pltpu.HBM) for v in operands])


def fits(mesh, n, lr, lc, c):
    rows, cols = mesh.shape["row"], mesh.shape["col"]
    return (
        cols == 2
        and rows >= 2
        and rows & (rows - 1) == 0
        and n == 2 * lc
        and lc == 2 * TILE
        and lc % (2 * lr) == 0
        and FULL_ARRAYS * 4 * n * n * c <= VMEM_BUDGET
    )


def solution(mesh):
    def dispatch(pair_act, cotangent, residue_mask, front_weight, out_weight):
        n = residue_mask.shape[0]
        if fits(mesh, n, *pair_act.shape):
            return crop_body(
                mesh.shape["row"], pair_act, cotangent, residue_mask, front_weight, out_weight
            )
        return body(pair_act, cotangent, residue_mask, front_weight, out_weight)

    placed = (P(("grp", "row"), "col", None), P(("grp", "row"), "col", None), P("grp"), P(), P())
    return jax.shard_map(
        dispatch,
        mesh=mesh,
        in_specs=placed,
        out_specs=P(("grp", "row"), "col", None),
        check_vma=False,
    )
```

```python
import functools

import jax
import jax.numpy as jnp
from jax import lax
from jax.experimental import pallas as pl
from jax.experimental.pallas import tpu as pltpu
from jax.sharding import PartitionSpec as P

H = 128
TILE = 8
F32 = jnp.float32
BF16 = jnp.bfloat16
MESH = pl.DeviceIdType.MESH
VMEM_BUDGET = 24 << 20
FULL_ARRAYS = 16


def sigmoid(x):
    return 0.5 * jnp.tanh(0.5 * x) + 0.5


def norm(v):
    centred = v - jnp.mean(v, axis=-1, keepdims=True)
    r = lax.rsqrt(jnp.mean(centred * centred, axis=-1, keepdims=True) + 1e-05)
    return centred * r, r


def scales(v):
    mean = jnp.mean(v, axis=-1, keepdims=True)
    centred = v - mean
    r = lax.rsqrt(jnp.mean(centred * centred, axis=-1, keepdims=True) + 1e-05)
    return r, r * mean


def column_sums(w):
    return jnp.sum(w.astype(F32), axis=0, keepdims=True)


def norm_back(y, r, d):
    return r * (d - jnp.mean(d, axis=-1, keepdims=True) - y * jnp.mean(d * y, axis=-1, keepdims=True))


def rounded(v):
    return v.astype(BF16).astype(F32)


def dot(a, b):
    return jnp.dot(a.astype(BF16), b, preferred_element_type=F32)


def dot_t(a, b):
    return lax.dot_general(
        a.astype(BF16), b, (((1,), (1,)), ((), ())), preferred_element_type=F32
    )


def part(p, n):
    return p[:, n * H : (n + 1) * H]


def factors(x, mask, weight):
    y, r = norm(x)
    p = dot(y, weight)
    s0, s2, s4 = sigmoid(part(p, 0)), sigmoid(part(p, 2)), sigmoid(part(p, 4))
    fa, fb = mask * s0, mask * s2
    return y, r, fa * part(p, 1) * (1.0 - s0), fa, fb * part(p, 3) * (1.0 - s2), fb, s4 * (1.0 - s4)


def front_back(f, weight, d_a, d_b, d_gate):
    y, r, f0, f1, f2, f3, f4 = f
    d = jnp.concatenate(
        [(v.astype(BF16)) for v in (d_a * f0, d_a * f1, d_b * f2, d_b * f3, d_gate * f4)], axis=1
    )
    return rounded(norm_back(y, r, rounded(dot_t(d, weight))))


def crop_kernel(
    rows, pair, cot, mask_in, wf_in, wo_in, out,
    x_h, ct_h, x_far, wf, wo, chain,
    left, right, in_left, in_right, sig, left_t, right_t, flip_r, flip_s,
    mask, mixed, gate, mid, in_mixed, in_gate, ct32, normed, along,
    saved, d_left, d_right, sig_row, sig_col, sig_out, sig_got,
    local_sem, x_send, x_recv, ct_send, ct_recv, psend, precv, ready, far_send, far_recv,
):
    n, c = left.shape[0], left.shape[2]
    lr, lc = out.shape[0], out.shape[1]
    bits = rows.bit_length() - 1
    me, my_col = lax.axis_index("row"), lax.axis_index("col")
    other = 1 - my_col
    me_bits = [lax.rem(lax.div(me, 1 << b), 2) for b in range(bits)]

    def flip(d, low=0):
        total = 0
        for b in range(low, bits):
            bit = me_bits[b]
            total = total + (1 - bit if d >> b & 1 else bit) * (1 << b)
        return total

    far = rows - 2 if rows > 4 else rows
    wide_row = jnp.logical_and(me >= far, my_col == 0)
    near_row = jnp.logical_and(me == 0, rows > 4)
    barrier = pltpu.get_barrier_semaphore()
    pl.semaphore_signal(barrier, inc=1, device_id={"col": other}, device_id_type=MESH)
    for row in range(1, rows):
        @pl.when(jnp.logical_and(me < row, me != row - 1) if row == far else me < row)
        def _():
            pl.semaphore_signal(barrier, inc=1, device_id={"row": row}, device_id_type=MESH)

    for row in range(far, rows):
        @pl.when(jnp.logical_and(me == 0, my_col == 1))
        def _():
            pl.semaphore_signal(
                barrier, inc=1, device_id={"row": row, "col": 0}, device_id_type=MESH
            )

    r0 = pl.multiple_of(me * lr, lr)
    c0 = pl.multiple_of(my_col * lc, lc)
    o0 = pl.multiple_of(other * lc, lc)
    jl = lax.rem(me * lr, lc)
    owner = lax.div(me * lr, lc) == my_col

    own = [
        pltpu.make_async_copy(src, dst.at[pl.ds(r0, lr)], local_sem.at[t])
        for t, (src, dst) in enumerate(((pair, x_h), (cot, ct_h)))
    ]
    weights = [
        pltpu.make_async_copy(wf_in, wf, local_sem.at[2]),
        pltpu.make_async_copy(wo_in, wo, local_sem.at[3]),
    ]
    chain_copy = pltpu.make_async_copy(mask_in, chain, local_sem.at[4])
    for copy in [chain_copy, own[0]] + weights + [own[1]]:
        copy.start()

    def group_of(row):
        if not isinstance(row, int):
            return 0
        apart = 0
        for b in range(1, bits):
            apart = apart + (1 - me_bits[b] if row >> b & 1 else me_bits[b]) * (1 << b)
        return jnp.maximum(lax.div(apart, 2) - 1, 0)

    def direct(t, row, mine=None):
        src, dst = ((pair, x_h), (cot, ct_h))[t]
        source = row if mine is None else mine
        return pltpu.make_async_remote_copy(
            src_ref=src,
            dst_ref=dst.at[pl.ds(pl.multiple_of(source * lr, lr), lr)],
            send_sem=x_send.at[row] if t == 0 else ct_send.at[0],
            recv_sem=x_recv.at[group_of(row)] if t == 0 else ct_recv.at[0],
            device_id={"row": row},
            device_id_type=MESH,
        )

    def lower(step, start=0):
        for row in range(start, rows - 1):
            @pl.when(jnp.logical_and(row < me, me != far) if row == far - 1 else row < me)
            def _():
                step(row)

    def higher(step):
        for row in range(1, rows):
            @pl.when(jnp.logical_or(row > me, me == far) if row == far - 1 else row > me)
            def _():
                step(row)

    def far_copy():
        at = pl.ds(pl.multiple_of((me - far) * lr, lr), lr)
        return pltpu.make_async_remote_copy(
            src_ref=pair,
            dst_ref=x_far.at[at],
            send_sem=far_send.at[0],
            recv_sem=far_recv.at[me - far],
            device_id={"row": 0, "col": 1},
            device_id_type=MESH,
        )

    def answer(row):
        if row == 0:
            @pl.when(jnp.logical_not(wide_row))
            def _():
                direct(0, row, me).start()
        elif row < 2:
            direct(0, row, me).start()
        pl.semaphore_signal(ready.at[me], inc=1, device_id={"row": row}, device_id_type=MESH)

    def send(row):
        if row >= 2:
            direct(0, row, me).start()

    def tell(row, about):
        pl.semaphore_signal(ready.at[about], inc=1, device_id={"row": row}, device_id_type=MESH)

    def follow(row):
        pl.semaphore_wait(ready.at[row], 1)
        direct(0, row, me).start()
        if row == far:
            @pl.when(me == far - 2)
            def _():
                tell(far, far - 1)
                tell(far - 1, far)

    def drain(row):
        direct(0, row, me).wait_send()

    def second(row):
        direct(1, row, me).start()

    def partner(q, r, ref):
        return pltpu.make_async_remote_copy(
            src_ref=ref,
            dst_ref=ref,
            send_sem=psend.at[q],
            recv_sem=precv.at[r],
            device_id={"col": other},
            device_id_type=MESH,
        )

    greeted = me + 1 - jnp.where(me == far, 1, 0)
    pl.semaphore_wait(barrier, greeted + jnp.where(wide_row, 1, 0))

    @pl.when(wide_row)
    def _():
        direct(0, 0, me).start()
        far_copy().start()

    lower(answer)

    chain_copy.wait()
    span = jnp.broadcast_to(chain[...].astype(F32), (n, n))
    here = lax.broadcasted_iota(jnp.int32, (n, n), 0) == lax.broadcasted_iota(jnp.int32, (n, n), 1)
    along[...] = jnp.broadcast_to(
        jnp.sum(jnp.where(here, span, 0.0), axis=1, keepdims=True), (n, c)
    )
    across = along[pl.ds(c0, lc), :]
    for i in range(n):
        mask[i * lc : (i + 1) * lc] = across * along[i : i + 1]
    lower(send)

    def block(ref, k0, nk):
        return ref[pl.ds(pl.multiple_of(k0 * lc, lc), nk * lc), :]

    def put(ref, k0, nk, v):
        ref[pl.ds(pl.multiple_of(k0 * lc, lc), nk * lc), :] = v

    def put_half(ref, k0, nk, v):
        ref[pl.ds(k0, nk), pl.ds(c0, lc), :] = v.reshape(nk, lc, c)

    def half(ref, k0, nk):
        return ref.at[pl.ds(k0, nk), pl.ds(c0, lc)]

    def projected(x, segments, weight, sums, a_ref, b_ref, g_ref):
        r, rm = scales(x.astype(F32))
        p = dot(x, weight)

        def part(p, q):
            return p[:, q * H : (q + 1) * H] * r - rm * sums[:, q * H : (q + 1) * H]

        m = jnp.concatenate([block(mask, k0, nk) for k0, nk in segments], axis=0)
        a = rounded(sigmoid(part(p, 0)) * part(p, 1) * m)
        b = rounded(sigmoid(part(p, 2)) * part(p, 3) * m)
        g = sigmoid(part(p, 4))
        at = 0
        for k0, nk in segments:
            span = slice(at * lc, (at + nk) * lc)
            put_half(a_ref, k0, nk, a[span])
            put_half(b_ref, k0, nk, b[span])
            put(g_ref, k0, nk, g[span])
            at += nk

    def triangle(count, width, first, depth, row_at, tile_at, acc=None):
        def term(q, acc):
            t = tile_at(first + q)
            return tuple(v + row_at(a, first + q) * t for a, v in enumerate(acc))

        if acc is None:
            acc = (jnp.zeros((width, c), F32),) * count
        return lax.fori_loop(0, depth, term, tuple(acc), unroll=True)

    def loop(count, step):
        def body(k, carry):
            step(k)
            return carry

        lax.fori_loop(0, count, body, 0)

    for copy in weights:
        copy.wait()
    sums_out, sums_in, sums_mix = (column_sums(w) for w in (wf[0], wf[1], wo[0]))
    groups = [[(0, 1)], [(1, 1), (2, 2)] if rows > 2 else [(1, 1)]]
    groups += [[(d, 2)] for d in range(4, rows, 2)]
    for g, group in enumerate(groups):
        if g == 0:
            own[0].wait()
        else:
            here = x_h.at[pl.ds(0, sum(count for _, count in group) * lr)]
            pltpu.make_async_remote_copy(
                src_ref=here,
                dst_ref=here,
                send_sem=x_send.at[0],
                recv_sem=x_recv.at[g - 1],
                device_id={"col": other},
                device_id_type=MESH,
            ).wait_recv()
        segments = [
            (pl.multiple_of(flip(d, count.bit_length() - 1) * lr, count * lr), count * lr)
            for d, count in group
        ]
        x = jnp.concatenate(
            [x_h[pl.ds(k0, nk)].reshape(nk * lc, c) for k0, nk in segments], axis=0
        )
        projected(x, segments, wf[0], sums_out, left, right, gate)
        def exchange():
            for k0, nk in segments:
                partner(0, 0, half(left, k0, nk)).start()
                partner(0, 0, half(right, k0, nk)).start()

        if g == len(groups) - 1 and rows > 4:
            pl.when(jnp.logical_not(jnp.logical_and(near_row, my_col == 0)))(exchange)
        else:
            exchange()
        if g == 0:
            higher(follow)

            @pl.when(me > 0)
            def _():
                second(0)

            lower(drain)
            pl.semaphore_signal(
                ready.at[rows], inc=1, device_id={"col": other}, device_id_type=MESH
            )
            pl.semaphore_wait(ready.at[rows], 1)
            lower(second, 1)
        if g == len(groups) - 1:
            higher(second)

    group = TILE

    def outgoing(k0, fresh):
        for b in range(lc // TILE):
            t = jnp.swapaxes(right[pl.ds(c0 + b * TILE, TILE), pl.ds(k0, lc), :], 0, 1)
            flip_r[:, b * TILE : (b + 1) * TILE, :] = t

        def step(b):
            i0 = b * group
            base = pl.multiple_of(i0 * lc, lc * group)
            acc = None
            if not fresh:
                acc = [mixed[pl.ds(base + a * lc, lc), :] for a in range(group)]
            acc = triangle(
                group, lc, 0, lc,
                lambda a, q: left[i0 + a, pl.ds(k0 + q, 1), :],
                lambda q: flip_r[q],
                acc,
            )
            for a in range(group):
                mixed[pl.ds(base + a * lc, lc), :] = acc[a]

        loop(n // group, step)

    outgoing(c0, True)

    @pl.when(jnp.logical_and(near_row, my_col == 1))
    def _():
        for q in range(2):
            pltpu.make_async_remote_copy(
                src_ref=pair,
                dst_ref=x_far.at[pl.ds(q * lr, lr)],
                send_sem=far_send.at[0],
                recv_sem=far_recv.at[q],
                device_id={"row": 0, "col": 0},
                device_id_type=MESH,
            ).wait_recv()
        x = x_far[...].reshape(2 * lr * lc, c)
        r, rm = scales(x.astype(F32))
        p = dot(x, wf[0, :, : 4 * H])

        def scaled(q):
            return part(p, q) * r - rm * part(sums_out, q)

        k0 = far * lr
        over = along[pl.ds(o0, lc), :]
        m = jnp.concatenate([over * along[k0 + i : k0 + i + 1] for i in range(2 * lr)], axis=0)
        a = rounded(sigmoid(scaled(0)) * scaled(1) * m)
        b = rounded(sigmoid(scaled(2)) * scaled(3) * m)
        left[k0:, pl.ds(o0, lc), :] = a.reshape(2 * lr, lc, c)
        right[k0:, pl.ds(o0, lc), :] = b.reshape(2 * lr, lc, c)

    def pair_bytes(column, step):
        @pl.when(jnp.logical_and(near_row, my_col == column))
        def _():
            step(partner(0, 0, left.at[pl.ds(0, far * lr)]))

        @pl.when(jnp.logical_not(jnp.logical_and(near_row, my_col == column)))
        def _():
            step(partner(0, 0, left))

    pair_bytes(1, lambda copy: copy.wait_recv())
    outgoing(o0, False)

    v = mixed[...]
    r, rm = scales(v)
    high = v.astype(BF16)
    low = (v - high.astype(F32)).astype(BF16)
    update = dot(
        jnp.concatenate([high, low], axis=1), jnp.concatenate([wo[0], wo[0]], axis=0)
    )
    x = x_h[...].reshape(n * lc, c).astype(F32)
    x = rounded(x + gate[...] * (update * r - rm * sums_mix))
    mid[...] = x
    r, rm = scales(x)

    def scaled(p, q, at):
        return part(p, q) * r - rm * part(sums_in, at + q)

    x = x.astype(BF16)
    normed[...] = x
    p = dot(x, wf[1, :, : 2 * H])
    put_half(in_left, 0, n, rounded(sigmoid(scaled(p, 0, 0)) * scaled(p, 1, 0) * mask[...]))
    e_in_left = [
        partner(1, 1 + b, in_left.at[:, pl.ds(c0 + b * TILE, TILE)]) for b in range(lc // TILE)
    ]
    for copy in e_in_left:
        copy.start()
    p = dot(normed[...], wf[1, :, 2 * H :])
    v = rounded(sigmoid(scaled(p, 0, 2)) * scaled(p, 1, 2) * mask[...])
    put_half(in_right, 0, n, v)
    in_gate[...] = sigmoid(scaled(p, 2, 2))
    e_in_right = partner(1, 3, half(in_right, 0, n))
    e_in_right.start()

    def incoming(i0, copies=()):
        few = 4

        def step(i1):
            acc = triangle(
                few, lc, 0, n,
                lambda a, q: in_left[q, pl.ds(i1 + a, 1), :],
                lambda q: in_right[q, pl.ds(c0, lc), :],
            )
            for a in range(few):
                in_mixed[pl.ds(pl.multiple_of((i1 + a) * lc, lc), lc), :] = acc[a]

        for b in range(lc // TILE):
            if copies:
                copies[b].wait_recv()
            for a in range(0, TILE, few):
                step(pl.multiple_of(i0 + b * TILE, TILE) + a)

    nr, nc = lr * lc, lr * n

    def row_of(ref):
        return ref[pl.ds(pl.multiple_of(r0 * lc, lc), nr), :]

    def col_of(ref):
        return jnp.concatenate([ref[pl.ds(jl + a, n, stride=lc), :] for a in range(lr)], axis=0)

    def strips(ref, wide):
        return jnp.concatenate([row_of(ref), col_of(ref)], axis=0) if wide else row_of(ref)

    def each(step, here=True):
        @pl.when(jnp.logical_and(here, owner))
        def _():
            step(True, nr + nc)

        @pl.when(jnp.logical_and(here, jnp.logical_not(owner)))
        def _():
            step(False, nr)

    def transposed(src, dst, j0):
        for b in range(n // TILE):
            t = jnp.swapaxes(src[b * TILE : (b + 1) * TILE, pl.ds(j0, lc), :], 0, 1)
            dst[pl.ds(j0, lc), b * TILE : (b + 1) * TILE, :] = t

    incoming(c0)

    def prepare(wide, m):
        f = factors(strips(mid, wide), strips(mask, wide), wf[1])
        for q, v in enumerate(f):
            saved[q, :m] = jnp.broadcast_to(v, (m, c))

    def early(wide, m):
        prepare(wide, m)
        if wide:
            transposed(in_left, left_t, c0)
            transposed(in_right, right_t, c0)

    each(early, my_col == 0)

    incoming(o0, e_in_left)

    others = pl.ds(0, (rows - 1) * lr)
    e_ct = pltpu.make_async_remote_copy(
        src_ref=ct_h.at[others],
        dst_ref=ct_h.at[others],
        send_sem=ct_send.at[0],
        recv_sem=ct_recv.at[0],
        device_id={"col": other},
        device_id_type=MESH,
    )
    e_ct.wait_recv()
    own[1].wait()

    def signal(i0):
        z, r = norm(block(in_mixed, i0, lc))
        ct = ct_h[pl.ds(i0, lc)].reshape(lc * lc, c).astype(F32)
        put(ct32, i0, lc, ct)
        dz = rounded(dot_t(ct * block(in_gate, i0, lc), wo[1]))
        v = norm_back(z, r, dz).astype(BF16)
        put_half(sig, i0, lc, v.astype(F32))
        return v

    sig_out[...] = signal(o0).reshape(lc, lc, c)
    e_sig = pltpu.make_async_remote_copy(
        src_ref=sig_out,
        dst_ref=sig_got,
        send_sem=psend.at[2],
        recv_sem=precv.at[4],
        device_id={"col": other},
        device_id_type=MESH,
    )
    e_sig.start()
    e_in_right.wait_recv()

    def turn_signal(j0):
        for b in range(lc // TILE):
            t = jnp.swapaxes(sig[pl.ds(c0 + b * TILE, TILE), pl.ds(j0, lc), :], 0, 1)
            flip_s[:, b * TILE : (b + 1) * TILE, :] = t

    def left_row(j0, acc):
        return triangle(
            lr, lc, 0, lc,
            lambda a, q: in_right[r0 + a, pl.ds(j0 + q, 1), :],
            lambda q: flip_s[q],
            acc,
        )

    def left_col(j0, acc):
        return triangle(
            lr, n, 0, lc,
            lambda a, q: sig[r0 + a, pl.ds(j0 + q, 1), :],
            lambda q: right_t[j0 + q],
            acc,
        )

    def keep(ref, start, width, acc, fix=lambda v: v):
        for a in range(lr):
            ref[start + a * width : start + (a + 1) * width] = fix(acc[a])

    def kept(ref, start, width):
        return [ref[start + a * width : start + (a + 1) * width] for a in range(lr)]

    def window(late):
        def step(wide, m):
            signal(c0)
            z1, _ = norm(strips(in_mixed, wide))
            u1 = dot(z1, wo[1])
            if late:
                prepare(wide, m)
            elif wide:
                transposed(in_left, left_t, o0)
                transposed(in_right, right_t, o0)
            turn_signal(c0)
            keep(d_right, 0, lc, triangle(
                lr, lc, 0, n,
                lambda a, q: in_left[r0 + a, pl.ds(q, 1), :],
                lambda q: sig[q, pl.ds(c0, lc), :],
            ), rounded)
            keep(d_left, 0, lc, left_row(c0, None))
            if wide:
                if late:
                    for j0 in (c0, o0):
                        transposed(in_left, left_t, j0)
                        transposed(in_right, right_t, j0)
                keep(d_right, nr, n, triangle(
                    lr, n, 0, n,
                    lambda a, q: sig[q, pl.ds(r0 + a, 1), :],
                    lambda q: left_t[q],
                ), rounded)
                keep(d_left, nr, n, left_col(c0, None))
            saved[7, :m] = strips(ct32, wide) * u1

        return step

    each(window(False), my_col == 0)
    each(window(True), my_col == 1)
    e_sig.wait_recv()

    def back(wide, m):
        for b in range(lc // TILE):
            t = sig_got[b * TILE : (b + 1) * TILE].astype(F32)
            flip_s[:, b * TILE : (b + 1) * TILE, :] = jnp.swapaxes(t, 0, 1)
        keep(d_left, 0, lc, left_row(o0, kept(d_left, 0, lc)), rounded)
        if wide:
            sig[pl.ds(r0, lr), pl.ds(o0, lc), :] = sig_got[pl.ds(jl, lr)].astype(F32)
            keep(d_left, nr, n, left_col(o0, kept(d_left, nr, n)), rounded)
        f = tuple(saved[q, :m] for q in range(7))
        g = rounded(strips(ct32, wide) + front_back(f, wf[1], d_left[:m], d_right[:m], saved[7, :m]))
        z0, r = norm(strips(mixed, wide))
        dz = rounded(dot_t(g * strips(gate, wide), wo[0]))
        s = rounded(norm_back(z0, r, dz))
        along_row = s[:nr].reshape(lr, lc, c)
        sig_row[:, pl.ds(c0, lc), :] = along_row
        saved[8, :nr] = g[:nr]
        if wide:
            sig_col[...] = s[nr:].reshape(lr, n, c)

    each(back)
    e_row = partner(3, 5, sig_row.at[:, pl.ds(c0, lc)])
    e_row.start()
    e_col = partner(4, 6, sig_col)

    @pl.when(owner)
    def _():
        e_col.start()

    x = x_h[pl.ds(r0, lr)].reshape(nr, c).astype(F32)
    f = factors(x, row_of(mask), wf[0])
    z0, _ = norm(row_of(mixed))
    g = saved[8, :nr]
    d_gate = g * dot(z0, wo[0])

    def out_left(j0, acc):
        return triangle(
            lr, lc, 0, lc,
            lambda a, q: sig_row[a, pl.ds(j0 + q, 1), :],
            lambda q: right[j0 + q, pl.ds(c0, lc), :],
            acc,
        )

    acc = out_left(c0, None)
    e_row.wait_recv()
    d_a = jnp.concatenate([rounded(v) for v in out_left(o0, acc)], axis=0)

    @pl.when(jnp.logical_not(owner))
    def _():
        e_col.wait_recv()

    d_b = jnp.concatenate([rounded(v) for v in triangle(
        lr, lc, 0, n,
        lambda a, q: sig_col[a, pl.ds(q, 1), :],
        lambda q: left[q, pl.ds(c0, lc), :],
    )], axis=0)
    out[...] = (g + front_back(f, wf[0], d_a, d_b, d_gate)).astype(BF16).reshape(lr, lc, c)

    higher(drain)
    e_ct.wait_send()
    pair_bytes(0, lambda copy: copy.wait_send())

    @pl.when(wide_row)
    def _():
        far_copy().wait_send()

    for copy in (partner(1, 3, in_left), e_sig, e_row):
        copy.wait_send()

    @pl.when(owner)
    def _():
        e_col.wait_send()


def from_root(array, axis, root):
    mine = lax.axis_index(axis) == root
    return lax.psum(jnp.where(mine, array, jnp.zeros_like(array)), axis)


def layer_norm(values):
    centred = values - jnp.mean(values, axis=-1, keepdims=True)
    spread = jnp.mean(centred * centred, axis=-1, keepdims=True)
    return centred * lax.rsqrt(spread + 1e-05)


def project_pair(inner_pair, mask_pair, weight):
    normed = layer_norm(inner_pair.astype(jnp.float32)).astype(jnp.bfloat16)
    linear = jnp.dot(normed, weight, preferred_element_type=jnp.float32)
    left_side = jax.nn.sigmoid(linear[..., :H]) * linear[..., H : 2 * H]
    right_side = jax.nn.sigmoid(linear[..., 2 * H : 3 * H]) * linear[..., 3 * H : 4 * H]
    operands = (jnp.stack((left_side, right_side)) * mask_pair[None, :, :, None]).astype(
        jnp.bfloat16
    )
    return (operands, jax.nn.sigmoid(linear[..., 4 * H :]))


def finish(mixed_part, gate_value, inner_pair, weight):
    normed = layer_norm(mixed_part).astype(jnp.bfloat16)
    update = jnp.dot(normed, weight, preferred_element_type=jnp.float32)
    return (inner_pair.astype(jnp.float32) + gate_value * update).astype(jnp.bfloat16)


def body(pair_act, cotangent, residue_mask, front_weight, out_weight):
    local_rows = pair_act.shape[0]
    local_cols = pair_act.shape[1]
    row_index = lax.axis_index("row")
    col_index = lax.axis_index("col")
    block_rows = lax.axis_size("row") // lax.axis_size("col")
    owner_col = row_index // block_rows
    offset = row_index % block_rows * local_rows
    chain_mask = residue_mask.astype(jnp.float32)
    mask_rows = lax.dynamic_slice_in_dim(chain_mask, row_index * local_rows, local_rows)
    mask_cols = lax.dynamic_slice_in_dim(chain_mask, col_index * local_cols, local_cols)
    mask_pair = mask_rows[:, None] * mask_cols[None, :]

    def gather_rows(stacked):
        return lax.all_gather(stacked, "row", axis=1, tiled=True)

    def column_block(gathered):
        slab = lax.dynamic_slice_in_dim(gathered, offset, local_rows, 1)
        return from_root(slab, "col", owner_col)

    def gather_cols(values):
        return lax.all_gather(values, "col", axis=1, tiled=True)

    def sum_cols(partial_term):
        return lax.psum_scatter(
            partial_term.astype(jnp.bfloat16), "col", scatter_dimension=1, tiled=True
        ).astype(jnp.float32)

    (out_ops, out_gate), out_front_back = jax.vjp(
        lambda inner_pair: project_pair(inner_pair, mask_pair, front_weight[0]), pair_act
    )
    fetched = gather_rows(out_ops)
    out_mixed = sum_cols(
        jnp.einsum("ikc,jkc->ijc", out_ops[0], fetched[-1], preferred_element_type=jnp.float32)
    )
    pair_mid, out_finish_back = jax.vjp(
        lambda mixed_part, gate_value, inner_pair: finish(
            mixed_part, gate_value, inner_pair, out_weight[0]
        ),
        out_mixed,
        out_gate,
        pair_act,
    )
    (in_ops, in_gate), in_front_back = jax.vjp(
        lambda inner_pair: project_pair(inner_pair, mask_pair, front_weight[1]), pair_mid
    )
    in_fetched = gather_rows(in_ops)
    left_block = column_block(in_fetched[0])
    in_mixed = jnp.einsum(
        "kic,kjc->ijc", left_block, in_fetched[1], preferred_element_type=jnp.float32
    )
    unused_pair, in_finish_back = jax.vjp(
        lambda mixed_part, gate_value, inner_pair: finish(
            mixed_part, gate_value, inner_pair, out_weight[1]
        ),
        in_mixed,
        in_gate,
        pair_mid,
    )
    grad_mixed, grad_gate, grad_inner = in_finish_back(cotangent)
    signal = grad_mixed.astype(jnp.bfloat16)
    signal_rows = gather_rows(signal[None])[0]
    left_rows = gather_cols(in_ops[0])
    grad_right = jnp.einsum(
        "kic,ijc->kjc", left_rows, signal_rows, preferred_element_type=jnp.float32
    )
    grad_left = sum_cols(
        jnp.einsum("kjc,ijc->kic", in_ops[1], signal_rows, preferred_element_type=jnp.float32)
    )
    (grad_front,) = in_front_back(
        (jnp.stack((grad_left, grad_right)).astype(jnp.bfloat16), grad_gate)
    )
    grad_mid = (grad_inner.astype(jnp.float32) + grad_front.astype(jnp.float32)).astype(
        jnp.bfloat16
    )
    grad_mixed, grad_gate, grad_inner = out_finish_back(grad_mid)
    signal = grad_mixed.astype(jnp.bfloat16)
    signal_cols = gather_cols(signal)
    grad_left = jnp.einsum(
        "ijc,jkc->ikc", signal_cols, fetched[-1], preferred_element_type=jnp.float32
    )
    signal_block = column_block(gather_rows(signal[None])[0])
    grad_right = jnp.einsum(
        "ijc,ikc->jkc", signal_block, fetched[0], preferred_element_type=jnp.float32
    )
    (grad_front,) = out_front_back(
        (jnp.stack((grad_left, grad_right)).astype(jnp.bfloat16), grad_gate)
    )
    return (grad_inner.astype(jnp.float32) + grad_front.astype(jnp.float32)).astype(jnp.bfloat16)


def crop_body(rows, pair_act, cotangent, residue_mask, front_weight, out_weight):
    lr, lc, c = pair_act.shape
    n = residue_mask.shape[0]
    strip = lr * lc + lr * n
    dma = pltpu.SemaphoreType.DMA
    operands = (pair_act, cotangent, residue_mask.reshape(1, n), front_weight, out_weight)
    return pl.pallas_call(
        functools.partial(crop_kernel, rows),
        out_shape=jax.ShapeDtypeStruct((lr, lc, c), BF16),
        in_specs=[pl.BlockSpec(memory_space=pl.ANY)] * 5,
        out_specs=pl.BlockSpec(memory_space=pltpu.VMEM),
        scratch_shapes=[
            pltpu.VMEM((n, lc, c), BF16),
            pltpu.VMEM((n, lc, c), BF16),
            pltpu.VMEM((2 * lr, lc, c), BF16),
            pltpu.VMEM(front_weight.shape, BF16),
            pltpu.VMEM(out_weight.shape, BF16),
            pltpu.VMEM((1, n), jnp.int32),
        ]
        + [pltpu.VMEM((n, n, c), F32)] * 7
        + [pltpu.VMEM((lc, lc, c), F32)] * 2
        + [pltpu.VMEM((n * lc, c), F32)] * 7
        + [
            pltpu.VMEM((n * lc, c), BF16),
            pltpu.VMEM((n, c), F32),
            pltpu.VMEM((9, strip, c), F32),
            pltpu.VMEM((strip, c), F32),
            pltpu.VMEM((strip, c), F32),
            pltpu.VMEM((lr, n, c), F32),
            pltpu.VMEM((lr, n, c), F32),
            pltpu.VMEM((lc, lc, c), BF16),
            pltpu.VMEM((lc, lc, c), BF16),
        ]
        + [dma((5,)), dma((rows,)), dma((max(rows // 2 - 1, 1),)), dma((1,)), dma((1,)), dma((5,)), dma((7,))]
        + [pltpu.SemaphoreType.REGULAR((rows + 1,)), dma((1,)), dma((2,))],
        compiler_params=pltpu.CompilerParams(
            collective_id=0, has_side_effects=True, vmem_limit_bytes=VMEM_BUDGET
        ),
    )(*[pltpu.with_memory_space_constraint(v, pltpu.HBM) for v in operands])


def fits(mesh, n, lr, lc, c):
    rows, cols = mesh.shape["row"], mesh.shape["col"]
    return (
        cols == 2
        and rows >= 2
        and rows & (rows - 1) == 0
        and n == 2 * lc
        and lc == 2 * TILE
        and lc % (2 * lr) == 0
        and FULL_ARRAYS * 4 * n * n * c <= VMEM_BUDGET
    )


def solution(mesh):
    def dispatch(pair_act, cotangent, residue_mask, front_weight, out_weight):
        n = residue_mask.shape[0]
        if fits(mesh, n, *pair_act.shape):
            return crop_body(
                mesh.shape["row"], pair_act, cotangent, residue_mask, front_weight, out_weight
            )
        return body(pair_act, cotangent, residue_mask, front_weight, out_weight)

    placed = (P(("grp", "row"), "col", None), P(("grp", "row"), "col", None), P("grp"), P(), P())
    return jax.shard_map(
        dispatch,
        mesh=mesh,
        in_specs=placed,
        out_specs=P(("grp", "row"), "col", None),
        check_vma=False,
    )
```

```python
import functools

import jax
import jax.numpy as jnp
from jax import lax
from jax.experimental import pallas as pl
from jax.experimental.pallas import tpu as pltpu
from jax.sharding import PartitionSpec as P

H = 128
TILE = 8
F32 = jnp.float32
BF16 = jnp.bfloat16
MESH = pl.DeviceIdType.MESH
VMEM_BUDGET = 24 << 20
FULL_ARRAYS = 16


def sigmoid(x):
    return 0.5 * jnp.tanh(0.5 * x) + 0.5


def norm(v):
    centred = v - jnp.mean(v, axis=-1, keepdims=True)
    r = lax.rsqrt(jnp.mean(centred * centred, axis=-1, keepdims=True) + 1e-05)
    return centred * r, r


def scales(v):
    mean = jnp.mean(v, axis=-1, keepdims=True)
    centred = v - mean
    r = lax.rsqrt(jnp.mean(centred * centred, axis=-1, keepdims=True) + 1e-05)
    return r, r * mean


def column_sums(w):
    return jnp.sum(w.astype(F32), axis=0, keepdims=True)


def norm_back(y, r, d):
    return r * (d - jnp.mean(d, axis=-1, keepdims=True) - y * jnp.mean(d * y, axis=-1, keepdims=True))


def rounded(v):
    return v.astype(BF16).astype(F32)


def dot(a, b):
    return jnp.dot(a.astype(BF16), b, preferred_element_type=F32)


def dot_t(a, b):
    return lax.dot_general(
        a.astype(BF16), b, (((1,), (1,)), ((), ())), preferred_element_type=F32
    )


def part(p, n):
    return p[:, n * H : (n + 1) * H]


def factors(x, mask, weight):
    y, r = norm(x)
    p = dot(y, weight)
    s0, s2, s4 = sigmoid(part(p, 0)), sigmoid(part(p, 2)), sigmoid(part(p, 4))
    fa, fb = mask * s0, mask * s2
    return y, r, fa * part(p, 1) * (1.0 - s0), fa, fb * part(p, 3) * (1.0 - s2), fb, s4 * (1.0 - s4)


def front_back(f, weight, d_a, d_b, d_gate):
    y, r, f0, f1, f2, f3, f4 = f
    d = jnp.concatenate(
        [(v.astype(BF16)) for v in (d_a * f0, d_a * f1, d_b * f2, d_b * f3, d_gate * f4)], axis=1
    )
    return rounded(norm_back(y, r, rounded(dot_t(d, weight))))


def crop_kernel(
    rows, pair, cot, mask_in, wf_in, wo_in, out,
    x_h, ct_h, x_far, wf, wo, chain,
    left, right, in_left, in_right, sig, left_t, right_t, flip_r, flip_s,
    mask, mixed, gate, mid, in_mixed, in_gate, ct32, normed, along,
    saved, d_left, d_right, sig_row, sig_col, sig_out, sig_got,
    local_sem, x_send, x_recv, ct_send, ct_recv, psend, precv, ready, far_send, far_recv,
):
    n, c = left.shape[0], left.shape[2]
    lr, lc = out.shape[0], out.shape[1]
    bits = rows.bit_length() - 1
    me, my_col = lax.axis_index("row"), lax.axis_index("col")
    other = 1 - my_col
    me_bits = [lax.rem(lax.div(me, 1 << b), 2) for b in range(bits)]

    def flip(d, low=0):
        total = 0
        for b in range(low, bits):
            bit = me_bits[b]
            total = total + (1 - bit if d >> b & 1 else bit) * (1 << b)
        return total

    far = rows - 2 if rows > 4 else rows
    wide_row = jnp.logical_and(me >= far, my_col == 0)
    near_row = jnp.logical_and(me == 0, rows > 4)
    barrier = pltpu.get_barrier_semaphore()
    pl.semaphore_signal(barrier, inc=1, device_id={"col": other}, device_id_type=MESH)
    for row in range(1, rows):
        @pl.when(jnp.logical_and(me < row, me != row - 1) if row == far else me < row)
        def _():
            pl.semaphore_signal(barrier, inc=1, device_id={"row": row}, device_id_type=MESH)

    for row in range(far, rows):
        @pl.when(jnp.logical_and(me == 0, my_col == 1))
        def _():
            pl.semaphore_signal(
                barrier, inc=1, device_id={"row": row, "col": 0}, device_id_type=MESH
            )

    r0 = pl.multiple_of(me * lr, lr)
    c0 = pl.multiple_of(my_col * lc, lc)
    o0 = pl.multiple_of(other * lc, lc)
    jl = lax.rem(me * lr, lc)
    owner = lax.div(me * lr, lc) == my_col

    own = [
        pltpu.make_async_copy(src, dst.at[pl.ds(r0, lr)], local_sem.at[t])
        for t, (src, dst) in enumerate(((pair, x_h), (cot, ct_h)))
    ]
    weights = [
        pltpu.make_async_copy(wf_in, wf, local_sem.at[2]),
        pltpu.make_async_copy(wo_in, wo, local_sem.at[3]),
    ]
    chain_copy = pltpu.make_async_copy(mask_in, chain, local_sem.at[4])
    for copy in [chain_copy, own[0]] + weights + [own[1]]:
        copy.start()

    def group_of(row):
        if not isinstance(row, int):
            return 0
        apart = 0
        for b in range(1, bits):
            apart = apart + (1 - me_bits[b] if row >> b & 1 else me_bits[b]) * (1 << b)
        return jnp.maximum(lax.div(apart, 2) - 1, 0)

    def direct(t, row, mine=None):
        src, dst = ((pair, x_h), (cot, ct_h))[t]
        source = row if mine is None else mine
        return pltpu.make_async_remote_copy(
            src_ref=src,
            dst_ref=dst.at[pl.ds(pl.multiple_of(source * lr, lr), lr)],
            send_sem=x_send.at[row] if t == 0 else ct_send.at[0],
            recv_sem=x_recv.at[group_of(row)] if t == 0 else ct_recv.at[0],
            device_id={"row": row},
            device_id_type=MESH,
        )

    def lower(step, start=0):
        for row in range(start, rows - 1):
            @pl.when(jnp.logical_and(row < me, me != far) if row == far - 1 else row < me)
            def _():
                step(row)

    def higher(step):
        for row in range(1, rows):
            @pl.when(jnp.logical_or(row > me, me == far) if row == far - 1 else row > me)
            def _():
                step(row)

    def far_copy():
        at = pl.ds(pl.multiple_of((me - far) * lr, lr), lr)
        return pltpu.make_async_remote_copy(
            src_ref=pair,
            dst_ref=x_far.at[at],
            send_sem=far_send.at[0],
            recv_sem=far_recv.at[me - far],
            device_id={"row": 0, "col": 1},
            device_id_type=MESH,
        )

    def answer(row):
        if row == 0:
            @pl.when(jnp.logical_not(wide_row))
            def _():
                direct(0, row, me).start()
        elif row < 2:
            direct(0, row, me).start()
        pl.semaphore_signal(ready.at[me], inc=1, device_id={"row": row}, device_id_type=MESH)

    def send(row):
        if row >= 2:
            direct(0, row, me).start()

    def tell(row, about):
        pl.semaphore_signal(ready.at[about], inc=1, device_id={"row": row}, device_id_type=MESH)

    def follow(row):
        pl.semaphore_wait(ready.at[row], 1)
        direct(0, row, me).start()
        if row == far:
            @pl.when(me == far - 2)
            def _():
                tell(far, far - 1)
                tell(far - 1, far)

    def drain(row):
        direct(0, row, me).wait_send()

    def second(row):
        direct(1, row, me).start()

    def partner(q, r, ref):
        return pltpu.make_async_remote_copy(
            src_ref=ref,
            dst_ref=ref,
            send_sem=psend.at[q],
            recv_sem=precv.at[r],
            device_id={"col": other},
            device_id_type=MESH,
        )

    greeted = me + 1 - jnp.where(me == far, 1, 0)
    pl.semaphore_wait(barrier, greeted + jnp.where(wide_row, 1, 0))

    @pl.when(wide_row)
    def _():
        direct(0, 0, me).start()
        far_copy().start()

    lower(answer)

    chain_copy.wait()
    span = jnp.broadcast_to(chain[...].astype(F32), (n, n))
    here = lax.broadcasted_iota(jnp.int32, (n, n), 0) == lax.broadcasted_iota(jnp.int32, (n, n), 1)
    along[...] = jnp.broadcast_to(
        jnp.sum(jnp.where(here, span, 0.0), axis=1, keepdims=True), (n, c)
    )
    across = along[pl.ds(c0, lc), :]
    for i in range(n):
        mask[i * lc : (i + 1) * lc] = across * along[i : i + 1]
    lower(send)

    def block(ref, k0, nk):
        return ref[pl.ds(pl.multiple_of(k0 * lc, lc), nk * lc), :]

    def put(ref, k0, nk, v):
        ref[pl.ds(pl.multiple_of(k0 * lc, lc), nk * lc), :] = v

    def put_half(ref, k0, nk, v):
        ref[pl.ds(k0, nk), pl.ds(c0, lc), :] = v.reshape(nk, lc, c)

    def half(ref, k0, nk):
        return ref.at[pl.ds(k0, nk), pl.ds(c0, lc)]

    def projected(x, segments, weight, sums, a_ref, b_ref, g_ref):
        r, rm = scales(x.astype(F32))
        p = dot(x, weight)

        def part(p, q):
            return p[:, q * H : (q + 1) * H] * r - rm * sums[:, q * H : (q + 1) * H]

        m = jnp.concatenate([block(mask, k0, nk) for k0, nk in segments], axis=0)
        a = rounded(sigmoid(part(p, 0)) * part(p, 1) * m)
        b = rounded(sigmoid(part(p, 2)) * part(p, 3) * m)
        g = sigmoid(part(p, 4))
        at = 0
        for k0, nk in segments:
            span = slice(at * lc, (at + nk) * lc)
            put_half(a_ref, k0, nk, a[span])
            put_half(b_ref, k0, nk, b[span])
            put(g_ref, k0, nk, g[span])
            at += nk

    def triangle(count, width, first, depth, row_at, tile_at, acc=None):
        def term(q, acc):
            t = tile_at(first + q)
            return tuple(v + row_at(a, first + q) * t for a, v in enumerate(acc))

        if acc is None:
            acc = (jnp.zeros((width, c), F32),) * count
        return lax.fori_loop(0, depth, term, tuple(acc), unroll=True)

    def loop(count, step):
        def body(k, carry):
            step(k)
            return carry

        lax.fori_loop(0, count, body, 0)

    for copy in weights:
        copy.wait()
    sums_out, sums_in, sums_mix = (column_sums(w) for w in (wf[0], wf[1], wo[0]))
    groups = [[(0, 1)], [(1, 1), (2, 2)] if rows > 2 else [(1, 1)]]
    groups += [[(d, 2)] for d in range(4, rows, 2)]
    for g, group in enumerate(groups):
        if g == 0:
            own[0].wait()
        else:
            here = x_h.at[pl.ds(0, sum(count for _, count in group) * lr)]
            pltpu.make_async_remote_copy(
                src_ref=here,
                dst_ref=here,
                send_sem=x_send.at[0],
                recv_sem=x_recv.at[g - 1],
                device_id={"col": other},
                device_id_type=MESH,
            ).wait_recv()
        segments = [
            (pl.multiple_of(flip(d, count.bit_length() - 1) * lr, count * lr), count * lr)
            for d, count in group
        ]
        x = jnp.concatenate(
            [x_h[pl.ds(k0, nk)].reshape(nk * lc, c) for k0, nk in segments], axis=0
        )
        projected(x, segments, wf[0], sums_out, left, right, gate)
        def exchange():
            for k0, nk in segments:
                partner(0, 0, half(left, k0, nk)).start()
                partner(0, 0, half(right, k0, nk)).start()

        if g == len(groups) - 1 and rows > 4:
            pl.when(jnp.logical_not(jnp.logical_and(near_row, my_col == 0)))(exchange)
        else:
            exchange()
        if g == 0:
            higher(follow)

            @pl.when(me > 0)
            def _():
                second(0)

            lower(drain)
            pl.semaphore_signal(
                ready.at[rows], inc=1, device_id={"col": other}, device_id_type=MESH
            )
            pl.semaphore_wait(ready.at[rows], 1)
            lower(second, 1)
        if g == len(groups) - 1:
            higher(second)

    group = TILE

    def outgoing(k0, fresh):
        for b in range(lc // TILE):
            t = jnp.swapaxes(right[pl.ds(c0 + b * TILE, TILE), pl.ds(k0, lc), :], 0, 1)
            flip_r[:, b * TILE : (b + 1) * TILE, :] = t

        def step(b):
            i0 = b * group
            base = pl.multiple_of(i0 * lc, lc * group)
            acc = None
            if not fresh:
                acc = [mixed[pl.ds(base + a * lc, lc), :] for a in range(group)]
            acc = triangle(
                group, lc, 0, lc,
                lambda a, q: left[i0 + a, pl.ds(k0 + q, 1), :],
                lambda q: flip_r[q],
                acc,
            )
            for a in range(group):
                mixed[pl.ds(base + a * lc, lc), :] = acc[a]

        loop(n // group, step)

    outgoing(c0, True)

    @pl.when(jnp.logical_and(near_row, my_col == 1))
    def _():
        for q in range(2):
            pltpu.make_async_remote_copy(
                src_ref=pair,
                dst_ref=x_far.at[pl.ds(q * lr, lr)],
                send_sem=far_send.at[0],
                recv_sem=far_recv.at[q],
                device_id={"row": 0, "col": 0},
                device_id_type=MESH,
            ).wait_recv()
        x = x_far[...].reshape(2 * lr * lc, c)
        r, rm = scales(x.astype(F32))
        p = dot(x, wf[0, :, : 4 * H])

        def scaled(q):
            return part(p, q) * r - rm * part(sums_out, q)

        k0 = far * lr
        over = along[pl.ds(o0, lc), :]
        m = jnp.concatenate([over * along[k0 + i : k0 + i + 1] for i in range(2 * lr)], axis=0)
        a = rounded(sigmoid(scaled(0)) * scaled(1) * m)
        b = rounded(sigmoid(scaled(2)) * scaled(3) * m)
        left[k0:, pl.ds(o0, lc), :] = a.reshape(2 * lr, lc, c)
        right[k0:, pl.ds(o0, lc), :] = b.reshape(2 * lr, lc, c)

    def pair_bytes(column, step):
        @pl.when(jnp.logical_and(near_row, my_col == column))
        def _():
            step(partner(0, 0, left.at[pl.ds(0, far * lr)]))

        @pl.when(jnp.logical_not(jnp.logical_and(near_row, my_col == column)))
        def _():
            step(partner(0, 0, left))

    pair_bytes(1, lambda copy: copy.wait_recv())
    outgoing(o0, False)

    v = mixed[...]
    r, rm = scales(v)
    high = v.astype(BF16)
    low = (v - high.astype(F32)).astype(BF16)
    update = dot(
        jnp.concatenate([high, low], axis=1), jnp.concatenate([wo[0], wo[0]], axis=0)
    )
    x = x_h[...].reshape(n * lc, c).astype(F32)
    x = rounded(x + gate[...] * (update * r - rm * sums_mix))
    mid[...] = x
    r, rm = scales(x)

    def scaled(p, q, at):
        return part(p, q) * r - rm * part(sums_in, at + q)

    x = x.astype(BF16)
    normed[...] = x
    p = dot(x, wf[1, :, : 2 * H])
    put_half(in_left, 0, n, rounded(sigmoid(scaled(p, 0, 0)) * scaled(p, 1, 0) * mask[...]))
    quarter = n // 4
    e_in_left = [
        partner(1, r, half(in_left, b * quarter, quarter)) for b, r in enumerate((1, 2, 7, 8))
    ]
    for copy in e_in_left:
        copy.start()
    p = dot(normed[...], wf[1, :, 2 * H :])
    v = rounded(sigmoid(scaled(p, 0, 2)) * scaled(p, 1, 2) * mask[...])
    put_half(in_right, 0, n, v)
    in_gate[...] = sigmoid(scaled(p, 2, 2))
    e_in_right = partner(1, 3, half(in_right, 0, n))
    e_in_right.start()

    def incoming(i0, copies=(None,)):
        depth = n // len(copies)
        for q, copy in enumerate(copies):
            if copy is not None:
                copy.wait_recv()
            for b in range(lc // TILE):
                i1 = pl.multiple_of(i0 + b * TILE, TILE)
                at = pl.multiple_of(i1 * lc, lc)
                acc = None
                if q:
                    acc = [in_mixed[pl.ds(at + a * lc, lc), :] for a in range(TILE)]
                acc = triangle(
                    TILE, lc, q * depth, depth,
                    lambda a, k: in_left[k, pl.ds(i1 + a, 1), :],
                    lambda k: in_right[k, pl.ds(c0, lc), :],
                    acc,
                )
                for a in range(TILE):
                    in_mixed[pl.ds(at + a * lc, lc), :] = acc[a]

    nr, nc = lr * lc, lr * n

    def row_of(ref):
        return ref[pl.ds(pl.multiple_of(r0 * lc, lc), nr), :]

    def col_of(ref):
        return jnp.concatenate([ref[pl.ds(jl + a, n, stride=lc), :] for a in range(lr)], axis=0)

    def strips(ref, wide):
        return jnp.concatenate([row_of(ref), col_of(ref)], axis=0) if wide else row_of(ref)

    def each(step, here=True):
        @pl.when(jnp.logical_and(here, owner))
        def _():
            step(True, nr + nc)

        @pl.when(jnp.logical_and(here, jnp.logical_not(owner)))
        def _():
            step(False, nr)

    def transposed(src, dst, j0):
        for b in range(n // TILE):
            t = jnp.swapaxes(src[b * TILE : (b + 1) * TILE, pl.ds(j0, lc), :], 0, 1)
            dst[pl.ds(j0, lc), b * TILE : (b + 1) * TILE, :] = t

    incoming(c0)

    def prepare(wide, m):
        f = factors(strips(mid, wide), strips(mask, wide), wf[1])
        for q, v in enumerate(f):
            saved[q, :m] = jnp.broadcast_to(v, (m, c))

    def early(wide, m):
        prepare(wide, m)
        if wide:
            transposed(in_left, left_t, c0)
            transposed(in_right, right_t, c0)

    each(early, my_col == 0)

    incoming(o0, e_in_left)

    others = pl.ds(0, (rows - 1) * lr)
    e_ct = pltpu.make_async_remote_copy(
        src_ref=ct_h.at[others],
        dst_ref=ct_h.at[others],
        send_sem=ct_send.at[0],
        recv_sem=ct_recv.at[0],
        device_id={"col": other},
        device_id_type=MESH,
    )
    e_ct.wait_recv()
    own[1].wait()

    def signal(i0):
        z, r = norm(block(in_mixed, i0, lc))
        ct = ct_h[pl.ds(i0, lc)].reshape(lc * lc, c).astype(F32)
        put(ct32, i0, lc, ct)
        dz = rounded(dot_t(ct * block(in_gate, i0, lc), wo[1]))
        v = norm_back(z, r, dz).astype(BF16)
        put_half(sig, i0, lc, v.astype(F32))
        return v

    sig_out[...] = signal(o0).reshape(lc, lc, c)
    e_sig = pltpu.make_async_remote_copy(
        src_ref=sig_out,
        dst_ref=sig_got,
        send_sem=psend.at[2],
        recv_sem=precv.at[4],
        device_id={"col": other},
        device_id_type=MESH,
    )
    e_sig.start()
    e_in_right.wait_recv()

    def turn_signal(j0):
        for b in range(lc // TILE):
            t = jnp.swapaxes(sig[pl.ds(c0 + b * TILE, TILE), pl.ds(j0, lc), :], 0, 1)
            flip_s[:, b * TILE : (b + 1) * TILE, :] = t

    def left_row(j0, acc):
        return triangle(
            lr, lc, 0, lc,
            lambda a, q: in_right[r0 + a, pl.ds(j0 + q, 1), :],
            lambda q: flip_s[q],
            acc,
        )

    def left_col(j0, acc):
        return triangle(
            lr, n, 0, lc,
            lambda a, q: sig[r0 + a, pl.ds(j0 + q, 1), :],
            lambda q: right_t[j0 + q],
            acc,
        )

    def keep(ref, start, width, acc, fix=lambda v: v):
        for a in range(lr):
            ref[start + a * width : start + (a + 1) * width] = fix(acc[a])

    def kept(ref, start, width):
        return [ref[start + a * width : start + (a + 1) * width] for a in range(lr)]

    def window(late):
        def step(wide, m):
            signal(c0)
            z1, _ = norm(strips(in_mixed, wide))
            u1 = dot(z1, wo[1])
            if late:
                prepare(wide, m)
            elif wide:
                transposed(in_left, left_t, o0)
                transposed(in_right, right_t, o0)
            turn_signal(c0)
            keep(d_right, 0, lc, triangle(
                lr, lc, 0, n,
                lambda a, q: in_left[r0 + a, pl.ds(q, 1), :],
                lambda q: sig[q, pl.ds(c0, lc), :],
            ), rounded)
            keep(d_left, 0, lc, left_row(c0, None))
            if wide:
                if late:
                    for j0 in (c0, o0):
                        transposed(in_left, left_t, j0)
                        transposed(in_right, right_t, j0)
                keep(d_right, nr, n, triangle(
                    lr, n, 0, n,
                    lambda a, q: sig[q, pl.ds(r0 + a, 1), :],
                    lambda q: left_t[q],
                ), rounded)
                keep(d_left, nr, n, left_col(c0, None))
            saved[7, :m] = strips(ct32, wide) * u1

        return step

    each(window(False), my_col == 0)
    each(window(True), my_col == 1)
    e_sig.wait_recv()

    def back(wide, m):
        for b in range(lc // TILE):
            t = sig_got[b * TILE : (b + 1) * TILE].astype(F32)
            flip_s[:, b * TILE : (b + 1) * TILE, :] = jnp.swapaxes(t, 0, 1)
        keep(d_left, 0, lc, left_row(o0, kept(d_left, 0, lc)), rounded)
        if wide:
            sig[pl.ds(r0, lr), pl.ds(o0, lc), :] = sig_got[pl.ds(jl, lr)].astype(F32)
            keep(d_left, nr, n, left_col(o0, kept(d_left, nr, n)), rounded)
        f = tuple(saved[q, :m] for q in range(7))
        g = rounded(strips(ct32, wide) + front_back(f, wf[1], d_left[:m], d_right[:m], saved[7, :m]))
        z0, r = norm(strips(mixed, wide))
        dz = rounded(dot_t(g * strips(gate, wide), wo[0]))
        s = rounded(norm_back(z0, r, dz))
        along_row = s[:nr].reshape(lr, lc, c)
        sig_row[:, pl.ds(c0, lc), :] = along_row
        saved[8, :nr] = g[:nr]
        if wide:
            sig_col[...] = s[nr:].reshape(lr, n, c)

    each(back)
    e_row = partner(3, 5, sig_row.at[:, pl.ds(c0, lc)])
    e_row.start()
    e_col = partner(4, 6, sig_col)

    @pl.when(owner)
    def _():
        e_col.start()

    x = x_h[pl.ds(r0, lr)].reshape(nr, c).astype(F32)
    f = factors(x, row_of(mask), wf[0])
    z0, _ = norm(row_of(mixed))
    g = saved[8, :nr]
    d_gate = g * dot(z0, wo[0])

    def out_left(j0, acc):
        return triangle(
            lr, lc, 0, lc,
            lambda a, q: sig_row[a, pl.ds(j0 + q, 1), :],
            lambda q: right[j0 + q, pl.ds(c0, lc), :],
            acc,
        )

    acc = out_left(c0, None)
    e_row.wait_recv()
    d_a = jnp.concatenate([rounded(v) for v in out_left(o0, acc)], axis=0)

    @pl.when(jnp.logical_not(owner))
    def _():
        e_col.wait_recv()

    d_b = jnp.concatenate([rounded(v) for v in triangle(
        lr, lc, 0, n,
        lambda a, q: sig_col[a, pl.ds(q, 1), :],
        lambda q: left[q, pl.ds(c0, lc), :],
    )], axis=0)
    out[...] = (g + front_back(f, wf[0], d_a, d_b, d_gate)).astype(BF16).reshape(lr, lc, c)

    higher(drain)
    e_ct.wait_send()
    pair_bytes(0, lambda copy: copy.wait_send())

    @pl.when(wide_row)
    def _():
        far_copy().wait_send()

    for copy in (partner(1, 3, in_left), e_sig, e_row):
        copy.wait_send()

    @pl.when(owner)
    def _():
        e_col.wait_send()


def from_root(array, axis, root):
    mine = lax.axis_index(axis) == root
    return lax.psum(jnp.where(mine, array, jnp.zeros_like(array)), axis)


def layer_norm(values):
    centred = values - jnp.mean(values, axis=-1, keepdims=True)
    spread = jnp.mean(centred * centred, axis=-1, keepdims=True)
    return centred * lax.rsqrt(spread + 1e-05)


def project_pair(inner_pair, mask_pair, weight):
    normed = layer_norm(inner_pair.astype(jnp.float32)).astype(jnp.bfloat16)
    linear = jnp.dot(normed, weight, preferred_element_type=jnp.float32)
    left_side = jax.nn.sigmoid(linear[..., :H]) * linear[..., H : 2 * H]
    right_side = jax.nn.sigmoid(linear[..., 2 * H : 3 * H]) * linear[..., 3 * H : 4 * H]
    operands = (jnp.stack((left_side, right_side)) * mask_pair[None, :, :, None]).astype(
        jnp.bfloat16
    )
    return (operands, jax.nn.sigmoid(linear[..., 4 * H :]))


def finish(mixed_part, gate_value, inner_pair, weight):
    normed = layer_norm(mixed_part).astype(jnp.bfloat16)
    update = jnp.dot(normed, weight, preferred_element_type=jnp.float32)
    return (inner_pair.astype(jnp.float32) + gate_value * update).astype(jnp.bfloat16)


def body(pair_act, cotangent, residue_mask, front_weight, out_weight):
    local_rows = pair_act.shape[0]
    local_cols = pair_act.shape[1]
    row_index = lax.axis_index("row")
    col_index = lax.axis_index("col")
    block_rows = lax.axis_size("row") // lax.axis_size("col")
    owner_col = row_index // block_rows
    offset = row_index % block_rows * local_rows
    chain_mask = residue_mask.astype(jnp.float32)
    mask_rows = lax.dynamic_slice_in_dim(chain_mask, row_index * local_rows, local_rows)
    mask_cols = lax.dynamic_slice_in_dim(chain_mask, col_index * local_cols, local_cols)
    mask_pair = mask_rows[:, None] * mask_cols[None, :]

    def gather_rows(stacked):
        return lax.all_gather(stacked, "row", axis=1, tiled=True)

    def column_block(gathered):
        slab = lax.dynamic_slice_in_dim(gathered, offset, local_rows, 1)
        return from_root(slab, "col", owner_col)

    def gather_cols(values):
        return lax.all_gather(values, "col", axis=1, tiled=True)

    def sum_cols(partial_term):
        return lax.psum_scatter(
            partial_term.astype(jnp.bfloat16), "col", scatter_dimension=1, tiled=True
        ).astype(jnp.float32)

    (out_ops, out_gate), out_front_back = jax.vjp(
        lambda inner_pair: project_pair(inner_pair, mask_pair, front_weight[0]), pair_act
    )
    fetched = gather_rows(out_ops)
    out_mixed = sum_cols(
        jnp.einsum("ikc,jkc->ijc", out_ops[0], fetched[-1], preferred_element_type=jnp.float32)
    )
    pair_mid, out_finish_back = jax.vjp(
        lambda mixed_part, gate_value, inner_pair: finish(
            mixed_part, gate_value, inner_pair, out_weight[0]
        ),
        out_mixed,
        out_gate,
        pair_act,
    )
    (in_ops, in_gate), in_front_back = jax.vjp(
        lambda inner_pair: project_pair(inner_pair, mask_pair, front_weight[1]), pair_mid
    )
    in_fetched = gather_rows(in_ops)
    left_block = column_block(in_fetched[0])
    in_mixed = jnp.einsum(
        "kic,kjc->ijc", left_block, in_fetched[1], preferred_element_type=jnp.float32
    )
    unused_pair, in_finish_back = jax.vjp(
        lambda mixed_part, gate_value, inner_pair: finish(
            mixed_part, gate_value, inner_pair, out_weight[1]
        ),
        in_mixed,
        in_gate,
        pair_mid,
    )
    grad_mixed, grad_gate, grad_inner = in_finish_back(cotangent)
    signal = grad_mixed.astype(jnp.bfloat16)
    signal_rows = gather_rows(signal[None])[0]
    left_rows = gather_cols(in_ops[0])
    grad_right = jnp.einsum(
        "kic,ijc->kjc", left_rows, signal_rows, preferred_element_type=jnp.float32
    )
    grad_left = sum_cols(
        jnp.einsum("kjc,ijc->kic", in_ops[1], signal_rows, preferred_element_type=jnp.float32)
    )
    (grad_front,) = in_front_back(
        (jnp.stack((grad_left, grad_right)).astype(jnp.bfloat16), grad_gate)
    )
    grad_mid = (grad_inner.astype(jnp.float32) + grad_front.astype(jnp.float32)).astype(
        jnp.bfloat16
    )
    grad_mixed, grad_gate, grad_inner = out_finish_back(grad_mid)
    signal = grad_mixed.astype(jnp.bfloat16)
    signal_cols = gather_cols(signal)
    grad_left = jnp.einsum(
        "ijc,jkc->ikc", signal_cols, fetched[-1], preferred_element_type=jnp.float32
    )
    signal_block = column_block(gather_rows(signal[None])[0])
    grad_right = jnp.einsum(
        "ijc,ikc->jkc", signal_block, fetched[0], preferred_element_type=jnp.float32
    )
    (grad_front,) = out_front_back(
        (jnp.stack((grad_left, grad_right)).astype(jnp.bfloat16), grad_gate)
    )
    return (grad_inner.astype(jnp.float32) + grad_front.astype(jnp.float32)).astype(jnp.bfloat16)


def crop_body(rows, pair_act, cotangent, residue_mask, front_weight, out_weight):
    lr, lc, c = pair_act.shape
    n = residue_mask.shape[0]
    strip = lr * lc + lr * n
    dma = pltpu.SemaphoreType.DMA
    operands = (pair_act, cotangent, residue_mask.reshape(1, n), front_weight, out_weight)
    return pl.pallas_call(
        functools.partial(crop_kernel, rows),
        out_shape=jax.ShapeDtypeStruct((lr, lc, c), BF16),
        in_specs=[pl.BlockSpec(memory_space=pl.ANY)] * 5,
        out_specs=pl.BlockSpec(memory_space=pltpu.VMEM),
        scratch_shapes=[
            pltpu.VMEM((n, lc, c), BF16),
            pltpu.VMEM((n, lc, c), BF16),
            pltpu.VMEM((2 * lr, lc, c), BF16),
            pltpu.VMEM(front_weight.shape, BF16),
            pltpu.VMEM(out_weight.shape, BF16),
            pltpu.VMEM((1, n), jnp.int32),
        ]
        + [pltpu.VMEM((n, n, c), F32)] * 7
        + [pltpu.VMEM((lc, lc, c), F32)] * 2
        + [pltpu.VMEM((n * lc, c), F32)] * 7
        + [
            pltpu.VMEM((n * lc, c), BF16),
            pltpu.VMEM((n, c), F32),
            pltpu.VMEM((9, strip, c), F32),
            pltpu.VMEM((strip, c), F32),
            pltpu.VMEM((strip, c), F32),
            pltpu.VMEM((lr, n, c), F32),
            pltpu.VMEM((lr, n, c), F32),
            pltpu.VMEM((lc, lc, c), BF16),
            pltpu.VMEM((lc, lc, c), BF16),
        ]
        + [dma((5,)), dma((rows,)), dma((max(rows // 2 - 1, 1),)), dma((1,)), dma((1,)), dma((5,)), dma((9,))]
        + [pltpu.SemaphoreType.REGULAR((rows + 1,)), dma((1,)), dma((2,))],
        compiler_params=pltpu.CompilerParams(
            collective_id=0, has_side_effects=True, vmem_limit_bytes=VMEM_BUDGET
        ),
    )(*[pltpu.with_memory_space_constraint(v, pltpu.HBM) for v in operands])


def fits(mesh, n, lr, lc, c):
    rows, cols = mesh.shape["row"], mesh.shape["col"]
    return (
        cols == 2
        and rows >= 2
        and rows & (rows - 1) == 0
        and n == 2 * lc
        and lc == 2 * TILE
        and lc % (2 * lr) == 0
        and FULL_ARRAYS * 4 * n * n * c <= VMEM_BUDGET
    )


def solution(mesh):
    def dispatch(pair_act, cotangent, residue_mask, front_weight, out_weight):
        n = residue_mask.shape[0]
        if fits(mesh, n, *pair_act.shape):
            return crop_body(
                mesh.shape["row"], pair_act, cotangent, residue_mask, front_weight, out_weight
            )
        return body(pair_act, cotangent, residue_mask, front_weight, out_weight)

    placed = (P(("grp", "row"), "col", None), P(("grp", "row"), "col", None), P("grp"), P(), P())
    return jax.shard_map(
        dispatch,
        mesh=mesh,
        in_specs=placed,
        out_specs=P(("grp", "row"), "col", None),
        check_vma=False,
    )
```
